32 devices in a mesh: img: 4 (over y, x), pix: 8 (over z, core).
Axes of the slice: x: 2, y: 2, z: 4, core: 2. Of those that a mesh axis runs over, the one named last changes fastest.
Arguments:
- latents: bfloat16 [8, 512, 1024], P('img'), may hold values from -6 to 6
- pixels: bfloat16 [8, 6272, 261], P('img', 'pix'), may hold values from -6 to 6
- keep_mask: int32 [8, 6272], P('img', 'pix'), may hold values from 0 to 1, as said below
- cotangent: bfloat16 [8, 512, 1024], P('img'), may hold values from -6 to 6
- w_query: bfloat16 [1024, 1024], replicated, may hold values from -0.375 to 0.375
- w_key: bfloat16 [261, 1024], replicated, may hold values from -0.375 to 0.375
- w_value: bfloat16 [261, 1024], replicated, may hold values from -0.375 to 0.375
- kv_bias: bfloat16 [1024], replicated, may hold values from -0.0625 to 0.0625
- w_out: bfloat16 [1024, 1024], replicated, may hold values from -3 to 3
- w_first: bfloat16 [1024, 1024], replicated, may hold values from -0.1875 to 0.1875
- w_second: bfloat16 [1024, 1024], replicated, may hold values from -0.1875 to 0.1875
- w_qkv: bfloat16 [1024, 3072], replicated, may hold values from -0.1875 to 0.1875
- w_self_out: bfloat16 [1024, 1024], replicated, may hold values from -0.75 to 0.75
- w_third: bfloat16 [1024, 1024], replicated, may hold values from -0.1875 to 0.1875
- w_fourth: bfloat16 [1024, 1024], replicated, may hold values from -0.1875 to 0.1875
- norm_gains: bfloat16 [4, 1024], replicated, may hold values from 0.5 to 1.5
- norm_shifts: bfloat16 [4, 1024], replicated, may hold values from -0.875 to 0.875
- proj_biases: bfloat16 [9, 1024], replicated, may hold values from -0.875 to 0.875
- pix_gain: bfloat16 [261], replicated, may hold values from 0.5 to 1.5
- pix_shift: bfloat16 [261], replicated, may hold values from -0.875 to 0.875
Outputs:
- latents_out: bfloat16 [8, 512, 1024], P('img')
- latents_grad: float32 [8, 512, 1024], P('img')
- pixels_grad: float32 [8, 6272, 261], P('img', 'pix')
- grad_query: float32 [1024, 1024], P(None, 'pix')
- grad_key: float32 [261, 1024], P(None, 'pix')
- grad_value: float32 [261, 1024], P(None, 'pix')
- grad_kv_bias: float32 [1024], P('pix')
- grad_out: float32 [1024, 1024], P(None, 'pix')
- grad_first: float32 [1024, 1024], P(None, 'pix')
- grad_second: float32 [1024, 1024], P(None, 'pix')
- grad_qkv: float32 [1024, 3072], P(None, 'pix')
- grad_self_out: float32 [1024, 1024], P(None, 'pix')
- grad_third: float32 [1024, 1024], P(None, 'pix')
- grad_fourth: float32 [1024, 1024], P(None, 'pix')
- grad_gains: float32 [4, 1024], P(None, 'pix')
- grad_shifts: float32 [4, 1024], P(None, 'pix')
- grad_biases: float32 [9, 1024], P(None, 'pix')
- grad_pix_gain: float32 [261], replicated
- grad_pix_shift: float32 [261], replicated
The draws below stay inside these ranges and needn't reach their ends.
Inputs may be any that keep to these rules, and one draw needn't show every extreme that they name: `keep_mask`: 1 keeps a pixel, 0 drops it; the first pixel of every image is kept, and each image keeps its own share of its pixels, roughly between a quarter and nineteen twentieths.
All inputs are finite; a program needn't handle non-finite values.
Results may differ from the reference program's by a relative error of at most 0.018.
Values may be sent and summed in bfloat16 or wider, within the bound.
No kernel may reach another device: no remote copies, remote signals or barrier semaphores. Data moves between devices by JAX's collectives and lax.ppermute only.
A program may use at most 512 MiB of HBM per device.

```python
import jax
import jax.numpy as jnp
from jax import lax

D = 1024
C = 261
LATENTS = 512
HEADS = 8
NORMS = 4
BIASES = 9
IMAGES = 8
PIXELS = 6272


def draw_keep_mask(key, part):
    share_key, pixel_key = jax.random.split(jax.random.fold_in(key, 17))
    shares = jax.random.randint(share_key, (IMAGES, 1), 250, 950)
    pixel_rolls = jax.random.randint(pixel_key, (IMAGES, PIXELS), 0, 1000)
    first_pixel = lax.broadcasted_iota(jnp.int32, (IMAGES, PIXELS), 1) == 0
    return jnp.where(first_pixel | (pixel_rolls < shares), 1, 0).astype(jnp.int32)


def steps_of(rng, dims, cuts, smallest, top_value):
    loudness = 1.0
    for position, shards_of in cuts:
        steps = jax.random.uniform(jax.random.fold_in(jax.random.fold_in(rng, 6), position), (shards_of,), jnp.float32, smallest / len(cuts), top_value / len(cuts))
        loudness = loudness * jnp.repeat(jnp.exp(steps), dims[position] // shards_of).reshape((-1,) + (1,) * (len(dims) - 1 - position))
    return loudness


def normal_values(own_key, shape, deviation, limit, cuts=(), held_as=jnp.bfloat16):
    values = jax.random.normal(own_key, shape, jnp.float32) * deviation
    if len(cuts) > 0:
        values = steps_of(own_key, shape, cuts, -0.22, 0.18) * values
    return jnp.clip(values, min=-limit, max=limit).astype(held_as)


def setup_inputs(seed: int = 0) -> dict:
    streams_of = jax.random.split(jax.random.key(seed), 21)
    return {
        "latents": normal_values(streams_of[0], (IMAGES, LATENTS, D), 1.0, 6.0, ((0, 4),)),
        "pixels": normal_values(streams_of[1], (IMAGES, PIXELS, C), 1.0, 6.0, ((0, 4), (1, 8))),
        "keep_mask": draw_keep_mask(jax.random.fold_in(streams_of[20], 71), 0),
        "cotangent": normal_values(streams_of[3], (IMAGES, LATENTS, D), 1.0, 6.0, ((0, 4),)),
        "w_query": normal_values(streams_of[4], (D, D), (D // 4) ** -0.5, 0.375),
        "w_key": normal_values(streams_of[5], (C, D), C ** -0.5, 0.375),
        "w_value": normal_values(streams_of[6], (C, D), C ** -0.5, 0.375),
        "kv_bias": normal_values(streams_of[7], (D,), 0.01, 0.0625),
        "w_out": normal_values(streams_of[8], (D, D), (max(D // 256, 4)) ** -0.5, 3.0),
        "w_first": normal_values(streams_of[9], (D, D), D ** -0.5, 0.1875),
        "w_second": normal_values(streams_of[10], (D, D), D ** -0.5, 0.1875),
        "w_qkv": normal_values(streams_of[11], (D, 3 * D), D ** -0.5, 0.1875),
        "w_self_out": normal_values(streams_of[12], (D, D), (max(D // 16, 4)) ** -0.5, 0.75),
        "w_third": normal_values(streams_of[13], (D, D), D ** -0.5, 0.1875),
        "w_fourth": normal_values(streams_of[14], (D, D), D ** -0.5, 0.1875),
        "norm_gains": jnp.clip(1.0 + 0.1 * jax.random.normal(streams_of[15], (NORMS, D), jnp.float32), 0.5, 1.5).astype(jnp.bfloat16),
        "norm_shifts": normal_values(streams_of[16], (NORMS, D), 0.15, 0.875),
        "proj_biases": normal_values(streams_of[17], (BIASES, D), 0.15, 0.875),
        "pix_gain": jnp.clip(1.0 + 0.1 * jax.random.normal(streams_of[18], (C,), jnp.float32), 0.5, 1.5).astype(jnp.bfloat16),
        "pix_shift": normal_values(streams_of[19], (C,), 0.15, 0.875),
    }


@jax.custom_vjp
def low(v):
    return lax.optimization_barrier(v.astype(jnp.bfloat16)).astype(jnp.float32)

@jax.custom_vjp
def low_back(v):
    return v

def low_keep(v):
    return (low(v), None)

def low_pass(kept, grad):
    return (grad,)

def back_keep(v):
    return (v, None)

def back_low(kept, grad):
    return (low(grad),)
low.defvjp(low_keep, low_pass)
low_back.defvjp(back_keep, back_low)
EPSILON = 1e-05
LOG_TWO = 0.6931471805599453
FLOOR_VALUE = -1e+30
EXACT = lax.Precision.HIGHEST

def layer_norm(values, norm_gain, norm_shift):
    centre = values - lax.optimization_barrier(jnp.mean(values, axis=-1, keepdims=True))
    inverse = lax.rsqrt(lax.optimization_barrier(jnp.mean(centre * centre, axis=-1, keepdims=True)) + EPSILON)
    return centre * inverse * norm_gain + norm_shift

def gelu_exact(values):
    return jax.nn.gelu(values, approximate=False)

def matmul(inputs, weight):
    return low_back(jnp.dot(inputs, weight, precision=EXACT))

def feed_forward(values, first_weight, second_weight, norm_gain, norm_shift, bias_one, bias_two):
    normed = low(layer_norm(values, norm_gain, norm_shift))
    hidden = low(gelu_exact(matmul(normed, first_weight) + bias_one))
    return values + matmul(hidden, second_weight) + bias_two

def softmax_parts(logit_scores, kept_pixels):
    if kept_pixels is None:
        masked = logit_scores
    else:
        masked = jnp.where(kept_pixels, logit_scores, FLOOR_VALUE)
    shift_level = LOG_TWO * jnp.floor(lax.optimization_barrier(jnp.max(masked, axis=-1, keepdims=True)) / LOG_TWO)
    weights = jnp.exp(logit_scores - shift_level)
    if kept_pixels is not None:
        weights = jnp.where(kept_pixels, weights, 0.0)
    return (weights, lax.optimization_barrier(jnp.sum(weights, axis=-1, keepdims=True)))

def one_image(latent, image_pixels, kept_pixels, w_query, w_key, w_value, kv_bias, w_out, w_first, w_second, w_qkv, w_self_out, w_third, w_fourth, norm_gains, norm_shifts, proj_biases, pix_gain, pix_shift):
    model_width = latent.shape[-1]
    normed = low(layer_norm(latent, norm_gains[0], norm_shifts[0]))
    reduced_query = low((matmul(normed, w_query) + proj_biases[0]) * model_width ** (-0.5))
    pixel_normed = low(layer_norm(image_pixels, pix_gain, pix_shift))
    reduced_keys = low(matmul(pixel_normed, w_key))
    reduced_values = low(matmul(pixel_normed, w_value) + kv_bias)
    logit_scores = low_back(jnp.dot(reduced_query, reduced_keys.T, precision=EXACT))
    weights, weight_sum = softmax_parts(logit_scores, kept_pixels[None, :])
    numerator = low_back(jnp.dot(low(weights), reduced_values, precision=EXACT))
    attended = low(numerator / weight_sum)
    after_cross = latent + matmul(attended, w_out) + proj_biases[1]
    middle = feed_forward(after_cross, w_first, w_second, norm_gains[1], norm_shifts[1], proj_biases[2], proj_biases[3])
    self_normed = low(layer_norm(middle, norm_gains[2], norm_shifts[2]))
    mixed_heads = matmul(self_normed, w_qkv)
    head_dim = model_width // HEADS
    head_shape = (latent.shape[0], HEADS, head_dim)
    self_query = low((mixed_heads[:, :model_width] + proj_biases[4]) * head_dim ** (-0.5)).reshape(head_shape)
    self_keys = low(mixed_heads[:, model_width:2 * model_width]).reshape(head_shape)
    self_values = low(mixed_heads[:, 2 * model_width:] + proj_biases[5]).reshape(head_shape)
    self_scores = low_back(jnp.einsum('qhe,khe->hqk', self_query, self_keys, precision=EXACT))
    self_weights, self_sum = softmax_parts(self_scores, None)
    self_numerator = low_back(jnp.einsum('hqk,khe->qhe', low(self_weights), self_values, precision=EXACT))
    self_attended = low((self_numerator / jnp.transpose(self_sum, (1, 0, 2))).reshape(latent.shape))
    after_self = middle + matmul(self_attended, w_self_out) + proj_biases[6]
    return feed_forward(after_self, w_third, w_fourth, norm_gains[3], norm_shifts[3], proj_biases[7], proj_biases[8])

def reference(latents, pixels, keep_mask, cotangent, w_query, w_key, w_value, kv_bias, w_out, w_first, w_second, w_qkv, w_self_out, w_third, w_fourth, norm_gains, norm_shifts, proj_biases, pix_gain, pix_shift):
    params = tuple((weight_arg.astype(jnp.float32) for weight_arg in (w_query, w_key, w_value, kv_bias, w_out, w_first, w_second, w_qkv, w_self_out, w_third, w_fourth, norm_gains, norm_shifts, proj_biases, pix_gain, pix_shift)))
    kept_all = keep_mask > 0

    def forward(latent_all, pixel_all, *weights):

        def per_image(pieces):
            return jax.checkpoint(one_image)(pieces[0], pieces[1], pieces[2], *weights)
        return lax.map(per_image, (latent_all, pixel_all, kept_all))
    outputs, pullback = jax.vjp(forward, latents.astype(jnp.float32), pixels.astype(jnp.float32), *params)
    grads = pullback(cotangent.astype(jnp.float32))
    return (outputs.astype(jnp.bfloat16), grads[0], grads[1], grads[2], grads[3], grads[4], grads[5], grads[6], grads[7], grads[8], grads[9], grads[10], grads[11], grads[12], grads[13], grads[14], grads[15], grads[16], grads[17])
```

```python
import functools

import jax
import jax.numpy as jnp
from jax import lax
from jax.experimental import pallas as pl
from jax.experimental.pallas import tpu as pltpu
from jax.sharding import Mesh
from jax.sharding import PartitionSpec as P

HEADS = 8
EPSILON = 1e-05
LOG_TWO = 0.6931471805599453
FLOOR_VALUE = -1e30
BF = jnp.bfloat16
F32 = jnp.float32
SWAP = [(0, 1), (1, 0)]
PIX = ("chip", "core")


def dot(a, b, ca, cb):
    return lax.dot_general(a, b, (((ca,), (cb,)), ((), ())), preferred_element_type=F32)


def layer_norm(values, norm_gain, norm_shift):
    centre = values - jnp.mean(values, axis=-1, keepdims=True)
    inverse = lax.rsqrt(jnp.mean(centre * centre, axis=-1, keepdims=True) + EPSILON)
    unit_rows = centre * inverse
    return (unit_rows * norm_gain + norm_shift, unit_rows, inverse)


def row_total(values):
    return jnp.sum(values, axis=tuple(range(values.ndim - 1)))


def norm_back(grad, unit_rows, inverse, norm_gain):
    scaled = grad * norm_gain
    d_values = inverse * (
        scaled
        - jnp.mean(scaled, axis=-1, keepdims=True)
        - unit_rows * jnp.mean(scaled * unit_rows, axis=-1, keepdims=True)
    )
    return (d_values, row_total(grad * unit_rows), row_total(grad))


def gelu_exact(values):
    return jax.nn.gelu(values, approximate=False)


def three_parts(values):
    high = values.astype(BF).astype(F32)
    rest = values - high
    middle = rest.astype(BF).astype(F32)
    return (high, middle, rest - middle)


ROOT_HALF = 0.7071067811865476
ROOT_TWO_PI = 0.3989422804014327


def trunk_body(
    channels,
    span,
    qkv_span,
    place,
    lat,
    mean,
    stats,
    cot,
    gains,
    shifts,
    biases,
    value_h,
    out_h,
    first_h,
    second_h,
    qkv_h,
    self_h,
    third_h,
    fourth_h,
    result,
    d_after,
    pack,
    small,
    keep_h,
    send_h,
    wv,
    wo,
    w1,
    w2,
    wq,
    ws,
    w3,
    w4,
    att,
    dg1,
    h1,
    x2,
    qkv,
    wl,
    inv_total,
    sl,
    x3,
    dg4,
    h4,
    acc,
    low,
    normed,
    stat,
    sums,
    stage,
    load_sem,
    store_sem,
):
    rows, width = lat.shape
    head_dim = width // HEADS
    head_scale = head_dim ** (-0.5)
    x1 = d_after
    block = min(128, rows)
    chip_start, qkv_start, flip = place[0], place[1], place[2]

    loads = []
    for at, (src, dst) in enumerate(
        [
            (value_h, wv),
            (out_h, wo),
            (first_h, w1),
            (second_h, w2),
            (qkv_h, wq),
            (self_h, ws),
            (third_h, w3),
            (fourth_h, w4),
        ]
    ):
        copy = pltpu.make_async_copy(src, dst, load_sem.at[at])
        copy.start()
        loads.append(copy)

    def over_rows(step):
        def run(i, carry):
            step(pl.ds(pl.multiple_of(i * block, block), block))
            return carry

        lax.fori_loop(0, rows // block, run, 0)

    def vector(ref, i):
        return ref[i : i + 1, :].astype(F32)

    def add_sum(at, value):
        sums[at] += jnp.sum(value.reshape(-1, 8, width), axis=0)

    def clear(*ats):
        for at in ats:
            sums[at] = jnp.zeros((8, width), F32)

    def flush(at, row):
        small[row : row + 1, :] = jnp.sum(sums[at], axis=0, keepdims=True)

    def norm_forward(x, i):
        g, s = vector(gains, i), vector(shifts, i)

        def step(at):
            v = x[at, :]
            m = jnp.mean(v, axis=1, keepdims=True)
            c = v - m
            iv = lax.rsqrt(jnp.mean(c * c, axis=1, keepdims=True) + EPSILON)
            normed[at, :] = (c * iv * g + s).astype(BF)
            stat[i - 1, 0, at, :] = jnp.broadcast_to(m, (block, 128))
            stat[i - 1, 1, at, :] = jnp.broadcast_to(iv, (block, 128))

        over_rows(step)

    def norm_again(x, i):
        g, s = vector(gains, i), vector(shifts, i)

        def step(at):
            m, iv = stat[i - 1, 0, at, 0:1], stat[i - 1, 1, at, 0:1]
            normed[at, :] = ((x[at, :] - m) * iv * g + s).astype(BF)

        over_rows(step)

    def norm_backward(x, skip, i, gain_row, shift_row, bias_row):
        g = vector(gains, i)
        clear(0, 1, 2)

        def step(at):
            m, iv = stat[i - 1, 0, at, 0:1], stat[i - 1, 1, at, 0:1]
            unit = (x[at, :] - m) * iv
            grad = acc[at, :]
            scaled = grad * g
            mean_one = jnp.mean(scaled, axis=1, keepdims=True)
            mean_two = jnp.mean(scaled * unit, axis=1, keepdims=True)
            total = skip[at, :].astype(F32) + iv * (scaled - mean_one - unit * mean_two)
            add_sum(0, grad * unit)
            add_sum(1, grad)
            add_sum(2, total)
            x[at, :] = total
            low[at, :] = total.astype(BF)

        over_rows(step)
        flush(0, gain_row)
        flush(1, shift_row)
        flush(2, bias_row)

    def hidden(bias_row, h, dg):
        b = vector(biases, bias_row)

        def step(at):
            v = acc[at, :] + b
            cdf = 0.5 * (1.0 + lax.erf(v * ROOT_HALF))
            h[at, :] = (v * cdf).astype(BF)
            dg[at, :] = cdf + v * (jnp.exp(-0.5 * v * v) * ROOT_TWO_PI)

        over_rows(step)

    def hidden_back(dg, bias_row):
        clear(0)

        def step(at):
            d = acc[at, :] * dg[at, :]
            add_sum(0, d)
            low[at, :] = d.astype(BF)

        over_rows(step)
        flush(0, bias_row)

    pending = [[], []]
    state = {"slot": 0, "row": 0}

    def emit(x, dy, start, span, ca):
        count = x.shape[1 - ca]
        blocks = span // 128
        for t in range(span // 256):
            slot = state["slot"]
            state["slot"] = 1 - slot
            for waiting in pending[slot]:
                waiting.wait()
            pending[slot] = []
            cols = pl.ds(pl.multiple_of(start + t * 256, 128), 256)
            stage[slot, :count, :] = dot(x[...], dy[:, cols], ca, 0).astype(BF)
            for side in range(2):
                at = 2 * t + side
                owner = at // (blocks // 2)
                target = pl.ds(state["row"] + (at % (blocks // 2)) * count, count)
                src = stage.at[slot, pl.ds(0, count), pl.ds(side * 128, 128)]
                sem = store_sem.at[slot, side]
                here = pltpu.make_async_copy(src, keep_h.at[target, :], sem)
                there = pltpu.make_async_copy(src, send_h.at[target, :], sem)

                @pl.when(flip == owner)
                def _():
                    here.start()

                @pl.when(flip != owner)
                def _():
                    there.start()

                pending[slot].append(here)
        state["row"] += count * (blocks // 2)

    loads[0].wait()
    att[...] = dot(mean[...], wv[...], 0, 0).astype(BF)
    loads[1].wait()
    acc[...] = dot(att[...], wo[...], 1, 0)
    out_bias = vector(biases, 1)

    def after_cross(at):
        x1[at, :] = lat[at, :].astype(F32) + acc[at, :] + out_bias

    over_rows(after_cross)
    norm_forward(x1, 1)
    loads[2].wait()
    acc[...] = dot(normed[...], w1[...], 1, 0)
    hidden(2, h1, dg1)
    loads[3].wait()
    x2[...] = x1[...] + dot(h1[...], w2[...], 1, 0) + vector(biases, 3)
    norm_forward(x2, 2)
    loads[4].wait()
    qkv[:, :width] = (
        (dot(normed[...], wq[:, :width], 1, 0) + vector(biases, 4)) * head_scale
    ).astype(BF)
    qkv[:, width : 2 * width] = dot(normed[...], wq[:, width : 2 * width], 1, 0).astype(BF)
    qkv[:, 2 * width :] = (
        dot(normed[...], wq[:, 2 * width :], 1, 0) + vector(biases, 5)
    ).astype(BF)
    ones = jnp.ones((rows, head_dim), BF)

    def head_at(h, part):
        return pl.ds(pl.multiple_of(h * head_dim + part * width, head_dim), head_dim)

    def head_forward(h, carry):
        scores = dot(qkv[:, head_at(h, 0)], qkv[:, head_at(h, 1)], 1, 1)
        top = jnp.max(scores, axis=1, keepdims=True)
        shift = LOG_TWO * jnp.floor(top / LOG_TWO)
        weights = jnp.exp(scores - shift).astype(BF)
        wl[h] = weights
        value = jnp.concatenate([qkv[:, head_at(h, 2)], ones], axis=1)
        both = dot(weights, value, 1, 0)
        over = 1.0 / both[:, head_dim:]
        inv_total[:, head_at(h, 0)] = over
        sl[:, head_at(h, 0)] = (both[:, :head_dim] * over).astype(BF)
        return carry

    lax.fori_loop(0, HEADS, head_forward, 0)
    loads[5].wait()
    x3[...] = x2[...] + dot(sl[...], ws[...], 1, 0) + vector(biases, 6)
    norm_forward(x3, 3)
    loads[6].wait()
    acc[...] = dot(normed[...], w3[...], 1, 0)
    hidden(7, h4, dg4)
    loads[7].wait()
    result[...] = (x3[...] + dot(h4[...], w4[...], 1, 0) + vector(biases, 8)).astype(BF)

    clear(0)

    def cot_sum(at):
        add_sum(0, cot[at, :].astype(F32))

    over_rows(cot_sum)
    flush(0, 13)
    emit(h4, cot, chip_start, span, 0)
    acc[...] = dot(cot[...], w4[...], 1, 1)
    hidden_back(dg4, 12)
    emit(normed, low, chip_start, span, 0)
    acc[...] = dot(low[...], w3[...], 1, 1)
    norm_backward(x3, cot, 3, 2, 5, 11)
    emit(sl, low, chip_start, span, 0)
    acc[...] = dot(low[...], ws[...], 1, 1)
    clear(0, 1)

    def head_backward(h, carry):
        head = head_at(h, 0)
        query, keys, value = qkv[:, head], qkv[:, head_at(h, 1)], qkv[:, head_at(h, 2)]
        grad = acc[:, head] * inv_total[:, head]
        numer_grad = grad.astype(BF)
        total_part = (-(grad * sl[:, head].astype(F32))).astype(BF)
        weights = wl[h]
        d_weights = dot(
            jnp.concatenate([numer_grad, total_part], axis=1),
            jnp.concatenate([value, ones], axis=1),
            1,
            1,
        )
        score_grad = (d_weights * weights.astype(F32)).astype(BF)
        d_value = dot(weights, numer_grad, 0, 0)
        d_query = dot(score_grad, keys, 1, 0) * head_scale
        d_keys = dot(score_grad, query, 0, 0)
        qkv[:, head] = d_query.astype(BF)
        qkv[:, head_at(h, 1)] = d_keys.astype(BF)
        qkv[:, head_at(h, 2)] = d_value.astype(BF)
        sums[0, :, head] = jnp.sum(d_query.reshape(-1, 8, head_dim), axis=0)
        sums[1, :, head] = jnp.sum(d_value.reshape(-1, 8, head_dim), axis=0)
        return carry

    lax.fori_loop(0, HEADS, head_backward, 0)
    flush(0, 9)
    flush(1, 10)
    norm_again(x2, 2)
    emit(normed, qkv, qkv_start, qkv_span, 0)
    acc[...] = dot(qkv[...], wq[...], 1, 1)
    norm_backward(x2, x3, 2, 1, 4, 8)
    emit(h1, low, chip_start, span, 0)
    acc[...] = dot(low[...], w2[...], 1, 1)
    hidden_back(dg1, 7)
    norm_again(x1, 1)
    emit(normed, low, chip_start, span, 0)
    acc[...] = dot(low[...], w1[...], 1, 1)
    norm_backward(x1, x2, 1, 0, 3, 6)
    emit(att, low, chip_start, span, 0)
    low[...] = dot(low[...], wo[...], 1, 1).astype(BF)
    emit(mean, low, chip_start, span, 1)
    grad_pix = dot(wv[...], low[...], 1, 1)
    over = stats[0:1, :]
    row = lax.broadcasted_iota(jnp.int32, grad_pix.shape, 0)
    line = jnp.sum(jnp.where(row == channels, grad_pix, 0.0), axis=0, keepdims=True)
    line = (line - jnp.sum(grad_pix * mean[...].astype(F32), axis=0, keepdims=True)) * over
    high = line.astype(BF).astype(F32)
    packed = jnp.where(row < channels, grad_pix * over, 0.0)
    extras = [high, line - high, stats[1:2, :], stats[2:3, :], stats[3:4, :]]
    for at, extra in enumerate(extras):
        packed = jnp.where(row == channels + at, extra, packed)
    pack[...] = packed.astype(BF)
    for slot in range(2):
        for waiting in pending[slot]:
            waiting.wait()

def trunk(place, lat, mean, stats, cot, gains, shifts, biases, weights, channels, span, qkv_span):
    rows, width = lat.shape
    padded = mean.shape[0]
    sent = width * (3 * (span // 256) + 3 * (span // 256) + qkv_span // 256) + padded * (span // 256)
    vmem = pl.BlockSpec(memory_space=pltpu.VMEM)
    anywhere = pl.BlockSpec(memory_space=pl.ANY)
    big = pltpu.VMEM((rows, width), F32)
    half = pltpu.VMEM((rows, width), BF)
    out_shape = (
        jax.ShapeDtypeStruct((rows, width), BF),
        jax.ShapeDtypeStruct((rows, width), F32),
        jax.ShapeDtypeStruct((padded, rows), BF),
        jax.ShapeDtypeStruct((16, width), F32),
        jax.ShapeDtypeStruct((sent, 128), BF),
        jax.ShapeDtypeStruct((sent, 128), BF),
    )
    scratch = [pltpu.VMEM(w.shape, BF) for w in weights] + [
        half,
        big,
        half,
        big,
        pltpu.VMEM((rows, 3 * width), BF),
        pltpu.VMEM((HEADS, rows, rows), BF),
        big,
        half,
        big,
        big,
        half,
        big,
        half,
        half,
        pltpu.VMEM((3, 2, rows, 128), F32),
        pltpu.VMEM((3, 8, width), F32),
        pltpu.VMEM((2, width, 256), BF),
        pltpu.SemaphoreType.DMA((8,)),
        pltpu.SemaphoreType.DMA((2, 2)),
    ]
    return pl.pallas_call(
        functools.partial(trunk_body, channels, span, qkv_span),
        out_shape=out_shape,
        in_specs=[pl.BlockSpec(memory_space=pltpu.SMEM)] + [vmem] * 7 + [anywhere] * 8,
        out_specs=[vmem] * 4 + [anywhere] * 2,
        scratch_shapes=scratch,
        compiler_params=pltpu.CompilerParams(vmem_limit_bytes=60 << 20),
        cost_estimate=pl.CostEstimate(
            flops=30 * 2 * rows * width * width, transcendentals=8 * rows * rows, bytes_accessed=30 << 20
        ),
        name="trunk",
    )(place, lat, mean, stats, cot, gains, shifts, biases, *weights)


def shifted(devices, step):
    return [(i, (i + step) % devices) for i in range(devices)]


def exchange(tiles, axis):
    devices = tiles.shape[0]
    if devices == 1:
        return tiles
    place = lax.axis_index(axis)
    got = [lax.dynamic_index_in_dim(tiles, place, 0, keepdims=False)]
    for step in range(1, devices):
        tile = lax.dynamic_index_in_dim(tiles, (place + step) % devices, 0, keepdims=False)
        got.append(lax.ppermute(tile, axis, shifted(devices, step)))
    return jnp.stack(got)


def gather(tile, axis):
    devices = lax.axis_size(axis)
    place = lax.axis_index(axis)
    got = [tile]
    for step in range(1, devices):
        got.append(lax.ppermute(tile, axis, shifted(devices, step)))
    stacked = jnp.stack(got)
    order = (place - jnp.arange(devices)) % devices
    return jnp.stack([lax.dynamic_index_in_dim(stacked, order[i], 0, keepdims=False) for i in range(devices)])


def in_tiles(rows, devices):
    return jnp.moveaxis(rows.reshape(rows.shape[0], devices, -1), 1, 0)


def from_tiles(tiles):
    return jnp.moveaxis(tiles, 0, 1).reshape(tiles.shape[1], -1)


def image_parts(rows):
    count = rows.shape[0]
    quarter = -(-count // 64) * 16
    tiles = jnp.pad(rows, ((0, 4 * quarter - count), (0, 0))).reshape(4, quarter, -1)
    return tiles


LOW_PAIRS = [(0, 1), (1, 0), (2, 3), (3, 2)]
HIGH_PAIRS = [(0, 2), (2, 0), (1, 3), (3, 1)]


def pick(pair, at):
    return jnp.where(at == 0, pair[0], pair[1])


def plus(a, b):
    return (a.astype(F32) + b.astype(F32)).astype(BF)


def image_places():
    place = lax.axis_index("img")
    return place // 2, place % 2


def image_first(rows):
    high, low = image_places()
    tiles = image_parts(rows)
    one, two = tiles[:2], tiles[2:]
    got_one = lax.ppermute(pick(one, 1 - low), "img", LOW_PAIRS)
    got_two = lax.ppermute(pick(two, 1 - high), "img", HIGH_PAIRS)
    return plus(pick(one, low), got_one), plus(pick(two, high), got_two)


def image_second(one, two):
    got_one = lax.ppermute(one, "img", HIGH_PAIRS)
    got_two = lax.ppermute(two, "img", LOW_PAIRS)
    return plus(one, got_one), plus(two, got_two)


def image_third(one, two):
    return lax.ppermute(one, "img", LOW_PAIRS), lax.ppermute(two, "img", HIGH_PAIRS)


def image_whole(one, two, got_one, got_two, count):
    high, low = image_places()
    whole = jnp.concatenate(
        [
            jnp.where(low == 0, one, got_one),
            jnp.where(low == 0, got_one, one),
            jnp.where(high == 0, two, got_two),
            jnp.where(high == 0, got_two, two),
        ]
    )
    return whole[:count]


def image_sum(rows):
    one, two = image_second(*image_first(rows))
    return image_whole(one, two, *image_third(one, two), rows.shape[0])


def on_device(
    latents,
    pixels,
    keep_mask,
    cotangent,
    w_query,
    w_key,
    w_value,
    kv_bias,
    w_out,
    w_first,
    w_second,
    w_qkv,
    w_self_out,
    w_third,
    w_fourth,
    norm_gains,
    norm_shifts,
    proj_biases,
    pix_gain,
    pix_shift,
):
    width = latents.shape[-1]
    rows = latents.shape[1]
    channels = pixels.shape[-1]
    padded = -(-(channels + 8) // 16) * 16
    cross_scale = width ** (-0.5)
    chips = lax.axis_size("chip")
    chip = lax.axis_index("chip")
    core = lax.axis_index("core")
    piece = width // (chips * 2)

    def columns(values):
        span = values.shape[-1] // chips
        return lax.dynamic_slice_in_dim(values, chip * span, span, values.ndim - 1)

    def mine(values):
        return lax.dynamic_index_in_dim(values, core, 0, keepdims=False)

    def other(values):
        return lax.dynamic_index_in_dim(values, 1 - core, 0, keepdims=False)

    def swapped(values):
        return lax.ppermute(values, "core", SWAP)

    gains = norm_gains.astype(F32)
    shifts = norm_shifts.astype(F32)
    biases = proj_biases.astype(F32)
    pixel_gain = pix_gain.astype(F32)
    pixel_shift = pix_shift.astype(F32)
    key_rows = jnp.pad(w_key, ((0, padded - channels), (0, 0)))
    value_rows = jnp.concatenate(
        [w_value, kv_bias[None], jnp.zeros((padded - channels - 1, width), BF)]
    )

    q_normed, _, _ = layer_norm(latents.astype(F32), gains[0], shifts[0])
    q_normed_low = q_normed.astype(BF)
    query = (
        (dot(q_normed_low.reshape(-1, width), w_query, 1, 0) + biases[0]) * cross_scale
    ).astype(BF)
    query_pix = jnp.stack(
        [dot(key_rows, query[:rows], 1, 1), dot(key_rows, query[rows:], 1, 1)]
    ).astype(BF)
    p_normed, p_unit, p_inverse = layer_norm(pixels.astype(F32), pixel_gain, pixel_shift)
    lane = jnp.arange(padded)
    ones_lanes = ((lane == channels) | (lane == channels + 1)).astype(BF)
    pix_low = jnp.pad(p_normed.astype(BF), ((0, 0), (0, 0), (0, padded - channels))) + ones_lanes
    kept_pixels = keep_mask[:, :, None] > 0
    scores = jnp.einsum("bpc,bci->bpi", pix_low, query_pix, preferred_element_type=F32)
    local_top = jnp.max(jnp.where(kept_pixels, scores, FLOOR_VALUE), axis=1)
    level = jnp.floor(local_top / LOG_TWO)
    first_weights = jnp.where(
        kept_pixels, jnp.exp(scores - (level * LOG_TWO)[:, None, :]), 0.0
    ).astype(BF)
    local_numer = jnp.einsum("bpc,bpi->bci", pix_low, first_weights, preferred_element_type=F32)

    def packed(body, extras):
        lead = jnp.concatenate([body] + [e[None, :] for e in extras]).astype(BF)
        return jnp.pad(lead, ((0, padded - lead.shape[0]), (0, 0)))

    def fwd_pack(numer, level):
        total = numer[channels]
        return packed(numer[:channels], three_parts(total)[:2] + three_parts(level))

    def fwd_unpack(pack):
        pack = pack.astype(F32)
        total = pack[channels] + pack[channels + 1]
        level = pack[channels + 2] + pack[channels + 3] + pack[channels + 4]
        return (jnp.concatenate([pack[:channels], total[None]]), level)

    def joined(parts):
        top = parts[0][1]
        for _, level in parts[1:]:
            top = jnp.maximum(top, level)
        return (sum(body * jnp.exp2(level - top)[None, :] for body, level in parts), top)

    sent = swapped(fwd_pack(other(local_numer), other(level)))
    body, top = joined([(mine(local_numer)[: channels + 1], mine(level)), fwd_unpack(sent)])
    got = exchange(in_tiles(fwd_pack(body, top), chips), "chip")
    body, top = joined([fwd_unpack(got[i]) for i in range(chips)])
    mean_tile = packed(
        body[:channels] / body[channels], three_parts(body[channels]) + three_parts(top)
    )
    mean_all = from_tiles(gather(mean_tile, "chip")).astype(F32)
    cross_total = mean_all[channels] + mean_all[channels + 1] + mean_all[channels + 2]
    cross_level = mean_all[channels + 3] + mean_all[channels + 4] + mean_all[channels + 5]
    row = jnp.arange(padded)[:, None]
    mean_pix = jnp.where(row < channels, mean_all, jnp.where(row == channels, 1.0, 0.0))
    mean_low = mean_pix.astype(BF)

    _, q_unit, q_inverse = layer_norm(mine(latents).astype(F32), gains[0], shifts[0])
    fast = piece % 128 == 0
    if fast:
        span, qkv_span = 2 * piece, 6 * piece
        starts = (chip * span, chip * qkv_span)
        flip = core
    else:
        span, qkv_span = 256, 256
        starts = tuple(
            jnp.minimum(chip * size // chips // 128 * 128, size - 256) for size in (width, 3 * width)
        )
        flip = 0 * core
    place = jnp.stack([starts[0], starts[1], flip]).astype(jnp.int32)
    stats = jnp.concatenate(
        [
            (1.0 / cross_total)[None],
            mean_all[channels + 3 : channels + 6],
            jnp.zeros((4, rows), F32),
        ]
    )
    output, d_after, own_pack, small_grads, keep, send = trunk(
        place,
        mine(latents),
        mean_low,
        stats,
        mine(cotangent),
        norm_gains,
        norm_shifts,
        proj_biases,
        [value_rows, w_out, w_first, w_second, w_qkv, w_self_out, w_third, w_fourth],
        channels,
        span,
        qkv_span,
    )
    def flat(arrays):
        return jnp.concatenate(
            [a.reshape(a.shape[0], -1, piece).swapaxes(0, 1).reshape(-1, piece) for a in arrays]
        ).astype(BF)

    def split(grads):
        keep, send = [], []
        for g in grads:
            half = g.shape[-1] // 2
            keep.append(lax.dynamic_slice_in_dim(g, core * half, half, 1))
            send.append(lax.dynamic_slice_in_dim(g, (1 - core) * half, half, 1))
        return flat(keep), flat(send)

    squares = [(width, piece)] * 3
    spans = squares + [(width, 3 * piece)] + squares + [(padded, piece)]
    if not fast:
        blocks, at = [], 0
        for r, c in spans:
            size = c * chips * 2
            block = jnp.concatenate([keep[at : at + r], send[at : at + r]], axis=1)
            offset = chip * 2 * c - (starts[1] if size > width else starts[0])
            blocks.append(lax.dynamic_slice_in_dim(block, offset, 2 * c, 1))
            at += r
        keep, send = split(blocks)
    got_pack, got_send = lax.optimization_barrier((swapped(own_pack), swapped(send)))
    both_cores = plus(keep, got_send)
    got_pack, both_cores = lax.optimization_barrier((got_pack, both_cores))
    one, two = image_first(both_cores)
    both = jnp.where(core == 0, jnp.stack([own_pack, got_pack]), jnp.stack([got_pack, own_pack]))

    levels = jnp.sum(both[:, channels + 2 : channels + 5].astype(F32), axis=1)
    weights = jnp.where(kept_pixels, jnp.exp(scores - (levels * LOG_TWO)[:, None, :]), 0.0)
    grad_rows = jnp.where(row[None] < channels + 2, both, jnp.zeros((), BF))
    d_weights = jnp.einsum("bpc,bci->bpi", pix_low, grad_rows, preferred_element_type=F32)
    score_grad = (d_weights * weights).astype(BF)
    query_part = jnp.einsum("bpc,bpi->bci", pix_low, score_grad, preferred_element_type=F32)
    d_pix_normed = jnp.einsum(
        "bpi,bci->bpc", score_grad, query_pix, preferred_element_type=F32
    ) + jnp.einsum("bpi,bci->bpc", weights.astype(BF), grad_rows, preferred_element_type=F32)
    d_pix_normed = d_pix_normed[..., :channels]
    scaled = d_pix_normed * pixel_gain
    d_pixels = p_inverse * (
        scaled
        - jnp.mean(scaled, axis=-1, keepdims=True)
        - p_unit * jnp.mean(scaled * p_unit, axis=-1, keepdims=True)
    )
    pix_sums = jnp.stack(
        [jnp.sum(d_pix_normed * p_unit, axis=1), jnp.sum(d_pix_normed, axis=1)], axis=1
    )
    pix_sums = jnp.pad(pix_sums, ((0, 0), (0, 0), (0, rows - channels)))

    def bwd_pack(body, sums):
        high, low, _ = three_parts(sums)
        return packed(body[:channels], [high[0], low[0], high[1], low[1]])

    def bwd_unpack(pack):
        pack = pack.astype(F32)
        sums = jnp.stack(
            [pack[channels] + pack[channels + 1], pack[channels + 2] + pack[channels + 3]]
        )
        return (pack[:channels], sums)

    query_part, pix_sums, one, two = lax.optimization_barrier((query_part, pix_sums, one, two))
    one, two = image_second(one, two)
    sent = swapped(bwd_pack(other(query_part), other(pix_sums)))
    body_two, sums_two = bwd_unpack(sent)
    body, sums = (mine(query_part)[:channels] + body_two, mine(pix_sums) + sums_two)
    got = exchange(in_tiles(bwd_pack(body, sums), chips), "chip")
    got = [bwd_unpack(got[i]) for i in range(chips)]
    body, sums = (sum(g[0] for g in got), sum(g[1] for g in got))
    body, sums, one, two = lax.optimization_barrier((body, sums, one, two))
    got_one, got_two = image_third(one, two)
    all_parts = from_tiles(gather(bwd_pack(body, sums), "chip"))
    _, sums = bwd_unpack(all_parts)
    query_sum = jnp.where(row < channels, all_parts, jnp.zeros((), BF))

    d_query = dot(query_sum, key_rows, 0, 0) * cross_scale
    d_query_low = d_query.astype(BF)
    own_normed = mine(q_normed_low)
    own_query = lax.dynamic_slice_in_dim(query, core * rows, rows, 0)
    d_w_query = dot(own_normed, columns(d_query_low), 0, 0)
    d_w_key = dot(query_sum, columns(own_query), 1, 0)
    d_q_normed = dot(d_query_low, w_query, 1, 1)
    d_q_in, d_gain_zero, d_shift_zero = norm_back(d_q_normed, q_unit, q_inverse, gains[0])
    d_latents_own = d_after + d_q_in

    def two_images(own):
        got = swapped(own.astype(BF)).astype(own.dtype)
        return jnp.where(core == 0, jnp.stack([own, got]), jnp.stack([got, own]))

    def unpacked(whole, spans):
        outs, at = [], 0
        for r, c in spans:
            count = r * (c // piece)
            part = whole[at : at + count].reshape(c // piece, r, piece).swapaxes(0, 1).reshape(r, c)
            outs.append(part.astype(F32))
            at += count
        return outs

    def reduced(keep, send, spans):
        return unpacked(image_sum(plus(keep, swapped(send))), spans)

    small = jnp.concatenate(
        [
            d_gain_zero[None],
            small_grads[0:3],
            d_shift_zero[None],
            small_grads[3:6],
            row_total(d_query)[None],
            small_grads[6:14],
        ]
    )
    sum_lanes = -(-channels // piece) * piece
    pix_rows = sums[:, :sum_lanes].reshape(-1, piece)
    pix_rows = jnp.concatenate([pix_rows, pix_rows], axis=1)
    last_spans = [(width, piece), (padded, piece), (small.shape[0], piece), (pix_rows.shape[0], piece)]
    keep, send = split([d_w_query, d_w_key, columns(small), pix_rows])
    keep, send, got_one, got_two = lax.optimization_barrier((keep, send, got_one, got_two))
    last = reduced(keep, send, last_spans)
    main = unpacked(image_whole(one, two, got_one, got_two, both_cores.shape[0]), spans)
    d_small = last[2]
    pix_out = last[3].reshape(2, sum_lanes)
    return (
        two_images(output.astype(BF)),
        two_images(d_latents_own),
        d_pixels,
        last[0],
        last[1][:channels],
        main[7][:channels],
        main[7][channels],
        main[6],
        main[5],
        main[4],
        main[3],
        main[2],
        main[1],
        main[0],
        d_small[0:4],
        d_small[4:8],
        d_small[8:17],
        pix_out[0, :channels],
        pix_out[1, :channels],
    )


def solution(mesh):
    images, pieces = mesh.devices.shape
    split = Mesh(mesh.devices.reshape(images, pieces // 2, 2), ("img", "chip", "core"))
    latent = P("img", None, None)
    weight = P(None, PIX)
    placed = (latent, P("img", PIX, None), P("img", PIX), latent) + (P(),) * 16
    return jax.shard_map(
        on_device,
        mesh=split,
        in_specs=placed,
        out_specs=(latent, latent, P("img", PIX, None), weight, weight, weight, P(PIX))
        + (weight,) * 10
        + (P(), P()),
        check_vma=False,
    )
```

```python
import functools

import jax
import jax.numpy as jnp
from jax import lax
from jax.experimental import pallas as pl
from jax.experimental.pallas import tpu as pltpu
from jax.sharding import Mesh
from jax.sharding import PartitionSpec as P

HEADS = 8
EPSILON = 1e-05
LOG_TWO = 0.6931471805599453
FLOOR_VALUE = -1e30
BF = jnp.bfloat16
F32 = jnp.float32
SWAP = [(0, 1), (1, 0)]
PIX = ("chip", "core")


def dot(a, b, ca, cb):
    return lax.dot_general(a, b, (((ca,), (cb,)), ((), ())), preferred_element_type=F32)


def layer_norm(values, norm_gain, norm_shift):
    centre = values - jnp.mean(values, axis=-1, keepdims=True)
    inverse = lax.rsqrt(jnp.mean(centre * centre, axis=-1, keepdims=True) + EPSILON)
    unit_rows = centre * inverse
    return (unit_rows * norm_gain + norm_shift, unit_rows, inverse)


def row_total(values):
    return jnp.sum(values, axis=tuple(range(values.ndim - 1)))


def norm_back(grad, unit_rows, inverse, norm_gain):
    scaled = grad * norm_gain
    d_values = inverse * (
        scaled
        - jnp.mean(scaled, axis=-1, keepdims=True)
        - unit_rows * jnp.mean(scaled * unit_rows, axis=-1, keepdims=True)
    )
    return (d_values, row_total(grad * unit_rows), row_total(grad))


def gelu_exact(values):
    return jax.nn.gelu(values, approximate=False)


def three_parts(values):
    high = values.astype(BF).astype(F32)
    rest = values - high
    middle = rest.astype(BF).astype(F32)
    return (high, middle, rest - middle)


ROOT_HALF = 0.7071067811865476
ROOT_TWO_PI = 0.3989422804014327


def trunk_core(
    channels,
    span,
    qkv_span,
    chip_start,
    qkv_start,
    flip,
    waits,
    lat,
    mean,
    stats,
    cot,
    gains,
    shifts,
    biases,
    result,
    d_after,
    pack,
    small,
    keep_h,
    send_h,
    wv,
    wo,
    w1,
    w2,
    wq,
    ws,
    w3,
    w4,
    att,
    dg1,
    h1,
    x2,
    qkv,
    wl,
    inv_total,
    sl,
    x3,
    dg4,
    h4,
    acc,
    low,
    normed,
    stat,
    sums,
    stage,
    store_sem,
):
    rows, width = lat.shape
    head_dim = width // HEADS
    head_scale = head_dim ** (-0.5)
    x1 = d_after
    def over_rows(step, most=256):
        block = min(most, rows)

        def run(i, carry):
            step(pl.ds(pl.multiple_of(i * block, block), block))
            return carry

        lax.fori_loop(0, rows // block, run, 0)

    def vector(ref, i):
        return ref[i : i + 1, :].astype(F32)

    def add_sum(at, value):
        sums[at] += jnp.sum(value.reshape(-1, 8, width), axis=0)

    def clear(*ats):
        for at in ats:
            sums[at] = jnp.zeros((8, width), F32)

    def flush(at, row):
        small[row : row + 1, :] = jnp.sum(sums[at], axis=0, keepdims=True)

    def norm_forward(x, i):
        g, s = vector(gains, i), vector(shifts, i)

        def step(at):
            v = x[at, :]
            m = jnp.mean(v, axis=1, keepdims=True)
            c = v - m
            iv = lax.rsqrt(jnp.mean(c * c, axis=1, keepdims=True) + EPSILON)
            normed[at, :] = (c * iv * g + s).astype(BF)
            stat[i - 1, 0, at, :] = jnp.broadcast_to(m, (m.shape[0], 128))
            stat[i - 1, 1, at, :] = jnp.broadcast_to(iv, (m.shape[0], 128))

        over_rows(step)

    def norm_again(x, i):
        g, s = vector(gains, i), vector(shifts, i)

        def step(at):
            m, iv = stat[i - 1, 0, at, 0:1], stat[i - 1, 1, at, 0:1]
            normed[at, :] = ((x[at, :] - m) * iv * g + s).astype(BF)

        over_rows(step)

    def norm_backward(x, skip, i, gain_row, shift_row, bias_row):
        g = vector(gains, i)
        clear(0, 1, 2)

        def step(at):
            m, iv = stat[i - 1, 0, at, 0:1], stat[i - 1, 1, at, 0:1]
            unit = (x[at, :] - m) * iv
            grad = acc[at, :]
            scaled = grad * g
            mean_one = jnp.mean(scaled, axis=1, keepdims=True)
            mean_two = jnp.mean(scaled * unit, axis=1, keepdims=True)
            total = skip[at, :].astype(F32) + iv * (scaled - mean_one - unit * mean_two)
            add_sum(0, grad * unit)
            add_sum(1, grad)
            add_sum(2, total)
            x[at, :] = total
            low[at, :] = total.astype(BF)

        over_rows(step)
        flush(0, gain_row)
        flush(1, shift_row)
        flush(2, bias_row)

    def hidden(bias_row, h, dg):
        b = vector(biases, bias_row)

        def step(at):
            v = acc[at, :] + b
            cdf = 0.5 * (1.0 + lax.erf(v * ROOT_HALF))
            h[at, :] = (v * cdf).astype(BF)
            dg[at, :] = cdf + v * (jnp.exp(-0.5 * v * v) * ROOT_TWO_PI)

        over_rows(step)

    def hidden_back(dg, bias_row):
        clear(0)

        def step(at):
            d = acc[at, :] * dg[at, :]
            add_sum(0, d)
            low[at, :] = d.astype(BF)

        over_rows(step)
        flush(0, bias_row)

    pending = [[], []]
    state = {"slot": 0, "row": 0}

    def emit(x, dy, start, span, ca):
        count = x.shape[1 - ca]
        blocks = span // 128
        for t in range(span // 256):
            slot = state["slot"]
            state["slot"] = 1 - slot
            for waiting in pending[slot]:
                waiting.wait()
            pending[slot] = []
            cols = pl.ds(pl.multiple_of(start + t * 256, 128), 256)
            stage[slot, :count, :] = dot(x[...], dy[:, cols], ca, 0).astype(BF)
            for side in range(2):
                at = 2 * t + side
                owner = at // (blocks // 2)
                target = pl.ds(state["row"] + (at % (blocks // 2)) * count, count)
                src = stage.at[slot, pl.ds(0, count), pl.ds(side * 128, 128)]
                sem = store_sem.at[slot, side]
                here = pltpu.make_async_copy(src, keep_h.at[target, :], sem)
                there = pltpu.make_async_copy(src, send_h.at[target, :], sem)

                @pl.when(flip == owner)
                def _():
                    here.start()

                @pl.when(flip != owner)
                def _():
                    there.start()

                pending[slot].append(here)
        state["row"] += count * (blocks // 2)

    waits[0]()
    att[...] = dot(mean[...], wv[...], 0, 0).astype(BF)
    waits[1]()
    acc[...] = dot(att[...], wo[...], 1, 0)
    out_bias = vector(biases, 1)

    def after_cross(at):
        x1[at, :] = lat[at, :].astype(F32) + acc[at, :] + out_bias

    over_rows(after_cross)
    norm_forward(x1, 1)
    waits[2]()
    acc[...] = dot(normed[...], w1[...], 1, 0)
    hidden(2, h1, dg1)
    waits[3]()
    x2[...] = x1[...] + dot(h1[...], w2[...], 1, 0) + vector(biases, 3)
    norm_forward(x2, 2)
    waits[4]()
    qkv[:, :width] = (
        (dot(normed[...], wq[:, :width], 1, 0) + vector(biases, 4)) * head_scale
    ).astype(BF)
    qkv[:, width : 2 * width] = dot(normed[...], wq[:, width : 2 * width], 1, 0).astype(BF)
    qkv[:, 2 * width :] = (
        dot(normed[...], wq[:, 2 * width :], 1, 0) + vector(biases, 5)
    ).astype(BF)
    ones = jnp.ones((rows, head_dim), BF)

    def head_at(h, part):
        return pl.ds(pl.multiple_of(h * head_dim + part * width, head_dim), head_dim)

    def head_forward(h, carry):
        scores = dot(qkv[:, head_at(h, 0)], qkv[:, head_at(h, 1)], 1, 1)
        top = jnp.max(scores, axis=1, keepdims=True)
        shift = LOG_TWO * jnp.floor(top / LOG_TWO)
        weights = jnp.exp(scores - shift).astype(BF)
        wl[h] = weights
        value = jnp.concatenate([qkv[:, head_at(h, 2)], ones], axis=1)
        both = dot(weights, value, 1, 0)
        over = 1.0 / both[:, head_dim:]
        inv_total[:, head_at(h, 0)] = over
        sl[:, head_at(h, 0)] = (both[:, :head_dim] * over).astype(BF)
        return carry

    lax.fori_loop(0, HEADS, head_forward, 0, unroll=True)
    waits[5]()
    x3[...] = x2[...] + dot(sl[...], ws[...], 1, 0) + vector(biases, 6)
    norm_forward(x3, 3)
    waits[6]()
    acc[...] = dot(normed[...], w3[...], 1, 0)
    hidden(7, h4, dg4)
    waits[7]()
    result[...] = (x3[...] + dot(h4[...], w4[...], 1, 0) + vector(biases, 8)).astype(BF)

    waits[8]()
    clear(0)

    def cot_sum(at):
        add_sum(0, cot[at, :].astype(F32))

    over_rows(cot_sum)
    flush(0, 13)
    emit(h4, cot, chip_start, span, 0)
    acc[...] = dot(cot[...], w4[...], 1, 1)
    hidden_back(dg4, 12)
    emit(normed, low, chip_start, span, 0)
    acc[...] = dot(low[...], w3[...], 1, 1)
    norm_backward(x3, cot, 3, 2, 5, 11)
    emit(sl, low, chip_start, span, 0)
    acc[...] = dot(low[...], ws[...], 1, 1)
    clear(0, 1)

    def head_backward(h, carry):
        head = head_at(h, 0)
        query, keys, value = qkv[:, head], qkv[:, head_at(h, 1)], qkv[:, head_at(h, 2)]
        grad = acc[:, head] * inv_total[:, head]
        numer_grad = grad.astype(BF)
        total_part = (-(grad * sl[:, head].astype(F32))).astype(BF)
        weights = wl[h]
        d_weights = dot(
            jnp.concatenate([numer_grad, total_part], axis=1),
            jnp.concatenate([value, ones], axis=1),
            1,
            1,
        )
        score_grad = (d_weights * weights.astype(F32)).astype(BF)
        d_value = dot(weights, numer_grad, 0, 0)
        d_query = dot(score_grad, keys, 1, 0) * head_scale
        d_keys = dot(score_grad, query, 0, 0)
        qkv[:, head] = d_query.astype(BF)
        qkv[:, head_at(h, 1)] = d_keys.astype(BF)
        qkv[:, head_at(h, 2)] = d_value.astype(BF)
        sums[0, :, head] = jnp.sum(d_query.reshape(-1, 8, head_dim), axis=0)
        sums[1, :, head] = jnp.sum(d_value.reshape(-1, 8, head_dim), axis=0)
        return carry

    lax.fori_loop(0, HEADS, head_backward, 0, unroll=True)
    flush(0, 9)
    flush(1, 10)
    norm_again(x2, 2)
    emit(normed, qkv, qkv_start, qkv_span, 0)
    acc[...] = dot(qkv[...], wq[...], 1, 1)
    norm_backward(x2, x3, 2, 1, 4, 8)
    emit(h1, low, chip_start, span, 0)
    acc[...] = dot(low[...], w2[...], 1, 1)
    hidden_back(dg1, 7)
    norm_again(x1, 1)
    emit(normed, low, chip_start, span, 0)
    acc[...] = dot(low[...], w1[...], 1, 1)
    norm_backward(x1, x2, 1, 0, 3, 6)
    emit(att, low, chip_start, span, 0)
    low[...] = dot(low[...], wo[...], 1, 1).astype(BF)
    emit(mean, low, chip_start, span, 1)
    grad_pix = dot(wv[...], low[...], 1, 1)
    over = stats[0:1, :]
    row = lax.broadcasted_iota(jnp.int32, grad_pix.shape, 0)
    line = jnp.sum(jnp.where(row == channels, grad_pix, 0.0), axis=0, keepdims=True)
    line = (line - jnp.sum(grad_pix * mean[...].astype(F32), axis=0, keepdims=True)) * over
    high = line.astype(BF).astype(F32)
    packed = jnp.where(row < channels, grad_pix * over, 0.0)
    extras = [high, line - high, stats[1:2, :], stats[2:3, :], stats[3:4, :]]
    for at, extra in enumerate(extras):
        packed = jnp.where(row == channels + at, extra, packed)
    pack[...] = packed.astype(BF)
    for slot in range(2):
        for waiting in pending[slot]:
            waiting.wait()


def trunk_slow_body(channels, span, qkv_span, place, lat, mean, stats, cot, gains, shifts, biases, *refs):
    load_sem, store_sem = refs[-2:]
    loads = []
    for at in range(8):
        copy = pltpu.make_async_copy(refs[at], refs[14 + at], load_sem.at[at])
        copy.start()
        loads.append(copy.wait)
    loads.append(lambda: None)
    trunk_core(
        channels, span, qkv_span, place[0], place[1], place[2], loads, lat, mean, stats, cot,
        gains, shifts, biases, *refs[8:-2], store_sem
    )


def trunk_fast_body(channels, chips, place, *refs):
    tiles, refs = refs[:chips], refs[chips:]
    lat_h, cot_h, gains, shifts, biases, value, kv_bias = refs[:7]
    weights_h, refs = refs[7:14], refs[14:]
    lat, cot, mean, raw, stats, tail, load_sem, store_sem = refs[-8:]
    wv = refs[6]
    chip, core = place[0], place[1]
    loads = []
    pairs = [(lat_h.at[core], lat)]
    pairs += [(weights_h[at], refs[7 + at]) for at in range(7)]
    pairs += [(cot_h.at[core], cot)]
    for at, (src, dst) in enumerate(pairs):
        copy = pltpu.make_async_copy(src, dst, load_sem.at[at])
        copy.start()
        loads.append(copy.wait)
    fill_rows(wv, value, tail, kv_bias[...].astype(F32))
    tiles_in(place, raw, tiles)
    full = raw[...].astype(F32)
    mean[...] = jnp.where(row_of(full) <= channels, full, 0.0).astype(BF)
    total = (
        full[channels + 1 : channels + 2]
        + full[channels + 2 : channels + 3]
        + full[channels + 3 : channels + 4]
    )
    stats[0:1, :] = 1.0 / total
    for at in range(3):
        stats[at + 1 : at + 2, :] = full[channels + 4 + at : channels + 5 + at]
    trunk_core(
        channels, 256, 768, chip * 256, chip * 768, core, loads, lat, mean, stats, cot,
        gains, shifts, biases, *refs[:-8], store_sem
    )


def trunk_scratch(rows, width, padded):
    big = pltpu.VMEM((rows, width), F32)
    half = pltpu.VMEM((rows, width), BF)
    square = pltpu.VMEM((width, width), BF)
    return [
        pltpu.VMEM((padded, width), BF),
        square,
        square,
        square,
        pltpu.VMEM((width, 3 * width), BF),
        square,
        square,
        square,
        half,
        big,
        half,
        big,
        pltpu.VMEM((rows, 3 * width), BF),
        pltpu.VMEM((HEADS, rows, rows), BF),
        big,
        half,
        big,
        big,
        half,
        big,
        half,
        half,
        pltpu.VMEM((3, 2, rows, 128), F32),
        pltpu.VMEM((3, 8, width), F32),
        pltpu.VMEM((2, width, 256), BF),
    ]


def trunk_outs(rows, width, padded, sent):
    return [
        ((rows, width), BF),
        ((rows, width), F32),
        ((padded, rows), BF),
        ((16, width), F32),
        ((sent, 128), BF),
        ((sent, 128), BF),
    ]


def trunk_slow(place, lat, mean, stats, cot, gains, shifts, biases, weights, channels, span, qkv_span):
    rows, width = lat.shape
    padded = mean.shape[0]
    sent = width * (6 * (span // 256) + qkv_span // 256) + padded * (span // 256)
    return call(
        functools.partial(trunk_slow_body, channels, span, qkv_span),
        trunk_outs(rows, width, padded, sent),
        trunk_scratch(rows, width, padded)
        + [pltpu.SemaphoreType.DMA((8,)), pltpu.SemaphoreType.DMA((2, 2))],
        (place, lat, mean, stats, cot, gains, shifts, biases, *weights),
        "s" + "v" * 7 + "a" * 8,
        "trunk",
        60 * rows * width * width,
        "vvvvaa",
        60,
    )


def trunk(
    place, tiles, latents, cotangent, gains, shifts, biases, value, kv_bias, weights, channels, padded
):
    _, rows, width = latents.shape
    sent = -(-(9 * width + padded) // 64) * 64
    vm = pltpu.VMEM
    return call(
        functools.partial(trunk_fast_body, channels, len(tiles)),
        trunk_outs(rows, width, padded, sent),
        trunk_scratch(rows, width, padded)
        + [
            vm((rows, width), BF),
            vm((rows, width), BF),
            vm((padded, rows), BF),
            vm((padded, rows), BF),
            vm((8, rows), F32),
            vm((16, width), F32),
            pltpu.SemaphoreType.DMA((9,)),
            pltpu.SemaphoreType.DMA((2, 2)),
        ],
        (place, *tiles, latents, cotangent, gains, shifts, biases, value, kv_bias, *weights),
        "s" + "v" * len(tiles) + "aavvvvv" + "a" * 7,
        "trunk",
        60 * rows * width * width,
        "vvvvaa",
        60,
    )


def shifted(devices, step):
    return [(i, (i + step) % devices) for i in range(devices)]


def exchange(tiles, axis):
    devices = tiles.shape[0]
    if devices == 1:
        return tiles
    place = lax.axis_index(axis)
    got = [lax.dynamic_index_in_dim(tiles, place, 0, keepdims=False)]
    for step in range(1, devices):
        tile = lax.dynamic_index_in_dim(tiles, (place + step) % devices, 0, keepdims=False)
        got.append(lax.ppermute(tile, axis, shifted(devices, step)))
    return jnp.stack(got)


def gather(tile, axis):
    devices = lax.axis_size(axis)
    place = lax.axis_index(axis)
    got = [tile]
    for step in range(1, devices):
        got.append(lax.ppermute(tile, axis, shifted(devices, step)))
    stacked = jnp.stack(got)
    order = (place - jnp.arange(devices)) % devices
    return jnp.stack([lax.dynamic_index_in_dim(stacked, order[i], 0, keepdims=False) for i in range(devices)])


def in_tiles(rows, devices):
    return jnp.moveaxis(rows.reshape(rows.shape[0], devices, -1), 1, 0)


def from_tiles(tiles):
    return jnp.moveaxis(tiles, 0, 1).reshape(tiles.shape[1], -1)


def image_parts(rows):
    count = rows.shape[0]
    quarter = -(-count // 64) * 16
    tiles = jnp.pad(rows, ((0, 4 * quarter - count), (0, 0))).reshape(4, quarter, -1)
    return tiles


LOW_PAIRS = [(0, 1), (1, 0), (2, 3), (3, 2)]
HIGH_PAIRS = [(0, 2), (2, 0), (1, 3), (3, 1)]


def pick(pair, at):
    return jnp.where(at == 0, pair[0], pair[1])


def plus(a, b):
    return (a.astype(F32) + b.astype(F32)).astype(BF)


def image_places():
    place = lax.axis_index("img")
    return place // 2, place % 2


def image_first(rows):
    high, low = image_places()
    tiles = image_parts(rows)
    one, two = tiles[:2], tiles[2:]
    got_one = lax.ppermute(pick(one, 1 - low), "img", LOW_PAIRS)
    got_two = lax.ppermute(pick(two, 1 - high), "img", HIGH_PAIRS)
    return plus(pick(one, low), got_one), plus(pick(two, high), got_two)


def image_second(one, two):
    got_one = lax.ppermute(one, "img", HIGH_PAIRS)
    got_two = lax.ppermute(two, "img", LOW_PAIRS)
    return plus(one, got_one), plus(two, got_two)


def image_third(one, two):
    return lax.ppermute(one, "img", LOW_PAIRS), lax.ppermute(two, "img", HIGH_PAIRS)


def image_whole(one, two, got_one, got_two, count):
    high, low = image_places()
    whole = jnp.concatenate(
        [
            jnp.where(low == 0, one, got_one),
            jnp.where(low == 0, got_one, one),
            jnp.where(high == 0, two, got_two),
            jnp.where(high == 0, got_two, two),
        ]
    )
    return whole[:count]


def image_sum(rows):
    one, two = image_second(*image_first(rows))
    return image_whole(one, two, *image_third(one, two), rows.shape[0])


def on_device_slow(
    latents,
    pixels,
    keep_mask,
    cotangent,
    w_query,
    w_key,
    w_value,
    kv_bias,
    w_out,
    w_first,
    w_second,
    w_qkv,
    w_self_out,
    w_third,
    w_fourth,
    norm_gains,
    norm_shifts,
    proj_biases,
    pix_gain,
    pix_shift,
):
    width = latents.shape[-1]
    rows = latents.shape[1]
    channels = pixels.shape[-1]
    padded = -(-(channels + 8) // 16) * 16
    cross_scale = width ** (-0.5)
    chips = lax.axis_size("chip")
    chip = lax.axis_index("chip")
    core = lax.axis_index("core")
    piece = width // (chips * 2)

    def columns(values):
        span = values.shape[-1] // chips
        return lax.dynamic_slice_in_dim(values, chip * span, span, values.ndim - 1)

    def mine(values):
        return lax.dynamic_index_in_dim(values, core, 0, keepdims=False)

    def other(values):
        return lax.dynamic_index_in_dim(values, 1 - core, 0, keepdims=False)

    def swapped(values):
        return lax.ppermute(values, "core", SWAP)

    gains = norm_gains.astype(F32)
    shifts = norm_shifts.astype(F32)
    biases = proj_biases.astype(F32)
    pixel_gain = pix_gain.astype(F32)
    pixel_shift = pix_shift.astype(F32)
    key_rows = jnp.pad(w_key, ((0, padded - channels), (0, 0)))
    value_rows = jnp.concatenate(
        [w_value, kv_bias[None], jnp.zeros((padded - channels - 1, width), BF)]
    )

    q_normed, _, _ = layer_norm(latents.astype(F32), gains[0], shifts[0])
    q_normed_low = q_normed.astype(BF)
    query = (
        (dot(q_normed_low.reshape(-1, width), w_query, 1, 0) + biases[0]) * cross_scale
    ).astype(BF)
    query_pix = jnp.stack(
        [dot(key_rows, query[:rows], 1, 1), dot(key_rows, query[rows:], 1, 1)]
    ).astype(BF)
    p_normed, p_unit, p_inverse = layer_norm(pixels.astype(F32), pixel_gain, pixel_shift)
    lane = jnp.arange(padded)
    ones_lanes = ((lane == channels) | (lane == channels + 1)).astype(BF)
    pix_low = jnp.pad(p_normed.astype(BF), ((0, 0), (0, 0), (0, padded - channels))) + ones_lanes
    kept_pixels = keep_mask[:, :, None] > 0
    scores = jnp.einsum("bpc,bci->bpi", pix_low, query_pix, preferred_element_type=F32)
    local_top = jnp.max(jnp.where(kept_pixels, scores, FLOOR_VALUE), axis=1)
    level = jnp.floor(local_top / LOG_TWO)
    first_weights = jnp.where(
        kept_pixels, jnp.exp(scores - (level * LOG_TWO)[:, None, :]), 0.0
    ).astype(BF)
    local_numer = jnp.einsum("bpc,bpi->bci", pix_low, first_weights, preferred_element_type=F32)

    def packed(body, extras):
        lead = jnp.concatenate([body] + [e[None, :] for e in extras]).astype(BF)
        return jnp.pad(lead, ((0, padded - lead.shape[0]), (0, 0)))

    def fwd_pack(numer, level):
        total = numer[channels]
        return packed(numer[:channels], three_parts(total)[:2] + three_parts(level))

    def fwd_unpack(pack):
        pack = pack.astype(F32)
        total = pack[channels] + pack[channels + 1]
        level = pack[channels + 2] + pack[channels + 3] + pack[channels + 4]
        return (jnp.concatenate([pack[:channels], total[None]]), level)

    def joined(parts):
        top = parts[0][1]
        for _, level in parts[1:]:
            top = jnp.maximum(top, level)
        return (sum(body * jnp.exp2(level - top)[None, :] for body, level in parts), top)

    sent = swapped(fwd_pack(other(local_numer), other(level)))
    body, top = joined([(mine(local_numer)[: channels + 1], mine(level)), fwd_unpack(sent)])
    got = exchange(in_tiles(fwd_pack(body, top), chips), "chip")
    body, top = joined([fwd_unpack(got[i]) for i in range(chips)])
    mean_tile = packed(
        body[:channels] / body[channels], three_parts(body[channels]) + three_parts(top)
    )
    mean_all = from_tiles(gather(mean_tile, "chip")).astype(F32)
    cross_total = mean_all[channels] + mean_all[channels + 1] + mean_all[channels + 2]
    cross_level = mean_all[channels + 3] + mean_all[channels + 4] + mean_all[channels + 5]
    row = jnp.arange(padded)[:, None]
    mean_pix = jnp.where(row < channels, mean_all, jnp.where(row == channels, 1.0, 0.0))
    mean_low = mean_pix.astype(BF)

    _, q_unit, q_inverse = layer_norm(mine(latents).astype(F32), gains[0], shifts[0])
    fast = piece % 128 == 0
    if fast:
        span, qkv_span = 2 * piece, 6 * piece
        starts = (chip * span, chip * qkv_span)
        flip = core
    else:
        span, qkv_span = 256, 256
        starts = tuple(
            jnp.minimum(chip * size // chips // 128 * 128, size - 256) for size in (width, 3 * width)
        )
        flip = 0 * core
    place = jnp.stack([starts[0], starts[1], flip]).astype(jnp.int32)
    stats = jnp.concatenate(
        [
            (1.0 / cross_total)[None],
            mean_all[channels + 3 : channels + 6],
            jnp.zeros((4, rows), F32),
        ]
    )
    output, d_after, own_pack, small_grads, keep, send = trunk_slow(
        place,
        mine(latents),
        mean_low,
        stats,
        mine(cotangent),
        norm_gains,
        norm_shifts,
        proj_biases,
        [value_rows, w_out, w_first, w_second, w_qkv, w_self_out, w_third, w_fourth],
        channels,
        span,
        qkv_span,
    )
    def flat(arrays):
        return jnp.concatenate(
            [a.reshape(a.shape[0], -1, piece).swapaxes(0, 1).reshape(-1, piece) for a in arrays]
        ).astype(BF)

    def split(grads):
        keep, send = [], []
        for g in grads:
            half = g.shape[-1] // 2
            keep.append(lax.dynamic_slice_in_dim(g, core * half, half, 1))
            send.append(lax.dynamic_slice_in_dim(g, (1 - core) * half, half, 1))
        return flat(keep), flat(send)

    squares = [(width, piece)] * 3
    spans = squares + [(width, 3 * piece)] + squares + [(padded, piece)]
    if not fast:
        blocks, at = [], 0
        for r, c in spans:
            size = c * chips * 2
            block = jnp.concatenate([keep[at : at + r], send[at : at + r]], axis=1)
            offset = chip * 2 * c - (starts[1] if size > width else starts[0])
            blocks.append(lax.dynamic_slice_in_dim(block, offset, 2 * c, 1))
            at += r
        keep, send = split(blocks)
    got_pack, got_send = lax.optimization_barrier((swapped(own_pack), swapped(send)))
    both_cores = plus(keep, got_send)
    got_pack, both_cores = lax.optimization_barrier((got_pack, both_cores))
    one, two = image_first(both_cores)
    both = jnp.where(core == 0, jnp.stack([own_pack, got_pack]), jnp.stack([got_pack, own_pack]))

    levels = jnp.sum(both[:, channels + 2 : channels + 5].astype(F32), axis=1)
    weights = jnp.where(kept_pixels, jnp.exp(scores - (levels * LOG_TWO)[:, None, :]), 0.0)
    grad_rows = jnp.where(row[None] < channels + 2, both, jnp.zeros((), BF))
    d_weights = jnp.einsum("bpc,bci->bpi", pix_low, grad_rows, preferred_element_type=F32)
    score_grad = (d_weights * weights).astype(BF)
    query_part = jnp.einsum("bpc,bpi->bci", pix_low, score_grad, preferred_element_type=F32)
    d_pix_normed = jnp.einsum(
        "bpi,bci->bpc", score_grad, query_pix, preferred_element_type=F32
    ) + jnp.einsum("bpi,bci->bpc", weights.astype(BF), grad_rows, preferred_element_type=F32)
    d_pix_normed = d_pix_normed[..., :channels]
    scaled = d_pix_normed * pixel_gain
    d_pixels = p_inverse * (
        scaled
        - jnp.mean(scaled, axis=-1, keepdims=True)
        - p_unit * jnp.mean(scaled * p_unit, axis=-1, keepdims=True)
    )
    pix_sums = jnp.stack(
        [jnp.sum(d_pix_normed * p_unit, axis=1), jnp.sum(d_pix_normed, axis=1)], axis=1
    )
    pix_sums = jnp.pad(pix_sums, ((0, 0), (0, 0), (0, rows - channels)))

    def bwd_pack(body, sums):
        high, low, _ = three_parts(sums)
        return packed(body[:channels], [high[0], low[0], high[1], low[1]])

    def bwd_unpack(pack):
        pack = pack.astype(F32)
        sums = jnp.stack(
            [pack[channels] + pack[channels + 1], pack[channels + 2] + pack[channels + 3]]
        )
        return (pack[:channels], sums)

    query_part, pix_sums, one, two = lax.optimization_barrier((query_part, pix_sums, one, two))
    one, two = image_second(one, two)
    sent = swapped(bwd_pack(other(query_part), other(pix_sums)))
    body_two, sums_two = bwd_unpack(sent)
    body, sums = (mine(query_part)[:channels] + body_two, mine(pix_sums) + sums_two)
    got = exchange(in_tiles(bwd_pack(body, sums), chips), "chip")
    got = [bwd_unpack(got[i]) for i in range(chips)]
    body, sums = (sum(g[0] for g in got), sum(g[1] for g in got))
    body, sums, one, two = lax.optimization_barrier((body, sums, one, two))
    got_one, got_two = image_third(one, two)
    all_parts = from_tiles(gather(bwd_pack(body, sums), "chip"))
    _, sums = bwd_unpack(all_parts)
    query_sum = jnp.where(row < channels, all_parts, jnp.zeros((), BF))

    d_query = dot(query_sum, key_rows, 0, 0) * cross_scale
    d_query_low = d_query.astype(BF)
    own_normed = mine(q_normed_low)
    own_query = lax.dynamic_slice_in_dim(query, core * rows, rows, 0)
    d_w_query = dot(own_normed, columns(d_query_low), 0, 0)
    d_w_key = dot(query_sum, columns(own_query), 1, 0)
    d_q_normed = dot(d_query_low, w_query, 1, 1)
    d_q_in, d_gain_zero, d_shift_zero = norm_back(d_q_normed, q_unit, q_inverse, gains[0])
    d_latents_own = d_after + d_q_in

    def two_images(own):
        got = swapped(own.astype(BF)).astype(own.dtype)
        return jnp.where(core == 0, jnp.stack([own, got]), jnp.stack([got, own]))

    def unpacked(whole, spans):
        outs, at = [], 0
        for r, c in spans:
            count = r * (c // piece)
            part = whole[at : at + count].reshape(c // piece, r, piece).swapaxes(0, 1).reshape(r, c)
            outs.append(part.astype(F32))
            at += count
        return outs

    def reduced(keep, send, spans):
        return unpacked(image_sum(plus(keep, swapped(send))), spans)

    small = jnp.concatenate(
        [
            d_gain_zero[None],
            small_grads[0:3],
            d_shift_zero[None],
            small_grads[3:6],
            row_total(d_query)[None],
            small_grads[6:14],
        ]
    )
    sum_lanes = -(-channels // piece) * piece
    pix_rows = sums[:, :sum_lanes].reshape(-1, piece)
    pix_rows = jnp.concatenate([pix_rows, pix_rows], axis=1)
    last_spans = [(width, piece), (padded, piece), (small.shape[0], piece), (pix_rows.shape[0], piece)]
    keep, send = split([d_w_query, d_w_key, columns(small), pix_rows])
    keep, send, got_one, got_two = lax.optimization_barrier((keep, send, got_one, got_two))
    last = reduced(keep, send, last_spans)
    main = unpacked(image_whole(one, two, got_one, got_two, both_cores.shape[0]), spans)
    d_small = last[2]
    pix_out = last[3].reshape(2, sum_lanes)
    return (
        two_images(output.astype(BF)),
        two_images(d_latents_own),
        d_pixels,
        last[0],
        last[1][:channels],
        main[7][:channels],
        main[7][channels],
        main[6],
        main[5],
        main[4],
        main[3],
        main[2],
        main[1],
        main[0],
        d_small[0:4],
        d_small[4:8],
        d_small[8:17],
        pix_out[0, :channels],
        pix_out[1, :channels],
    )


LOWEST_LEVEL = -16777216.0


def row_of(value):
    return lax.broadcasted_iota(jnp.int32, value.shape, 0)


def with_rows(body, first, extras):
    row = row_of(body)
    for at, extra in enumerate(extras):
        body = jnp.where(row == first + at, extra, body)
    return body


def pack_sum(body, channels, level):
    total = body[channels : channels + 1]
    extras = three_parts(total)[:2] + three_parts(level)
    return with_rows(body, channels, extras).astype(BF)


def unpack_sum(pack, channels):
    pack = pack.astype(F32)
    total = pack[channels : channels + 1] + pack[channels + 1 : channels + 2]
    level = (
        pack[channels + 2 : channels + 3]
        + pack[channels + 3 : channels + 4]
        + pack[channels + 4 : channels + 5]
    )
    return with_rows(pack, channels, [total]), level


def join_sums(parts):
    top = parts[0][1]
    for _, level in parts[1:]:
        top = jnp.maximum(top, level)
    body = None
    for part, level in parts:
        scaled = part * jnp.exp2(level - top)
        body = scaled if body is None else body + scaled
    return body, top


def fill_rows(dst, src, tail, extra=None):
    count = src.shape[0]
    base = count // 16 * 16
    dst[:base, :] = src[:base, :]
    tail[...] = jnp.zeros_like(tail)
    tail[: count - base, :] = src[base:count, :].astype(F32)
    if extra is not None:
        tail[count - base : count - base + 1, :] = extra
    dst[base : base + 16, :] = tail[...].astype(BF)


def pixel_units(pix, image, xs, channels):
    xs[:channels, :] = pix[image].astype(F32)
    x = xs[...]
    inside = row_of(x) < channels
    mean = jnp.sum(x, axis=0, keepdims=True) * (1.0 / channels)
    c = jnp.where(inside, x - mean, 0.0)
    iv = lax.rsqrt(jnp.sum(c * c, axis=0, keepdims=True) * (1.0 / channels) + EPSILON)
    return c * iv, iv, inside


def look_body(
    channels,
    place,
    lat,
    pix,
    mask,
    par,
    gains,
    shifts,
    biases,
    wk_in,
    wq_h,
    keep,
    send,
    qp_out,
    q_out,
    pn_out,
    wq,
    normed,
    qs,
    wk,
    xs,
    tail,
    sem,
):
    images, rows, width = lat.shape
    core = place[1]
    copy = pltpu.make_async_copy(wq_h, wq, sem)
    copy.start()
    g, s = gains[0:1, :].astype(F32), shifts[0:1, :].astype(F32)

    def norm_step(image, carry):
        v = lat[image].astype(F32)
        c = v - jnp.mean(v, axis=1, keepdims=True)
        iv = lax.rsqrt(jnp.mean(c * c, axis=1, keepdims=True) + EPSILON)
        normed[image] = (c * iv * g + s).astype(BF)
        return carry

    lax.fori_loop(0, images, norm_step, 0)
    fill_rows(wk, wk_in, tail)
    xs[...] = jnp.zeros_like(xs)
    copy.wait()
    bias = biases[0:1, :].astype(F32)

    def per_image(image, carry):
        qs[image] = ((dot(normed[image], wq[...], 1, 0) + bias) * width ** (-0.5)).astype(BF)
        scored = dot(wk[...], qs[image], 1, 1)
        qp_out[image] = with_rows(scored, channels + 2, [jnp.ones((1, rows), F32)]).astype(BF)
        unit, _, _ = pixel_units(pix, image, xs, channels)
        n = unit * par[:, 0:1] + par[:, 1:2]
        off = jnp.where(mask[pl.ds(image, 1), :] > 0, 0.0, FLOOR_VALUE)
        one = jnp.ones_like(off)
        pn_out[image] = with_rows(n, channels, [one, one, off]).astype(BF)
        scores = dot(pn_out[image], qp_out[image], 0, 0)
        top = jnp.max(scores, axis=0, keepdims=True)
        level = jnp.maximum(jnp.floor(top / LOG_TWO), LOWEST_LEVEL)
        weights = jnp.exp(scores - level * LOG_TWO).astype(BF)
        body = dot(pn_out[image], weights, 1, 0)

        @pl.when(core == image)
        def _():
            keep[...] = with_rows(body, channels + 1, [level])

        @pl.when(core != image)
        def _():
            send[...] = pack_sum(body, channels, level)

        return carry

    lax.fori_loop(0, images, per_image, 0)
    q_out[...] = qs[core]


def tiles_out(place, whole, outs):
    chips = len(outs)
    lanes = outs[0].shape[1]
    for step in range(chips):
        at = lax.rem(place[0] + step, chips)
        outs[step][...] = whole[:, pl.ds(pl.multiple_of(at * lanes, lanes), lanes)]


def tiles_in(place, whole, tiles):
    chips = len(tiles)
    lanes = tiles[0].shape[1]
    for step in range(chips):
        at = lax.rem(place[0] + chips - step, chips)
        whole[:, pl.ds(pl.multiple_of(at * lanes, lanes), lanes)] = tiles[step][...]


def join_one_body(channels, place, keep, got, *refs):
    outs, whole = refs[:-1], refs[-1]
    own = keep[...]
    body, top = join_sums(
        [(own, own[channels + 1 : channels + 2]), unpack_sum(got[...], channels)]
    )
    whole[...] = pack_sum(body, channels, top)
    tiles_out(place, whole, outs)


def join_two_body(channels, *refs):
    tiles, out = refs[:-1], refs[-1]
    body, top = join_sums([unpack_sum(t[...], channels) for t in tiles])
    total = body[channels : channels + 1]
    extras = (jnp.ones_like(total),) + three_parts(total) + three_parts(top)
    out[...] = with_rows(body / total, channels, extras).astype(BF)


def back_one_body(
    channels, place, own, got, qp_in, pn, keep, send, both, score_grad, weights_low, pair
):
    images, padded, rows = qp_in.shape
    core = place[1]
    pair[core] = own[...]
    pair[1 - core] = got[...]

    def per_image(image, carry):
        pack = pair[image].astype(F32)
        level = (
            pack[channels + 2 : channels + 3]
            + pack[channels + 3 : channels + 4]
            + pack[channels + 4 : channels + 5]
        )
        grads = jnp.where(row_of(pack) < channels + 2, pack, 0.0).astype(BF)
        both[image] = grads
        scores = dot(pn[image], qp_in[image], 0, 0)
        weights = jnp.exp(scores - level * LOG_TWO)
        weights_low[image] = weights.astype(BF)
        score_grad[image] = (dot(pn[image], grads, 0, 0) * weights).astype(BF)
        body = dot(pn[image], score_grad[image], 1, 0)

        @pl.when(core == image)
        def _():
            keep[...] = body

        @pl.when(core != image)
        def _():
            send[...] = body.astype(BF)

        return carry

    lax.fori_loop(0, images, per_image, 0)


def back_join_one_body(place, keep, got, *refs):
    outs, whole = refs[:-1], refs[-1]
    whole[...] = (keep[...] + got[...].astype(F32)).astype(BF)
    tiles_out(place, whole, outs)


def back_two_body(
    channels, place, score_grad, weights_low, qp, both, pix, par, out_own, out_got,
    d_pix, sums, out_both, xs, turn
):
    images = pix.shape[0]
    padded = qp.shape[1]
    core = place[1]
    out_both[core] = out_own[...]
    out_both[1 - core] = out_got[...]
    xs[...] = jnp.zeros_like(xs)

    def per_image(image, carry):
        dn = dot(qp[image], score_grad[image], 1, 1) + dot(both[image], weights_low[image], 1, 1)
        unit, iv, inside = pixel_units(pix, image, xs, channels)
        grad = jnp.where(inside, dn, 0.0)
        scaled = grad * par[:, 0:1]
        one = jnp.sum(scaled, axis=0, keepdims=True) * (1.0 / channels)
        two = jnp.sum(scaled * unit, axis=0, keepdims=True) * (1.0 / channels)
        d_pix[image] = (iv * (scaled - one - unit * two))[:channels]
        d_gain = jnp.sum(grad * unit, axis=1, keepdims=True)
        d_shift = jnp.sum(grad, axis=1, keepdims=True)
        return carry[0] + d_gain, carry[1] + d_shift

    zero = jnp.zeros((padded, 1), F32)
    d_gain, d_shift = lax.fori_loop(0, images, per_image, (zero, zero))
    turn[...] = jnp.zeros_like(turn)
    lane = lax.broadcasted_iota(jnp.int32, (padded, 128), 1)
    turn[:padded, :] = jnp.where(lane == 0, d_gain, jnp.where(lane == 1, d_shift, 0.0))
    sums[...] = turn[...].T[:8]


def back_join_two_body(channels, *refs):
    tiles, sums, out = refs[:-2], refs[-2], refs[-1]
    body = tiles[0][...].astype(F32)
    for t in tiles[1:]:
        body = body + t[...].astype(F32)
    lanes = out.shape[1]
    count = sums.shape[1] // lanes
    extras = [sums[r : r + 1, j * lanes : (j + 1) * lanes] for r in range(2) for j in range(count)]
    out[...] = with_rows(body, channels, extras).astype(BF)


def tail_body(channels, place, *refs):
    chips = len(refs) - 27
    tiles = refs[:chips]
    (
        lat_h,
        wq_h,
        d_after_h,
        query,
        wk_in,
        gains,
        shifts,
        small_in,
        d_lat,
        d_lat_low,
        keep,
        send,
        lat,
        wq,
        d_after,
        part,
        wk,
        tail,
        normed,
        low,
        acc,
        stat,
        sums,
        small,
        lat_sem,
        wq_sem,
        after_sem,
    ) = refs[chips:]
    rows, width = query.shape
    padded = part.shape[0]
    chip, core = place[0], place[1]
    copies = [
        pltpu.make_async_copy(lat_h.at[core], lat, lat_sem),
        pltpu.make_async_copy(wq_h, wq, wq_sem),
        pltpu.make_async_copy(d_after_h, d_after, after_sem),
    ]
    for copy in copies:
        copy.start()
    tiles_in(place, part, tiles)
    base = channels // 16 * 16
    tail[:, :rows] = part[base : base + 16, :].astype(F32)
    extra_rows = tail[channels - base : channels - base + 6, :rows]
    lanes = tiles[0].shape[1]
    pix_rows = extra_rows[:, :lanes]
    for at in range(1, chips):
        pix_rows = pix_rows + extra_rows[:, at * lanes : (at + 1) * lanes]
    part_value = part[...]
    clean = jnp.where(row_of(part_value) < channels, part_value.astype(F32), 0.0).astype(BF)
    part[...] = clean
    fill_rows(wk, wk_in, tail)
    d_query = dot(part[...], wk[...], 0, 0) * width ** (-0.5)
    low[...] = d_query.astype(BF)
    bias_row = jnp.sum(jnp.sum(d_query.reshape(-1, 8, width), axis=0), axis=0, keepdims=True)
    copies[0].wait()
    g, s = gains[0:1, :].astype(F32), shifts[0:1, :].astype(F32)

    def norm_step(i, carry):
        at = pl.ds(pl.multiple_of(i * 128, 128), 128)
        v = lat[at, :].astype(F32)
        m = jnp.mean(v, axis=1, keepdims=True)
        c = v - m
        iv = lax.rsqrt(jnp.mean(c * c, axis=1, keepdims=True) + EPSILON)
        normed[at, :] = (c * iv * g + s).astype(BF)
        stat[0, at, :] = jnp.broadcast_to(m, (128, 128))
        stat[1, at, :] = jnp.broadcast_to(iv, (128, 128))
        return carry

    lax.fori_loop(0, rows // 128, norm_step, 0)

    def put(first, value):
        count = value.shape[0]

        @pl.when(core == 0)
        def _():
            keep[first : first + count, :] = value[:, :128]
            send[first : first + count, :] = value[:, 128:]

        @pl.when(core != 0)
        def _():
            send[first : first + count, :] = value[:, :128]
            keep[first : first + count, :] = value[:, 128:]

    cols = pl.ds(pl.multiple_of(chip * 256, 256), 256)
    put(0, dot(normed[...], low[:, cols], 0, 0).astype(BF))
    put(width, dot(part[...], query[:, cols], 1, 0).astype(BF))
    copies[1].wait()
    acc[...] = dot(low[...], wq[...], 1, 1)
    copies[2].wait()
    sums[...] = jnp.zeros_like(sums)

    def back_step(i, carry):
        at = pl.ds(pl.multiple_of(i * 128, 128), 128)
        m, iv = stat[0, at, 0:1], stat[1, at, 0:1]
        unit = (lat[at, :].astype(F32) - m) * iv
        grad = acc[at, :]
        scaled = grad * g
        one = jnp.mean(scaled, axis=1, keepdims=True)
        two = jnp.mean(scaled * unit, axis=1, keepdims=True)
        total = d_after[at, :] + iv * (scaled - one - unit * two)
        d_lat[at, :] = total
        d_lat_low[at, :] = total.astype(BF)
        sums[0] += jnp.sum((grad * unit).reshape(-1, 8, width), axis=0)
        sums[1] += jnp.sum(grad.reshape(-1, 8, width), axis=0)
        return carry

    lax.fori_loop(0, rows // 128, back_step, 0)
    small[...] = jnp.zeros_like(small)
    small[0:1, :] = jnp.sum(sums[0], axis=0, keepdims=True)
    small[1:4, :] = small_in[0:3, :]
    small[4:5, :] = jnp.sum(sums[1], axis=0, keepdims=True)
    small[5:8, :] = small_in[3:6, :]
    small[8:9, :] = bias_row
    small[9:17, :] = small_in[6:14, :]
    put(width + padded, small[:, cols].astype(BF))
    tail[...] = jnp.zeros_like(tail)
    tail[0:6, :lanes] = pix_rows
    spread = tail[:, :128].astype(BF)
    first = width + padded + small.shape[0]
    keep[first : first + 16, :] = spread
    send[first : first + 16, :] = spread


def unpack_body(pieces, place, *refs):
    unpack_core(pieces, place, refs[:4], refs[4:-3], *refs[-3:])


def unpack_more_body(pieces, place, *refs):
    lat_own, lat_got = refs[4:6]
    wide, lat_both, sems = refs[-5], refs[6], refs[-4]
    core = place[1]
    first = pltpu.make_async_copy(lat_own, lat_both.at[core], sems.at[0])
    first.start()
    wide[...] = lat_got[...].astype(F32)
    second = pltpu.make_async_copy(wide, lat_both.at[1 - core], sems.at[1])
    second.start()
    unpack_core(pieces, place, refs[:4], refs[7:-5], *refs[-3:])
    first.wait()
    second.wait()


def unpack_core(pieces, place, parts, outs, whole, some, sems):
    quarter = parts[0].shape[0]
    img = place[2]
    high, low = lax.div(img, 2), lax.rem(img, 2)
    spots = [low, 2 + high, 1 - low, 3 - high]
    copies = []
    for at, spot in enumerate(spots):
        target = whole.at[pl.ds(pl.multiple_of(spot * quarter, 16), quarter), :]
        copy = pltpu.make_async_copy(parts[at], target, sems.at[at])
        copy.start()
        copies.append(copy)
    for copy in copies:
        copy.wait()
    for out, (first, count, across) in zip(outs, pieces):
        for j in range(across):
            at = first + j * count
            rows = out.shape[0]
            if rows > 16:
                out[:, j * 128 : (j + 1) * 128] = whole[at : at + rows, :].astype(F32)
            else:
                base = min(at // 16 * 16, whole.shape[0] - 32)
                some[...] = whole[base : base + 32, :].astype(F32)
                out[:, j * 128 : (j + 1) * 128] = some[at - base : at - base + rows, :]


def call(body, outs, scratch, args, spaces, name, flops, out_spaces=None, vmem=48):
    where = {
        "v": pl.BlockSpec(memory_space=pltpu.VMEM),
        "a": pl.BlockSpec(memory_space=pl.ANY),
        "s": pl.BlockSpec(memory_space=pltpu.SMEM),
    }
    return pl.pallas_call(
        body,
        out_shape=[jax.ShapeDtypeStruct(*o) for o in outs],
        in_specs=[where[s] for s in spaces],
        out_specs=[where[s] for s in (out_spaces or "v" * len(outs))],
        scratch_shapes=scratch,
        compiler_params=pltpu.CompilerParams(vmem_limit_bytes=vmem << 20),
        cost_estimate=pl.CostEstimate(flops=flops, transcendentals=0, bytes_accessed=8 << 20),
        name=name,
    )(*args)


def on_device_fast(
    latents,
    pixels,
    keep_mask,
    cotangent,
    w_query,
    w_key,
    w_value,
    kv_bias,
    w_out,
    w_first,
    w_second,
    w_qkv,
    w_self_out,
    w_third,
    w_fourth,
    norm_gains,
    norm_shifts,
    proj_biases,
    pix_gain,
    pix_shift,
):
    images, rows, width = latents.shape
    _, pix, channels = pixels.shape
    padded = -(-(channels + 8) // 16) * 16
    wide = -(-(channels + 8) // 128) * 128
    chips = lax.axis_size("chip")
    lanes = rows // chips
    vm = pltpu.VMEM
    dma = pltpu.SemaphoreType.DMA
    place = jnp.stack(
        [lax.axis_index("chip"), lax.axis_index("core"), lax.axis_index("img")]
    ).astype(jnp.int32)
    par = jnp.pad(
        jnp.stack([pix_gain, pix_shift], axis=1).astype(F32), ((0, padded - channels), (0, 0))
    )
    pix_rows = jnp.transpose(pixels, (0, 2, 1))
    unit = 2 * rows * width * width
    cross = 2 * rows * pix * wide * images

    def swapped(values):
        return lax.ppermute(values, "core", SWAP)

    def around(tiles):
        return [
            lax.ppermute(t, "chip", shifted(chips, step + 1)) for step, t in enumerate(tiles)
        ]

    keep, send, query_pix, query, pix_normed = call(
        functools.partial(look_body, channels),
        [
            ((padded, rows), F32),
            ((padded, rows), BF),
            ((images, padded, rows), BF),
            ((rows, width), BF),
            ((images, padded, pix), BF),
        ],
        [
            vm((width, width), BF),
            vm((images, rows, width), BF),
            vm((images, rows, width), BF),
            vm((padded, width), BF),
            vm((padded, pix), F32),
            vm((16, width), F32),
            dma,
        ],
        (
            place,
            latents,
            pix_rows,
            keep_mask,
            par,
            norm_gains,
            norm_shifts,
            proj_biases,
            w_key,
            w_query,
        ),
        "svvvvvvvva",
        "look",
        3 * unit + 2 * cross,
    )
    tiles = call(
        functools.partial(join_one_body, channels),
        [((padded, lanes), BF)] * chips,
        [vm((padded, rows), BF)],
        (place, keep, swapped(send)),
        "svv",
        "join_one",
        1,
    )
    (tile,) = call(
        functools.partial(join_two_body, channels),
        [((padded, lanes), BF)],
        [],
        (tiles[0], *around(tiles[1:])),
        "v" * chips,
        "join_two",
        1,
    )
    tiles = [tile] + around([tile] * (chips - 1))
    output, d_after, own_pack, small_grads, keep, send = trunk(
        place,
        tiles,
        latents,
        cotangent,
        norm_gains,
        norm_shifts,
        proj_biases,
        w_value,
        kv_bias[None],
        [w_out, w_first, w_second, w_qkv, w_self_out, w_third, w_fourth],
        channels,
        padded,
    )
    got_pack, send, output = lax.optimization_barrier((swapped(own_pack), send, output))
    got_send, got_output = swapped(send), swapped(output)
    both_keep = keep
    keep, send, both, score_grad, weights_low = call(
        functools.partial(back_one_body, channels),
        [
            ((padded, rows), F32),
            ((padded, rows), BF),
            ((images, padded, rows), BF),
            ((images, pix, rows), BF),
            ((images, pix, rows), BF),
        ],
        [vm((images, padded, rows), BF)],
        (place, own_pack, got_pack, query_pix, pix_normed),
        "svvvv",
        "back_one",
        3 * cross,
    )
    keep, send, got_send = lax.optimization_barrier((keep, send, got_send))
    both_cores = plus(both_keep, got_send)
    tiles = call(
        back_join_one_body,
        [((padded, lanes), BF)] * chips,
        [vm((padded, rows), BF)],
        (place, keep, swapped(send)),
        "svv",
        "back_join_one",
        1,
    )
    tiles, score_grad, both_cores = lax.optimization_barrier((tiles, score_grad, both_cores))
    one, two = image_first(both_cores)
    d_pixels, sums, both_outputs = call(
        functools.partial(back_two_body, channels),
        [((images, channels, pix), F32), ((8, wide), F32), ((images, rows, width), BF)],
        [vm((padded, pix), F32), vm((wide, 128), F32)],
        (place, score_grad, weights_low, query_pix, both, pix_rows, par, output, got_output),
        "svvvvvvvv",
        "back_two",
        2 * cross,
    )
    (tile,) = call(
        functools.partial(back_join_two_body, channels),
        [((padded, lanes), BF)],
        [],
        (tiles[0], *around(tiles[1:]), sums),
        "v" * (chips + 1),
        "back_join_two",
        1,
    )
    tile, one, two = lax.optimization_barrier((tile, one, two))
    one, two = image_second(one, two)
    tiles = [tile] + around([tile] * (chips - 1))
    last_rows = width + padded + 32 + 16
    d_lat, d_lat_low, keep, send = call(
        functools.partial(tail_body, channels),
        [
            ((rows, width), F32),
            ((rows, width), BF),
            ((last_rows, 128), BF),
            ((last_rows, 128), BF),
        ],
        [
            vm((rows, width), BF),
            vm((width, width), BF),
            vm((rows, width), F32),
            vm((padded, rows), BF),
            vm((padded, width), BF),
            vm((16, width), F32),
            vm((rows, width), BF),
            vm((rows, width), BF),
            vm((rows, width), F32),
            vm((2, rows, 128), F32),
            vm((2, 8, width), F32),
            vm((32, width), F32),
            dma,
            dma,
            dma,
        ],
        (
            place,
            *tiles,
            latents,
            w_query,
            d_after,
            query,
            w_key,
            norm_gains,
            norm_shifts,
            small_grads,
        ),
        "s" + "v" * chips + "aaavvvvv",
        "tail",
        3 * unit,
    )
    keep, send, d_lat_low, one, two = lax.optimization_barrier((keep, send, d_lat_low, one, two))
    got_one, got_two = image_third(one, two)
    last = plus(keep, swapped(send))
    last_one, last_two = image_second(*image_first(last))
    last_gots = image_third(last_one, last_two)

    def unpacked(parts, shapes, pieces, name, latent=None):
        scratch = [vm((4 * parts[0].shape[0], 128), BF), vm((32, 128), F32), dma((4,))]
        outs = [(shape, F32) for shape in shapes]
        body, more, spaces = unpack_body, (), ""
        out_spaces = "v" * len(outs)
        if latent is not None:
            outs = [((images, rows, width), F32)] + outs
            scratch = [vm((rows, width), F32), dma((2,))] + scratch
            body, more, spaces = unpack_more_body, latent, "av"
            out_spaces = "a" + out_spaces
        return call(
            functools.partial(body, pieces),
            outs,
            scratch,
            (place, *parts, *more),
            "saaaa" + spaces,
            name,
            1,
            out_spaces,
        )

    square = (width, 128)
    first, pieces, shapes = 0, [], []
    for shape, across in [(square, 1)] * 3 + [((width, 384), 3)] + [(square, 1)] * 3:
        pieces.append((first, width, across))
        shapes.append(shape)
        first += width * across
    pieces += [(first, padded, 1), (first + channels, 1, 1)]
    shapes += [(channels, 128), (1, 128)]
    both_latents, *main = unpacked(
        (one, two, got_one, got_two), shapes, pieces, "unpack_main", (d_lat, swapped(d_lat_low))
    )
    at = width + padded
    rest = unpacked(
        (last_one, last_two, *last_gots),
        [square, (channels, 128), (4, 128), (4, 128), (9, 128), (1, 384), (1, 384)],
        [
            (0, width, 1),
            (width, padded, 1),
            (at, 4, 1),
            (at + 4, 4, 1),
            (at + 8, 9, 1),
            (at + 32, 1, 3),
            (at + 35, 1, 3),
        ],
        "unpack_last",
    )
    return (
        both_outputs,
        both_latents,
        jnp.transpose(d_pixels, (0, 2, 1)),
        rest[0],
        rest[1],
        main[7],
        main[8][0],
        main[6],
        main[5],
        main[4],
        main[3],
        main[2],
        main[1],
        main[0],
        rest[2],
        rest[3],
        rest[4],
        rest[5][0, :channels],
        rest[6][0, :channels],
    )


def on_device(*args):
    rows, width = args[0].shape[1:]
    chips = lax.axis_size("chip")
    if (width // chips) % 256 == 0 and width // chips == 256 and (rows // chips) % 128 == 0:
        return on_device_fast(*args)
    return on_device_slow(*args)


def solution(mesh):
    images, pieces = mesh.devices.shape
    split = Mesh(mesh.devices.reshape(images, pieces // 2, 2), ("img", "chip", "core"))
    latent = P("img", None, None)
    weight = P(None, PIX)
    placed = (latent, P("img", PIX, None), P("img", PIX), latent) + (P(),) * 16
    return jax.shard_map(
        on_device,
        mesh=split,
        in_specs=placed,
        out_specs=(latent, latent, P("img", PIX, None), weight, weight, weight, P(PIX))
        + (weight,) * 10
        + (P(), P()),
        check_vma=False,
    )
```

```python
import functools

import jax
import jax.numpy as jnp
from jax import lax
from jax.experimental import pallas as pl
from jax.experimental.pallas import tpu as pltpu
from jax.sharding import Mesh
from jax.sharding import PartitionSpec as P

HEADS = 8
EPSILON = 1e-05
LOG_TWO = 0.6931471805599453
FLOOR_VALUE = -1e30
BF = jnp.bfloat16
F32 = jnp.float32
SWAP = [(0, 1), (1, 0)]
PIX = ("chip", "core")


def dot(a, b, ca, cb):
    return lax.dot_general(a, b, (((ca,), (cb,)), ((), ())), preferred_element_type=F32)


def layer_norm(values, norm_gain, norm_shift):
    centre = values - jnp.mean(values, axis=-1, keepdims=True)
    inverse = lax.rsqrt(jnp.mean(centre * centre, axis=-1, keepdims=True) + EPSILON)
    unit_rows = centre * inverse
    return (unit_rows * norm_gain + norm_shift, unit_rows, inverse)


def row_total(values):
    return jnp.sum(values, axis=tuple(range(values.ndim - 1)))


def norm_back(grad, unit_rows, inverse, norm_gain):
    scaled = grad * norm_gain
    d_values = inverse * (
        scaled
        - jnp.mean(scaled, axis=-1, keepdims=True)
        - unit_rows * jnp.mean(scaled * unit_rows, axis=-1, keepdims=True)
    )
    return (d_values, row_total(grad * unit_rows), row_total(grad))


def gelu_exact(values):
    return jax.nn.gelu(values, approximate=False)


def three_parts(values):
    high = values.astype(BF).astype(F32)
    rest = values - high
    middle = rest.astype(BF).astype(F32)
    return (high, middle, rest - middle)


ROOT_HALF = 0.7071067811865476
ROOT_TWO_PI = 0.3989422804014327


def trunk_core(
    channels,
    span,
    qkv_span,
    chip_start,
    qkv_start,
    flip,
    waits,
    lat,
    mean,
    stats,
    cot,
    gains,
    shifts,
    biases,
    result,
    d_after,
    pack,
    small,
    keep_h,
    send_h,
    wv,
    wo,
    w1,
    w2,
    wq,
    ws,
    w3,
    w4,
    att,
    dg1,
    h1,
    x2,
    qkv,
    wl,
    inv_total,
    sl,
    x3,
    dg4,
    h4,
    acc,
    low,
    low_two,
    normed,
    stat,
    sums,
    stage,
    spare_sem,
    store_sem,
):
    rows, width = lat.shape
    head_dim = width // HEADS
    head_scale = head_dim ** (-0.5)
    x1 = d_after
    def over_rows(step, most=512):
        block = min(most, rows)
        if block == rows:
            step(pl.ds(0, rows))
            return

        def run(i, carry):
            step(pl.ds(pl.multiple_of(i * block, block), block))
            return carry

        lax.fori_loop(0, rows // block, run, 0)

    def vector(ref, i):
        return ref[i : i + 1, :].astype(F32)

    def add_sum(at, value):
        sums[at] += jnp.sum(value.reshape(-1, 8, width), axis=0)

    def clear(*ats):
        for at in ats:
            sums[at] = jnp.zeros((8, width), F32)

    def flush(at, row):
        small[row : row + 1, :] = jnp.sum(sums[at], axis=0, keepdims=True)

    def norm_forward(x, i):
        g, s = vector(gains, i), vector(shifts, i)

        def step(at):
            v = x[at, :]
            m = jnp.mean(v, axis=1, keepdims=True)
            c = v - m
            iv = lax.rsqrt(jnp.mean(c * c, axis=1, keepdims=True) + EPSILON)
            normed[at, :] = (c * iv * g + s).astype(BF)
            stat[i - 1, 0, at, :] = jnp.broadcast_to(m, (m.shape[0], 128))
            stat[i - 1, 1, at, :] = jnp.broadcast_to(iv, (m.shape[0], 128))

        over_rows(step)

    def norm_again(x, i):
        g, s = vector(gains, i), vector(shifts, i)

        def step(at):
            m, iv = stat[i - 1, 0, at, 0:1], stat[i - 1, 1, at, 0:1]
            normed[at, :] = ((x[at, :] - m) * iv * g + s).astype(BF)

        over_rows(step)

    def norm_backward(x, skip, i, gain_row, shift_row, bias_row):
        g = vector(gains, i)
        clear(0, 1, 2)

        def step(at):
            m, iv = stat[i - 1, 0, at, 0:1], stat[i - 1, 1, at, 0:1]
            unit = (x[at, :] - m) * iv
            grad = acc[at, :]
            scaled = grad * g
            mean_one = jnp.mean(scaled, axis=1, keepdims=True)
            mean_two = jnp.mean(scaled * unit, axis=1, keepdims=True)
            total = skip[at, :].astype(F32) + iv * (scaled - mean_one - unit * mean_two)
            add_sum(0, grad * unit)
            add_sum(1, grad)
            add_sum(2, total)
            x[at, :] = total
            low_two[at, :] = total.astype(BF)

        over_rows(step)
        flush(0, gain_row)
        flush(1, shift_row)
        flush(2, bias_row)

    def hidden(bias_row, h, dg):
        b = vector(biases, bias_row)

        def step(at):
            v = acc[at, :] + b
            cdf = 0.5 * (1.0 + lax.erf(v * ROOT_HALF))
            h[at, :] = (v * cdf).astype(BF)
            dg[at, :] = cdf + v * (jnp.exp(-0.5 * v * v) * ROOT_TWO_PI)

        over_rows(step)

    def hidden_back(dg, bias_row):
        clear(0)

        def step(at):
            d = acc[at, :] * dg[at, :]
            add_sum(0, d)
            low[at, :] = d.astype(BF)

        over_rows(step)
        flush(0, bias_row)

    pending = [[], []]
    state = {"slot": 0, "row": 0}

    def emit(x, dy, start, span, ca, beside=None):
        count = x.shape[1 - ca]
        half = span // 2
        for t in range(half // 128):
            slot = state["slot"]
            state["slot"] = 1 - slot
            for waiting in pending[slot]:
                waiting.wait()
            pending[slot] = []
            mine = dy[:, pl.ds(pl.multiple_of(start + flip * half + t * 128, 128), 128)]
            other = dy[:, pl.ds(pl.multiple_of(start + (1 - flip) * half + t * 128, 128), 128)]
            both = jnp.concatenate([mine, other], axis=1)
            stage[slot, :count, :] = dot(x[...], both, ca, 0).astype(BF)
            if beside is not None and t == half // 128 - 1:
                beside()
            target = pl.ds(state["row"] + t * count, count)
            for side, out in enumerate((keep_h, send_h)):
                src = stage.at[slot, pl.ds(0, count), pl.ds(side * 128, 128)]
                copy = pltpu.make_async_copy(src, out.at[target, :], store_sem.at[slot, side])
                copy.start()
                pending[slot].append(copy)
        state["row"] += count * (half // 128)

    waits[0]()
    att[...] = dot(mean[...], wv[...], 0, 0).astype(BF)
    waits[1]()
    acc[...] = dot(att[...], wo[...], 1, 0)
    out_bias = vector(biases, 1)

    def after_cross(at):
        x1[at, :] = lat[at, :].astype(F32) + acc[at, :] + out_bias

    over_rows(after_cross)
    waits[9]()
    norm_forward(x1, 1)
    waits[2]()
    acc[...] = dot(normed[...], w1[...], 1, 0)
    hidden(2, h1, dg1)
    waits[3]()
    x2[...] = x1[...] + dot(h1[...], w2[...], 1, 0) + vector(biases, 3)
    norm_forward(x2, 2)
    waits[4]()
    qkv[:, :width] = (
        (dot(normed[...], wq[:, :width], 1, 0) + vector(biases, 4)) * head_scale
    ).astype(BF)
    qkv[:, width : 2 * width] = dot(normed[...], wq[:, width : 2 * width], 1, 0).astype(BF)
    qkv[:, 2 * width :] = (
        dot(normed[...], wq[:, 2 * width :], 1, 0) + vector(biases, 5)
    ).astype(BF)
    ones = jnp.ones((rows, head_dim), BF)

    def head_at(h, part):
        return pl.ds(pl.multiple_of(h * head_dim + part * width, head_dim), head_dim)

    def head_forward(h, carry):
        scores = dot(qkv[:, head_at(h, 0)], qkv[:, head_at(h, 1)], 1, 1)
        top = jnp.max(scores, axis=1, keepdims=True)
        shift = LOG_TWO * jnp.floor(top / LOG_TWO)
        weights = jnp.exp(scores - shift).astype(BF)
        wl[h] = weights
        value = jnp.concatenate([qkv[:, head_at(h, 2)], ones], axis=1)
        both = dot(weights, value, 1, 0)
        over = 1.0 / both[:, head_dim:]
        inv_total[:, head_at(h, 0)] = over
        sl[:, head_at(h, 0)] = (both[:, :head_dim] * over).astype(BF)
        return carry

    lax.fori_loop(0, HEADS, head_forward, 0, unroll=True)
    waits[5]()
    x3[...] = x2[...] + dot(sl[...], ws[...], 1, 0) + vector(biases, 6)
    norm_forward(x3, 3)
    waits[6]()
    acc[...] = dot(normed[...], w3[...], 1, 0)
    hidden(7, h4, dg4)
    waits[7]()
    low[...] = (x3[...] + dot(h4[...], w4[...], 1, 0) + vector(biases, 8)).astype(BF)
    result_copy = pltpu.make_async_copy(low, result, spare_sem)
    result_copy.start()

    waits[8]()
    clear(0)

    def cot_sum(at):
        add_sum(0, cot[at, :].astype(F32))

    over_rows(cot_sum)
    flush(0, 13)
    acc[...] = dot(cot[...], w4[...], 1, 1)
    result_copy.wait()
    emit(h4, cot, chip_start, span, 0, lambda: hidden_back(dg4, 12))
    acc[...] = dot(low[...], w3[...], 1, 1)
    emit(normed, low, chip_start, span, 0, lambda: norm_backward(x3, cot, 3, 2, 5, 11))
    acc[...] = dot(low_two[...], ws[...], 1, 1)
    clear(0, 1)

    def head_backward(h, carry):
        head = head_at(h, 0)
        query, keys, value = qkv[:, head], qkv[:, head_at(h, 1)], qkv[:, head_at(h, 2)]
        grad = acc[:, head] * inv_total[:, head]
        numer_grad = grad.astype(BF)
        total_part = (-(grad * sl[:, head].astype(F32))).astype(BF)
        weights = wl[h]
        d_weights = dot(
            jnp.concatenate([numer_grad, total_part], axis=1),
            jnp.concatenate([value, ones], axis=1),
            1,
            1,
        )
        score_grad = (d_weights * weights.astype(F32)).astype(BF)
        d_value = dot(weights, numer_grad, 0, 0)
        d_query = dot(score_grad, keys, 1, 0) * head_scale
        d_keys = dot(score_grad, query, 0, 0)
        qkv[:, head] = d_query.astype(BF)
        qkv[:, head_at(h, 1)] = d_keys.astype(BF)
        qkv[:, head_at(h, 2)] = d_value.astype(BF)
        sums[0, :, head] = jnp.sum(d_query.reshape(-1, 8, head_dim), axis=0)
        sums[1, :, head] = jnp.sum(d_value.reshape(-1, 8, head_dim), axis=0)
        return carry

    def heads_backward():
        lax.fori_loop(0, HEADS, head_backward, 0, unroll=True)

    emit(sl, low_two, chip_start, span, 0, heads_backward)
    flush(0, 9)
    flush(1, 10)
    norm_again(x2, 2)
    acc[...] = dot(qkv[...], wq[...], 1, 1)
    emit(normed, qkv, qkv_start, qkv_span, 0, lambda: norm_backward(x2, x3, 2, 1, 4, 8))
    acc[...] = dot(low_two[...], w2[...], 1, 1)

    def early_hidden():
        hidden_back(dg1, 7)
        norm_again(x1, 1)

    emit(h1, low_two, chip_start, span, 0, early_hidden)
    acc[...] = dot(low[...], w1[...], 1, 1)
    emit(normed, low, chip_start, span, 0, lambda: norm_backward(x1, x2, 1, 0, 3, 6))
    low[...] = dot(low_two[...], wo[...], 1, 1).astype(BF)
    emit(att, low_two, chip_start, span, 0)
    emit(mean, low, chip_start, span, 1)
    grad_pix = dot(wv[...], low[...], 1, 1)
    over = stats[0:1, :]
    row = lax.broadcasted_iota(jnp.int32, grad_pix.shape, 0)
    line = jnp.sum(jnp.where(row == channels, grad_pix, 0.0), axis=0, keepdims=True)
    line = (line - jnp.sum(grad_pix * mean[...].astype(F32), axis=0, keepdims=True)) * over
    high = line.astype(BF).astype(F32)
    packed = jnp.where(row < channels, grad_pix * over, 0.0)
    extras = [high, line - high, stats[1:2, :], stats[2:3, :], stats[3:4, :]]
    for at, extra in enumerate(extras):
        packed = jnp.where(row == channels + at, extra, packed)
    pack[...] = packed.astype(BF)
    for slot in range(2):
        for waiting in pending[slot]:
            waiting.wait()


def trunk_slow_body(channels, span, qkv_span, place, lat, mean, stats, cot, gains, shifts, biases, *refs):
    load_sem, store_sem = refs[-2:]
    loads = []
    for at in range(8):
        copy = pltpu.make_async_copy(refs[at], refs[14 + at], load_sem.at[at])
        copy.start()
        loads.append(copy.wait)
    loads += [lambda: None, lambda: None]
    trunk_core(
        channels, span, qkv_span, place[0], place[1], place[2], loads, lat, mean, stats, cot,
        gains, shifts, biases, *refs[8:-2], load_sem.at[0], store_sem
    )


def trunk_fast_body(channels, chips, *refs):
    tiles, refs = refs[:chips], refs[chips:]
    lat_h, cot_h, gains, shifts, biases, value, kv_bias = refs[:7]
    weights_h, refs = refs[7:14], refs[14:]
    lat, mean, raw, stats, tail, load_sem, store_sem = refs[-7:]
    cot = lat
    wv = refs[6]
    place = places()
    chip, core = place[0], place[1]
    tile_copies = tiles_in(place, raw, tiles, load_sem.at[pl.ds(9, chips)])
    loads = []
    pairs = [(lat_h.at[core], lat)]
    pairs += [(weights_h[at], refs[7 + at]) for at in range(7)]
    for at, (src, dst) in enumerate(pairs):
        copy = pltpu.make_async_copy(src, dst, load_sem.at[at])
        copy.start()
        loads.append(copy.wait)
    cot_copy = pltpu.make_async_copy(cot_h.at[core], cot, load_sem.at[8])
    loads += [cot_copy.wait, cot_copy.start]
    fill_rows(wv, value, tail, kv_bias[...].astype(F32))
    for copy in tile_copies:
        copy.wait()
    full = raw[...].astype(F32)
    mean[...] = jnp.where(row_of(full) <= channels, full, 0.0).astype(BF)
    total = (
        full[channels + 1 : channels + 2]
        + full[channels + 2 : channels + 3]
        + full[channels + 3 : channels + 4]
    )
    stats[0:1, :] = 1.0 / total
    for at in range(3):
        stats[at + 1 : at + 2, :] = full[channels + 4 + at : channels + 5 + at]
    trunk_core(
        channels, 256, 768, chip * 256, chip * 768, core, loads, lat, mean, stats, cot,
        gains, shifts, biases, *refs[:-7], load_sem.at[0], store_sem
    )


def trunk_scratch(rows, width, padded):
    big = pltpu.VMEM((rows, width), F32)
    half = pltpu.VMEM((rows, width), BF)
    square = pltpu.VMEM((width, width), BF)
    return [
        pltpu.VMEM((padded, width), BF),
        square,
        square,
        square,
        pltpu.VMEM((width, 3 * width), BF),
        square,
        square,
        square,
        half,
        big,
        half,
        big,
        pltpu.VMEM((rows, 3 * width), BF),
        pltpu.VMEM((HEADS, rows, rows), BF),
        big,
        half,
        big,
        big,
        half,
        big,
        half,
        half,
        half,
        pltpu.VMEM((3, 2, rows, 128), F32),
        pltpu.VMEM((3, 8, width), F32),
        pltpu.VMEM((2, width, 256), BF),
    ]


def trunk_outs(rows, width, padded, sent):
    return [
        ((rows, width), BF),
        ((rows, width), F32),
        ((padded, rows), BF),
        ((16, width), F32),
        ((sent, 128), BF),
        ((sent, 128), BF),
    ]


def trunk_slow(place, lat, mean, stats, cot, gains, shifts, biases, weights, channels, span, qkv_span):
    rows, width = lat.shape
    padded = mean.shape[0]
    sent = width * (6 * (span // 256) + qkv_span // 256) + padded * (span // 256)
    return call(
        functools.partial(trunk_slow_body, channels, span, qkv_span),
        trunk_outs(rows, width, padded, sent),
        trunk_scratch(rows, width, padded)
        + [pltpu.SemaphoreType.DMA((8,)), pltpu.SemaphoreType.DMA((2, 2))],
        (place, lat, mean, stats, cot, gains, shifts, biases, *weights),
        "s" + "v" * 7 + "n" * 8,
        "trunk",
        60 * rows * width * width,
        "avvvaa",
        58,
    )


def trunk(
    tiles, latents, cotangent, gains, shifts, biases, value, kv_bias, weights, channels, padded
):
    _, rows, width = latents.shape
    sent = -(-(9 * width + padded) // 64) * 64
    vm = pltpu.VMEM
    return call(
        functools.partial(trunk_fast_body, channels, len(tiles)),
        trunk_outs(rows, width, padded, sent),
        trunk_scratch(rows, width, padded)
        + [
            vm((rows, width), BF),
            vm((padded, rows), BF),
            vm((padded, rows), BF),
            vm((8, rows), F32),
            vm((16, width), F32),
            pltpu.SemaphoreType.DMA((9 + len(tiles),)),
            pltpu.SemaphoreType.DMA((2, 2)),
        ],
        (*tiles, latents, cotangent, gains, shifts, biases, value, kv_bias, *weights),
        "n" * len(tiles) + "aahhhhv" + "a" * 7,
        "trunk",
        60 * rows * width * width,
        "avvvaa",
        58,
    )


def shifted(devices, step):
    return [(i, (i + step) % devices) for i in range(devices)]


def exchange(tiles, axis):
    devices = tiles.shape[0]
    if devices == 1:
        return tiles
    place = lax.axis_index(axis)
    got = [lax.dynamic_index_in_dim(tiles, place, 0, keepdims=False)]
    for step in range(1, devices):
        tile = lax.dynamic_index_in_dim(tiles, (place + step) % devices, 0, keepdims=False)
        got.append(lax.ppermute(tile, axis, shifted(devices, step)))
    return jnp.stack(got)


def gather(tile, axis):
    devices = lax.axis_size(axis)
    place = lax.axis_index(axis)
    got = [tile]
    for step in range(1, devices):
        got.append(lax.ppermute(tile, axis, shifted(devices, step)))
    stacked = jnp.stack(got)
    order = (place - jnp.arange(devices)) % devices
    return jnp.stack([lax.dynamic_index_in_dim(stacked, order[i], 0, keepdims=False) for i in range(devices)])


def in_tiles(rows, devices):
    return jnp.moveaxis(rows.reshape(rows.shape[0], devices, -1), 1, 0)


def from_tiles(tiles):
    return jnp.moveaxis(tiles, 0, 1).reshape(tiles.shape[1], -1)


def image_parts(rows):
    count = rows.shape[0]
    quarter = -(-count // 64) * 16
    tiles = jnp.pad(rows, ((0, 4 * quarter - count), (0, 0))).reshape(4, quarter, -1)
    return tiles


LOW_PAIRS = [(0, 1), (1, 0), (2, 3), (3, 2)]
HIGH_PAIRS = [(0, 2), (2, 0), (1, 3), (3, 1)]


def pick(pair, at):
    return jnp.where(at == 0, pair[0], pair[1])


def plus(a, b):
    return (a.astype(F32) + b.astype(F32)).astype(BF)


def image_places():
    place = lax.axis_index("img")
    return place // 2, place % 2


def image_first(rows):
    high, low = image_places()
    tiles = image_parts(rows)
    one, two = tiles[:2], tiles[2:]
    got_one = lax.ppermute(pick(one, 1 - low), "img", LOW_PAIRS)
    got_two = lax.ppermute(pick(two, 1 - high), "img", HIGH_PAIRS)
    return plus(pick(one, low), got_one), plus(pick(two, high), got_two)


def image_second(one, two):
    got_one = lax.ppermute(one, "img", HIGH_PAIRS)
    got_two = lax.ppermute(two, "img", LOW_PAIRS)
    return plus(one, got_one), plus(two, got_two)


def image_third(one, two):
    return lax.ppermute(one, "img", LOW_PAIRS), lax.ppermute(two, "img", HIGH_PAIRS)


def image_whole(one, two, got_one, got_two, count):
    high, low = image_places()
    whole = jnp.concatenate(
        [
            jnp.where(low == 0, one, got_one),
            jnp.where(low == 0, got_one, one),
            jnp.where(high == 0, two, got_two),
            jnp.where(high == 0, got_two, two),
        ]
    )
    return whole[:count]


def image_sum(rows):
    one, two = image_second(*image_first(rows))
    return image_whole(one, two, *image_third(one, two), rows.shape[0])


def on_device_slow(
    latents,
    pixels,
    keep_mask,
    cotangent,
    w_query,
    w_key,
    w_value,
    kv_bias,
    w_out,
    w_first,
    w_second,
    w_qkv,
    w_self_out,
    w_third,
    w_fourth,
    norm_gains,
    norm_shifts,
    proj_biases,
    pix_gain,
    pix_shift,
):
    width = latents.shape[-1]
    rows = latents.shape[1]
    channels = pixels.shape[-1]
    padded = -(-(channels + 8) // 16) * 16
    cross_scale = width ** (-0.5)
    chips = lax.axis_size("chip")
    chip = lax.axis_index("chip")
    core = lax.axis_index("core")
    piece = width // (chips * 2)

    def columns(values):
        span = values.shape[-1] // chips
        return lax.dynamic_slice_in_dim(values, chip * span, span, values.ndim - 1)

    def mine(values):
        return lax.dynamic_index_in_dim(values, core, 0, keepdims=False)

    def other(values):
        return lax.dynamic_index_in_dim(values, 1 - core, 0, keepdims=False)

    def swapped(values):
        return lax.ppermute(values, "core", SWAP)

    gains = norm_gains.astype(F32)
    shifts = norm_shifts.astype(F32)
    biases = proj_biases.astype(F32)
    pixel_gain = pix_gain.astype(F32)
    pixel_shift = pix_shift.astype(F32)
    key_rows = jnp.pad(w_key, ((0, padded - channels), (0, 0)))
    value_rows = jnp.concatenate(
        [w_value, kv_bias[None], jnp.zeros((padded - channels - 1, width), BF)]
    )

    q_normed, _, _ = layer_norm(latents.astype(F32), gains[0], shifts[0])
    q_normed_low = q_normed.astype(BF)
    query = (
        (dot(q_normed_low.reshape(-1, width), w_query, 1, 0) + biases[0]) * cross_scale
    ).astype(BF)
    query_pix = jnp.stack(
        [dot(key_rows, query[:rows], 1, 1), dot(key_rows, query[rows:], 1, 1)]
    ).astype(BF)
    p_normed, p_unit, p_inverse = layer_norm(pixels.astype(F32), pixel_gain, pixel_shift)
    lane = jnp.arange(padded)
    ones_lanes = ((lane == channels) | (lane == channels + 1)).astype(BF)
    pix_low = jnp.pad(p_normed.astype(BF), ((0, 0), (0, 0), (0, padded - channels))) + ones_lanes
    kept_pixels = keep_mask[:, :, None] > 0
    scores = jnp.einsum("bpc,bci->bpi", pix_low, query_pix, preferred_element_type=F32)
    local_top = jnp.max(jnp.where(kept_pixels, scores, FLOOR_VALUE), axis=1)
    level = jnp.floor(local_top / LOG_TWO)
    first_weights = jnp.where(
        kept_pixels, jnp.exp(scores - (level * LOG_TWO)[:, None, :]), 0.0
    ).astype(BF)
    local_numer = jnp.einsum("bpc,bpi->bci", pix_low, first_weights, preferred_element_type=F32)

    def packed(body, extras):
        lead = jnp.concatenate([body] + [e[None, :] for e in extras]).astype(BF)
        return jnp.pad(lead, ((0, padded - lead.shape[0]), (0, 0)))

    def fwd_pack(numer, level):
        total = numer[channels]
        return packed(numer[:channels], three_parts(total)[:2] + three_parts(level))

    def fwd_unpack(pack):
        pack = pack.astype(F32)
        total = pack[channels] + pack[channels + 1]
        level = pack[channels + 2] + pack[channels + 3] + pack[channels + 4]
        return (jnp.concatenate([pack[:channels], total[None]]), level)

    def joined(parts):
        top = parts[0][1]
        for _, level in parts[1:]:
            top = jnp.maximum(top, level)
        return (sum(body * jnp.exp2(level - top)[None, :] for body, level in parts), top)

    sent = swapped(fwd_pack(other(local_numer), other(level)))
    body, top = joined([(mine(local_numer)[: channels + 1], mine(level)), fwd_unpack(sent)])
    got = exchange(in_tiles(fwd_pack(body, top), chips), "chip")
    body, top = joined([fwd_unpack(got[i]) for i in range(chips)])
    mean_tile = packed(
        body[:channels] / body[channels], three_parts(body[channels]) + three_parts(top)
    )
    mean_all = from_tiles(gather(mean_tile, "chip")).astype(F32)
    cross_total = mean_all[channels] + mean_all[channels + 1] + mean_all[channels + 2]
    cross_level = mean_all[channels + 3] + mean_all[channels + 4] + mean_all[channels + 5]
    row = jnp.arange(padded)[:, None]
    mean_pix = jnp.where(row < channels, mean_all, jnp.where(row == channels, 1.0, 0.0))
    mean_low = mean_pix.astype(BF)

    _, q_unit, q_inverse = layer_norm(mine(latents).astype(F32), gains[0], shifts[0])
    fast = piece % 128 == 0
    if fast:
        span, qkv_span = 2 * piece, 6 * piece
        starts = (chip * span, chip * qkv_span)
        flip = core
    else:
        span, qkv_span = 256, 256
        starts = tuple(
            jnp.minimum(chip * size // chips // 128 * 128, size - 256) for size in (width, 3 * width)
        )
        flip = 0 * core
    place = jnp.stack([starts[0], starts[1], flip]).astype(jnp.int32)
    stats = jnp.concatenate(
        [
            (1.0 / cross_total)[None],
            mean_all[channels + 3 : channels + 6],
            jnp.zeros((4, rows), F32),
        ]
    )
    output, d_after, own_pack, small_grads, keep, send = trunk_slow(
        place,
        mine(latents),
        mean_low,
        stats,
        mine(cotangent),
        norm_gains,
        norm_shifts,
        proj_biases,
        [value_rows, w_out, w_first, w_second, w_qkv, w_self_out, w_third, w_fourth],
        channels,
        span,
        qkv_span,
    )
    def flat(arrays):
        return jnp.concatenate(
            [a.reshape(a.shape[0], -1, piece).swapaxes(0, 1).reshape(-1, piece) for a in arrays]
        ).astype(BF)

    def split(grads):
        keep, send = [], []
        for g in grads:
            half = g.shape[-1] // 2
            keep.append(lax.dynamic_slice_in_dim(g, core * half, half, 1))
            send.append(lax.dynamic_slice_in_dim(g, (1 - core) * half, half, 1))
        return flat(keep), flat(send)

    squares = [(width, piece)] * 3
    spans = squares + [(width, 3 * piece)] + squares + [(padded, piece)]
    if not fast:
        blocks, at = [], 0
        for r, c in spans:
            size = c * chips * 2
            block = jnp.concatenate([keep[at : at + r], send[at : at + r]], axis=1)
            offset = chip * 2 * c - (starts[1] if size > width else starts[0])
            blocks.append(lax.dynamic_slice_in_dim(block, offset, 2 * c, 1))
            at += r
        keep, send = split(blocks)
    got_pack, got_send = lax.optimization_barrier((swapped(own_pack), swapped(send)))
    both_cores = plus(keep, got_send)
    got_pack, both_cores = lax.optimization_barrier((got_pack, both_cores))
    one, two = image_first(both_cores)
    both = jnp.where(core == 0, jnp.stack([own_pack, got_pack]), jnp.stack([got_pack, own_pack]))

    levels = jnp.sum(both[:, channels + 2 : channels + 5].astype(F32), axis=1)
    weights = jnp.where(kept_pixels, jnp.exp(scores - (levels * LOG_TWO)[:, None, :]), 0.0)
    grad_rows = jnp.where(row[None] < channels + 2, both, jnp.zeros((), BF))
    d_weights = jnp.einsum("bpc,bci->bpi", pix_low, grad_rows, preferred_element_type=F32)
    score_grad = (d_weights * weights).astype(BF)
    query_part = jnp.einsum("bpc,bpi->bci", pix_low, score_grad, preferred_element_type=F32)
    d_pix_normed = jnp.einsum(
        "bpi,bci->bpc", score_grad, query_pix, preferred_element_type=F32
    ) + jnp.einsum("bpi,bci->bpc", weights.astype(BF), grad_rows, preferred_element_type=F32)
    d_pix_normed = d_pix_normed[..., :channels]
    scaled = d_pix_normed * pixel_gain
    d_pixels = p_inverse * (
        scaled
        - jnp.mean(scaled, axis=-1, keepdims=True)
        - p_unit * jnp.mean(scaled * p_unit, axis=-1, keepdims=True)
    )
    pix_sums = jnp.stack(
        [jnp.sum(d_pix_normed * p_unit, axis=1), jnp.sum(d_pix_normed, axis=1)], axis=1
    )
    pix_sums = jnp.pad(pix_sums, ((0, 0), (0, 0), (0, rows - channels)))

    def bwd_pack(body, sums):
        high, low, _ = three_parts(sums)
        return packed(body[:channels], [high[0], low[0], high[1], low[1]])

    def bwd_unpack(pack):
        pack = pack.astype(F32)
        sums = jnp.stack(
            [pack[channels] + pack[channels + 1], pack[channels + 2] + pack[channels + 3]]
        )
        return (pack[:channels], sums)

    query_part, pix_sums, one, two = lax.optimization_barrier((query_part, pix_sums, one, two))
    one, two = image_second(one, two)
    sent = swapped(bwd_pack(other(query_part), other(pix_sums)))
    body_two, sums_two = bwd_unpack(sent)
    body, sums = (mine(query_part)[:channels] + body_two, mine(pix_sums) + sums_two)
    got = exchange(in_tiles(bwd_pack(body, sums), chips), "chip")
    got = [bwd_unpack(got[i]) for i in range(chips)]
    body, sums = (sum(g[0] for g in got), sum(g[1] for g in got))
    body, sums, one, two = lax.optimization_barrier((body, sums, one, two))
    got_one, got_two = image_third(one, two)
    all_parts = from_tiles(gather(bwd_pack(body, sums), "chip"))
    _, sums = bwd_unpack(all_parts)
    query_sum = jnp.where(row < channels, all_parts, jnp.zeros((), BF))

    d_query = dot(query_sum, key_rows, 0, 0) * cross_scale
    d_query_low = d_query.astype(BF)
    own_normed = mine(q_normed_low)
    own_query = lax.dynamic_slice_in_dim(query, core * rows, rows, 0)
    d_w_query = dot(own_normed, columns(d_query_low), 0, 0)
    d_w_key = dot(query_sum, columns(own_query), 1, 0)
    d_q_normed = dot(d_query_low, w_query, 1, 1)
    d_q_in, d_gain_zero, d_shift_zero = norm_back(d_q_normed, q_unit, q_inverse, gains[0])
    d_latents_own = d_after + d_q_in

    def two_images(own):
        got = swapped(own.astype(BF)).astype(own.dtype)
        return jnp.where(core == 0, jnp.stack([own, got]), jnp.stack([got, own]))

    def unpacked(whole, spans):
        outs, at = [], 0
        for r, c in spans:
            count = r * (c // piece)
            part = whole[at : at + count].reshape(c // piece, r, piece).swapaxes(0, 1).reshape(r, c)
            outs.append(part.astype(F32))
            at += count
        return outs

    def reduced(keep, send, spans):
        return unpacked(image_sum(plus(keep, swapped(send))), spans)

    small = jnp.concatenate(
        [
            d_gain_zero[None],
            small_grads[0:3],
            d_shift_zero[None],
            small_grads[3:6],
            row_total(d_query)[None],
            small_grads[6:14],
        ]
    )
    sum_lanes = -(-channels // piece) * piece
    pix_rows = sums[:, :sum_lanes].reshape(-1, piece)
    pix_rows = jnp.concatenate([pix_rows, pix_rows], axis=1)
    last_spans = [(width, piece), (padded, piece), (small.shape[0], piece), (pix_rows.shape[0], piece)]
    keep, send = split([d_w_query, d_w_key, columns(small), pix_rows])
    keep, send, got_one, got_two = lax.optimization_barrier((keep, send, got_one, got_two))
    last = reduced(keep, send, last_spans)
    main = unpacked(image_whole(one, two, got_one, got_two, both_cores.shape[0]), spans)
    d_small = last[2]
    pix_out = last[3].reshape(2, sum_lanes)
    return (
        two_images(output.astype(BF)),
        two_images(d_latents_own),
        d_pixels,
        last[0],
        last[1][:channels],
        main[7][:channels],
        main[7][channels],
        main[6],
        main[5],
        main[4],
        main[3],
        main[2],
        main[1],
        main[0],
        d_small[0:4],
        d_small[4:8],
        d_small[8:17],
        pix_out[0, :channels],
        pix_out[1, :channels],
    )


VMEM_MIB = {
    "look": 28,
    "join_one": 6,
    "join_two": 6,
    "back_one": 20,
    "back_join_one": 6,
    "back_two": 24,
    "back_join_two": 6,
    "tail": 24,
    "last_add": 8,
    "first_add": 8,
    "second_add": 8,
    "last_sum": 6,
    "unpack_main": 24,
    "unpack_last": 8,
}
LOWEST_LEVEL = -16777216.0


def row_of(value):
    return lax.broadcasted_iota(jnp.int32, value.shape, 0)


def with_rows(body, first, extras):
    row = row_of(body)
    for at, extra in enumerate(extras):
        body = jnp.where(row == first + at, extra, body)
    return body


def pack_sum(body, channels, level):
    total = body[channels : channels + 1]
    extras = three_parts(total)[:2] + three_parts(level)
    return with_rows(body, channels, extras).astype(BF)


def unpack_sum(pack, channels):
    pack = pack.astype(F32)
    total = pack[channels : channels + 1] + pack[channels + 1 : channels + 2]
    level = (
        pack[channels + 2 : channels + 3]
        + pack[channels + 3 : channels + 4]
        + pack[channels + 4 : channels + 5]
    )
    return with_rows(pack, channels, [total]), level


def join_sums(parts):
    top = parts[0][1]
    for _, level in parts[1:]:
        top = jnp.maximum(top, level)
    body = None
    for part, level in parts:
        scaled = part * jnp.exp2(level - top)
        body = scaled if body is None else body + scaled
    return body, top


def fill_rows(dst, src, tail, extra=None):
    count = src.shape[0]
    base = count // 16 * 16
    dst[:base, :] = src[:base, :]
    tail[...] = jnp.zeros_like(tail)
    tail[: count - base, :] = src[base:count, :].astype(F32)
    if extra is not None:
        tail[count - base : count - base + 1, :] = extra
    dst[base : base + 16, :] = tail[...].astype(BF)


def pixel_units(pix, image, xs, channels):
    xs[:channels, :] = pix[image].astype(F32)
    x = xs[...]
    inside = row_of(x) < channels
    mean = jnp.sum(x, axis=0, keepdims=True) * (1.0 / channels)
    c = jnp.where(inside, x - mean, 0.0)
    iv = lax.rsqrt(jnp.sum(c * c, axis=0, keepdims=True) * (1.0 / channels) + EPSILON)
    return c * iv, iv, inside


def look_body(
    channels,
    lat_h,
    pix,
    mask,
    pix_gain,
    pix_shift,
    gains,
    shifts,
    biases,
    wk_in,
    wq_h,
    keep,
    send,
    par,
    qp_h,
    q_h,
    pn_h,
    wq,
    held,
    turn,
    normed,
    qs,
    wk,
    xs,
    tail,
    qp_out,
    pn_out,
    sem,
    out_sem,
):
    images, rows, width = lat_h.shape
    core = places()[1]
    lat_copies = [
        pltpu.make_async_copy(lat_h.at[image], held.at[image], out_sem.at[image])
        for image in range(images)
    ]
    for lat_copy in lat_copies:
        lat_copy.start()
    copy = pltpu.make_async_copy(wq_h, wq, sem)
    copy.start()
    turn[...] = jnp.zeros_like(turn)
    turn[0:1, :channels] = pix_gain[...].astype(F32).reshape(1, channels)
    turn[1:2, :channels] = pix_shift[...].astype(F32).reshape(1, channels)
    par[...] = turn[...].T[: par.shape[0]]
    g, s = gains[0:1, :].astype(F32), shifts[0:1, :].astype(F32)

    fill_rows(wk, wk_in, tail)
    xs[...] = jnp.zeros_like(xs)
    for image in range(images):
        lat_copies[image].wait()
        v = held[image].astype(F32)
        c = v - jnp.mean(v, axis=1, keepdims=True)
        iv = lax.rsqrt(jnp.mean(c * c, axis=1, keepdims=True) + EPSILON)
        normed[image] = (c * iv * g + s).astype(BF)
    copy.wait()
    bias = biases[0:1, :].astype(F32)

    def per_image(image, carry):
        qs[image] = ((dot(normed[image], wq[...], 1, 0) + bias) * width ** (-0.5)).astype(BF)
        scored = dot(wk[...], qs[image], 1, 1)
        qp_out[image] = with_rows(scored, channels + 2, [jnp.ones((1, rows), F32)]).astype(BF)
        unit, _, _ = pixel_units(pix, image, xs, channels)
        n = unit * par[:, 0:1] + par[:, 1:2]
        off = jnp.where(mask[pl.ds(image, 1), :] > 0, 0.0, FLOOR_VALUE)
        one = jnp.ones_like(off)
        pn_out[image] = with_rows(n, channels, [one, one, off]).astype(BF)
        scores = dot(pn_out[image], qp_out[image], 0, 0)
        top = jnp.max(scores, axis=0, keepdims=True)
        level = jnp.maximum(jnp.floor(top / LOG_TWO), LOWEST_LEVEL)
        weights = jnp.exp(scores - level * LOG_TWO).astype(BF)
        body = dot(pn_out[image], weights, 1, 0)

        @pl.when(core == image)
        def _():
            keep[...] = with_rows(body, channels + 1, [level])

        @pl.when(core != image)
        def _():
            send[...] = pack_sum(body, channels, level)

        return carry

    lax.fori_loop(0, images, per_image, 0)
    copies = [
        pltpu.make_async_copy(qs.at[core], q_h, out_sem.at[0]),
        pltpu.make_async_copy(qp_out, qp_h, out_sem.at[1]),
        pltpu.make_async_copy(pn_out, pn_h, out_sem.at[2]),
    ]
    for out in copies:
        out.start()
    for out in copies:
        out.wait()


def tiles_out(place, whole, outs):
    chips = len(outs)
    lanes = outs[0].shape[1]
    for step in range(chips):
        at = lax.rem(place[0] + step, chips)
        outs[step][...] = whole[:, pl.ds(pl.multiple_of(at * lanes, lanes), lanes)]


def tiles_in(place, whole, tiles, sem):
    chips = len(tiles)
    lanes = tiles[0].shape[1]
    copies = []
    for step in range(chips):
        at = lax.rem(place[0] + chips - step, chips)
        target = whole.at[:, pl.ds(pl.multiple_of(at * lanes, lanes), lanes)]
        copies.append(pltpu.make_async_copy(tiles[step], target, sem.at[step]))
        copies[-1].start()
    return copies


def places():
    return lax.axis_index("chip"), lax.axis_index("core"), lax.axis_index("img")


def join_one_body(channels, keep, got, *refs):
    outs, whole = refs[:-1], refs[-1]
    place = places()
    own = keep[...]
    body, top = join_sums(
        [(own, own[channels + 1 : channels + 2]), unpack_sum(got[...], channels)]
    )
    whole[...] = pack_sum(body, channels, top)
    tiles_out(place, whole, outs)


def load_all(tiles, held, sem):
    copies = [
        pltpu.make_async_copy(tile, held.at[at], sem.at[at]) for at, tile in enumerate(tiles)
    ]
    for copy in copies:
        copy.start()
    for copy in copies:
        copy.wait()
    return [held[at] for at in range(len(tiles))]


def join_two_body(channels, *refs):
    tiles, out, held, sem = refs[:-3], refs[-3], refs[-2], refs[-1]
    body, top = join_sums([unpack_sum(t, channels) for t in load_all(tiles, held, sem)])
    total = body[channels : channels + 1]
    extras = (jnp.ones_like(total),) + three_parts(total) + three_parts(top)
    out[...] = with_rows(body / total, channels, extras).astype(BF)


def back_one_body(
    channels, own, got, qp_h, pn_h, keep, send, both, score_grad, weights_low, pair, qp_in, pn, sem
):
    images, padded, rows = qp_in.shape
    core = places()[1]
    pairs = [(pn_h, pn), (qp_h, qp_in), (own, pair.at[core]), (got, pair.at[1 - core])]
    copies = [pltpu.make_async_copy(s, d, sem.at[at]) for at, (s, d) in enumerate(pairs)]
    for copy in copies:
        copy.start()
    for copy in copies:
        copy.wait()

    def per_image(image, carry):
        pack = pair[image].astype(F32)
        level = (
            pack[channels + 2 : channels + 3]
            + pack[channels + 3 : channels + 4]
            + pack[channels + 4 : channels + 5]
        )
        grads = jnp.where(row_of(pack) < channels + 2, pack, 0.0).astype(BF)
        both[image] = grads
        scores = dot(pn[image], qp_in[image], 0, 0)
        weights = jnp.exp(scores - level * LOG_TWO)
        weights_low[image] = weights.astype(BF)
        score_grad[image] = (dot(pn[image], grads, 0, 0) * weights).astype(BF)
        body = dot(pn[image], score_grad[image], 1, 0)

        @pl.when(core == image)
        def _():
            keep[...] = body

        @pl.when(core != image)
        def _():
            send[...] = body.astype(BF)

        return carry

    lax.fori_loop(0, images, per_image, 0)


def back_join_one_body(keep, got, *refs):
    outs, whole = refs[:-1], refs[-1]
    place = places()
    whole[...] = (keep[...] + got[...].astype(F32)).astype(BF)
    tiles_out(place, whole, outs)


def back_two_body(
    channels, score_grad, weights_low, qp_h, both, pix, par, out_own, out_got,
    d_pix, sums, out_both, xs, turn, qp, sem
):
    images = pix.shape[0]
    padded = qp.shape[1]
    core = places()[1]
    pairs = [(qp_h, qp), (out_own, out_both.at[core]), (out_got, out_both.at[1 - core])]
    copies = [pltpu.make_async_copy(s, d, sem.at[at]) for at, (s, d) in enumerate(pairs)]
    for copy in copies:
        copy.start()
    copies[0].wait()
    xs[...] = jnp.zeros_like(xs)

    def per_image(image, carry):
        dn = dot(qp[image], score_grad[image], 1, 1) + dot(both[image], weights_low[image], 1, 1)
        unit, iv, inside = pixel_units(pix, image, xs, channels)
        grad = jnp.where(inside, dn, 0.0)
        scaled = grad * par[:, 0:1]
        one = jnp.sum(scaled, axis=0, keepdims=True) * (1.0 / channels)
        two = jnp.sum(scaled * unit, axis=0, keepdims=True) * (1.0 / channels)
        d_pix[image] = (iv * (scaled - one - unit * two))[:channels]
        d_gain = jnp.sum(grad * unit, axis=1, keepdims=True)
        d_shift = jnp.sum(grad, axis=1, keepdims=True)
        return carry[0] + d_gain, carry[1] + d_shift

    zero = jnp.zeros((padded, 1), F32)
    d_gain, d_shift = lax.fori_loop(0, images, per_image, (zero, zero))
    turn[...] = jnp.zeros_like(turn)
    lane = lax.broadcasted_iota(jnp.int32, (padded, 128), 1)
    turn[:padded, :] = jnp.where(lane == 0, d_gain, jnp.where(lane == 1, d_shift, 0.0))
    sums[...] = turn[...].T[:8]
    copies[1].wait()
    copies[2].wait()


def back_join_two_body(channels, *refs):
    tiles, (sums, out, held, sem) = refs[:-4], refs[-4:]
    body = None
    for tile in load_all(tiles, held, sem):
        body = tile.astype(F32) if body is None else body + tile.astype(F32)
    lanes = out.shape[1]
    count = sums.shape[1] // lanes
    extras = [sums[r : r + 1, j * lanes : (j + 1) * lanes] for r in range(2) for j in range(count)]
    out[...] = with_rows(body, channels, extras).astype(BF)


def tail_body(channels, *refs):
    chips = len(refs) - 28
    place = places()
    tiles = refs[:chips]
    (
        lat_h,
        wq_h,
        d_after_h,
        query,
        wk_in,
        gains,
        shifts,
        small_in,
        d_lat,
        d_lat_low,
        keep,
        send,
        lat,
        wq,
        d_after,
        part,
        wk,
        tail,
        normed,
        low,
        acc,
        stat,
        sums,
        small,
        lat_sem,
        wq_sem,
        after_sem,
        tile_sem,
    ) = refs[chips:]
    rows, width = query.shape
    padded = part.shape[0]
    chip, core = place[0], place[1]
    copies = [
        pltpu.make_async_copy(lat_h.at[core], lat, lat_sem),
        pltpu.make_async_copy(wq_h, wq, wq_sem),
        pltpu.make_async_copy(d_after_h, d_after, after_sem),
    ]
    tile_copies = tiles_in(place, part, tiles, tile_sem)
    for copy in copies:
        copy.start()
    fill_rows(wk, wk_in, tail)
    for copy in tile_copies:
        copy.wait()
    base = channels // 16 * 16
    tail[:, :rows] = part[base : base + 16, :].astype(F32)
    extra_rows = tail[channels - base : channels - base + 6, :rows]
    lanes = tiles[0].shape[1]
    pix_rows = extra_rows[:, :lanes]
    for at in range(1, chips):
        pix_rows = pix_rows + extra_rows[:, at * lanes : (at + 1) * lanes]
    part_value = part[...]
    clean = jnp.where(row_of(part_value) < channels, part_value.astype(F32), 0.0).astype(BF)
    part[...] = clean
    d_query = dot(part[...], wk[...], 0, 0) * width ** (-0.5)
    low[...] = d_query.astype(BF)
    bias_row = jnp.sum(jnp.sum(d_query.reshape(-1, 8, width), axis=0), axis=0, keepdims=True)
    copies[0].wait()
    g, s = gains[0:1, :].astype(F32), shifts[0:1, :].astype(F32)

    def norm_step(i, carry):
        at = pl.ds(pl.multiple_of(i * 128, 128), 128)
        v = lat[at, :].astype(F32)
        m = jnp.mean(v, axis=1, keepdims=True)
        c = v - m
        iv = lax.rsqrt(jnp.mean(c * c, axis=1, keepdims=True) + EPSILON)
        normed[at, :] = (c * iv * g + s).astype(BF)
        stat[0, at, :] = jnp.broadcast_to(m, (128, 128))
        stat[1, at, :] = jnp.broadcast_to(iv, (128, 128))
        return carry

    lax.fori_loop(0, rows // 128, norm_step, 0)

    def put(first, value):
        count = value.shape[0]

        @pl.when(core == 0)
        def _():
            keep[first : first + count, :] = value[:, :128]
            send[first : first + count, :] = value[:, 128:]

        @pl.when(core != 0)
        def _():
            send[first : first + count, :] = value[:, :128]
            keep[first : first + count, :] = value[:, 128:]

    cols = pl.ds(pl.multiple_of(chip * 256, 256), 256)
    put(0, dot(normed[...], low[:, cols], 0, 0).astype(BF))
    put(width, dot(part[...], query[:, cols], 1, 0).astype(BF))
    copies[1].wait()
    acc[...] = dot(low[...], wq[...], 1, 1)
    copies[2].wait()
    sums[...] = jnp.zeros_like(sums)

    def back_step(i, carry):
        at = pl.ds(pl.multiple_of(i * 128, 128), 128)
        m, iv = stat[0, at, 0:1], stat[1, at, 0:1]
        unit = (lat[at, :].astype(F32) - m) * iv
        grad = acc[at, :]
        scaled = grad * g
        one = jnp.mean(scaled, axis=1, keepdims=True)
        two = jnp.mean(scaled * unit, axis=1, keepdims=True)
        total = d_after[at, :] + iv * (scaled - one - unit * two)
        d_lat[at, :] = total
        d_lat_low[at, :] = total.astype(BF)
        sums[0] += jnp.sum((grad * unit).reshape(-1, 8, width), axis=0)
        sums[1] += jnp.sum(grad.reshape(-1, 8, width), axis=0)
        return carry

    lax.fori_loop(0, rows // 128, back_step, 0)
    small[...] = jnp.zeros_like(small)
    small[0:1, :] = jnp.sum(sums[0], axis=0, keepdims=True)
    small[1:4, :] = small_in[0:3, :]
    small[4:5, :] = jnp.sum(sums[1], axis=0, keepdims=True)
    small[5:8, :] = small_in[3:6, :]
    small[8:9, :] = bias_row
    small[9:17, :] = small_in[6:14, :]
    put(width + padded, small[:, cols].astype(BF))
    tail[...] = jnp.zeros_like(tail)
    tail[0:6, :lanes] = pix_rows
    spread = tail[:, :128].astype(BF)
    first = width + padded + small.shape[0]
    keep[first : first + 16, :] = spread
    send[first : first + 16, :] = spread


def first_add_body(keep_h, got_h, one, two, keep, got, sem):
    img = places()[2]
    quarter = one.shape[0]
    spots = [1 - lax.rem(img, 2), 3 - lax.div(img, 2)]
    copies = []
    for at, spot in enumerate(spots):
        source = pl.ds(pl.multiple_of(spot * quarter, 16), quarter)
        copies.append(pltpu.make_async_copy(keep_h.at[source, :], keep.at[at], sem.at[at, 0]))
        copies.append(pltpu.make_async_copy(got_h.at[source, :], got.at[at], sem.at[at, 1]))
    for copy in copies:
        copy.start()
    for at, out in enumerate((one, two)):
        copies[2 * at].wait()
        copies[2 * at + 1].wait()
        out[...] = (keep[at].astype(F32) + got[at].astype(F32)).astype(BF)


def second_add_body(keep_h, got_h, more_one, more_two, one, two, keep, got, sem):
    img = places()[2]
    quarter = one.shape[0]
    spots = [lax.rem(img, 2), 2 + lax.div(img, 2)]
    copies = []
    for at, spot in enumerate(spots):
        source = pl.ds(pl.multiple_of(spot * quarter, 16), quarter)
        copies.append(pltpu.make_async_copy(keep_h.at[source, :], keep.at[at], sem.at[at, 0]))
        copies.append(pltpu.make_async_copy(got_h.at[source, :], got.at[at], sem.at[at, 1]))
    for copy in copies:
        copy.start()
    for at, (more, out) in enumerate(((more_one, one), (more_two, two))):
        copies[2 * at].wait()
        copies[2 * at + 1].wait()
        total = keep[at].astype(F32) + got[at].astype(F32) + more[...].astype(F32)
        out[...] = total.astype(BF)


def last_add_body(keep, got, *outs):
    img = places()[2]
    part = outs[0].shape[0]
    for step, out in enumerate(outs):
        at = pl.ds(pl.multiple_of((img ^ step) * part, 16), part)
        out[...] = (keep[at, :].astype(F32) + got[at, :].astype(F32)).astype(BF)


def last_sum_body(*refs):
    tiles, (out, held, sem) = refs[:-3], refs[-3:]
    body = None
    for tile in load_all(tiles, held, sem):
        body = tile.astype(F32) if body is None else body + tile.astype(F32)
    out[...] = body.astype(BF)


def give(outs, pieces, whole, some):
    for out, (first, count, across) in zip(outs, pieces):
        for j in range(across):
            at = first + j * count
            rows = out.shape[0]
            if rows > 16:
                out[:, j * 128 : (j + 1) * 128] = whole[at : at + rows, :].astype(F32)
            else:
                base = min(at // 16 * 16, whole.shape[0] - 32)
                some[...] = whole[base : base + 32, :].astype(F32)
                out[:, j * 128 : (j + 1) * 128] = some[at - base : at - base + rows, :]


def fetch(parts, spots, whole, sem):
    part = parts[0].shape[0]
    copies = []
    for at, spot in enumerate(spots):
        target = whole.at[pl.ds(pl.multiple_of(spot * part, 16), part), :]
        copies.append(pltpu.make_async_copy(parts[at], target, sem.at[at]))
        copies[-1].start()
    for copy in copies:
        copy.wait()


def unpack_last_body(pieces, *refs):
    parts, outs, (whole, some, sem) = refs[:4], refs[4:-3], refs[-3:]
    img = places()[2]
    fetch(parts, [img ^ step for step in range(4)], whole, sem)
    give(outs, pieces, whole, some)


def unpack_main_body(pieces, *refs):
    parts, (lat_own, lat_got, lat_both) = refs[:4], refs[4:7]
    outs, (whole, some, sem) = refs[7:-3], refs[-3:]
    core, img = places()[1:]
    high, low = lax.div(img, 2), lax.rem(img, 2)
    lat_both[core] = lat_own[...]
    lat_both[1 - core] = lat_got[...].astype(F32)
    fetch(parts, [low, 2 + high, 1 - low, 3 - high], whole, sem)
    give(outs, pieces, whole, some)


def call(body, outs, scratch, args, spaces, name, flops, out_spaces=None, vmem=None):
    vmem = vmem or VMEM_MIB[name]
    where = {
        "v": pl.BlockSpec(memory_space=pltpu.VMEM),
        "a": pl.BlockSpec(memory_space=pltpu.HBM),
        "n": pl.BlockSpec(memory_space=pl.ANY),
        "h": pl.BlockSpec(memory_space=pltpu.VMEM),
        "s": pl.BlockSpec(memory_space=pltpu.SMEM),
    }
    out_spaces = out_spaces or "v" * len(outs)
    args = [
        pltpu.with_memory_space_constraint(arg, pltpu.HBM) if s in "ah" else arg
        for arg, s in zip(args, spaces)
    ]
    return pl.pallas_call(
        body,
        out_shape=[
            pltpu.HBM(*o) if s == "a" else jax.ShapeDtypeStruct(*o) for o, s in zip(outs, out_spaces)
        ],
        in_specs=[where[s] for s in spaces],
        out_specs=[where[s] for s in out_spaces],
        scratch_shapes=scratch,
        compiler_params=pltpu.CompilerParams(vmem_limit_bytes=vmem << 20),
        cost_estimate=pl.CostEstimate(flops=flops, transcendentals=0, bytes_accessed=8 << 20),
        name=name,
    )(*args)


def on_device_fast(
    latents,
    pixels,
    keep_mask,
    cotangent,
    w_query,
    w_key,
    w_value,
    kv_bias,
    w_out,
    w_first,
    w_second,
    w_qkv,
    w_self_out,
    w_third,
    w_fourth,
    norm_gains,
    norm_shifts,
    proj_biases,
    pix_gain,
    pix_shift,
):
    images, rows, width = latents.shape
    _, pix, channels = pixels.shape
    padded = -(-(channels + 8) // 16) * 16
    wide = -(-(channels + 8) // 128) * 128
    chips = lax.axis_size("chip")
    lanes = rows // chips
    vm = pltpu.VMEM
    dma = pltpu.SemaphoreType.DMA
    pix_rows = jnp.transpose(pixels, (0, 2, 1))
    unit = 2 * rows * width * width
    cross = 2 * rows * pix * wide * images

    def swapped(values):
        return lax.ppermute(values, "core", SWAP)

    def around(tiles):
        return [
            lax.ppermute(t, "chip", shifted(chips, step + 1)) for step, t in enumerate(tiles)
        ]

    keep, send, par, query_pix, query, pix_normed = call(
        functools.partial(look_body, channels),
        [
            ((padded, rows), F32),
            ((padded, rows), BF),
            ((padded, 128), F32),
            ((images, padded, rows), BF),
            ((rows, width), BF),
            ((images, padded, pix), BF),
        ],
        [
            vm((width, width), BF),
            vm((images, rows, width), BF),
            vm((128, wide), F32),
            vm((images, rows, width), BF),
            vm((images, rows, width), BF),
            vm((padded, width), BF),
            vm((padded, pix), F32),
            vm((16, width), F32),
            vm((images, padded, rows), BF),
            vm((images, padded, pix), BF),
            dma,
            dma((3,)),
        ],
        (
            latents,
            pix_rows,
            keep_mask,
            pix_gain,
            pix_shift,
            norm_gains,
            norm_shifts,
            proj_biases,
            w_key,
            w_query,
        ),
        "avhhhhhhha",
        "look",
        3 * unit + 2 * cross,
        "vvvaaa",
    )
    tiles = call(
        functools.partial(join_one_body, channels),
        [((padded, lanes), BF)] * chips,
        [vm((padded, rows), BF)],
        (keep, swapped(send)),
        "vv",
        "join_one",
        1,
    )
    (tile,) = call(
        functools.partial(join_two_body, channels),
        [((padded, lanes), BF)],
        [vm((chips, padded, lanes), BF), dma((chips,))],
        (tiles[0], *around(tiles[1:])),
        "n" * chips,
        "join_two",
        1,
    )
    tiles = [tile] + around([tile] * (chips - 1))
    output, d_after, own_pack, small_grads, keep, send = trunk(
        tiles,
        latents,
        cotangent,
        norm_gains,
        norm_shifts,
        proj_biases,
        w_value,
        kv_bias[None],
        [w_out, w_first, w_second, w_qkv, w_self_out, w_third, w_fourth],
        channels,
        padded,
    )
    got_pack, send = lax.optimization_barrier((swapped(own_pack), send))
    got_send = swapped(send)
    both_keep = keep
    keep, send, both, score_grad, weights_low = call(
        functools.partial(back_one_body, channels),
        [
            ((padded, rows), F32),
            ((padded, rows), BF),
            ((images, padded, rows), BF),
            ((images, pix, rows), BF),
            ((images, pix, rows), BF),
        ],
        [
            vm((images, padded, rows), BF),
            vm((images, padded, rows), BF),
            vm((images, padded, pix), BF),
            dma((4,)),
        ],
        (own_pack, got_pack, query_pix, pix_normed),
        "nnaa",
        "back_one",
        3 * cross,
    )
    keep, send, got_send = lax.optimization_barrier((keep, send, got_send))
    quarter = both_keep.shape[0] // 4
    adds = [vm((2, quarter, 128), BF), vm((2, quarter, 128), BF), dma((2, 2))]
    one, two = call(
        first_add_body,
        [((quarter, 128), BF)] * 2,
        adds,
        (both_keep, got_send),
        "an",
        "first_add",
        1,
    )
    got_output = swapped(output)
    tiles = call(
        back_join_one_body,
        [((padded, lanes), BF)] * chips,
        [vm((padded, rows), BF)],
        (keep, swapped(send)),
        "vv",
        "back_join_one",
        1,
    )
    tiles, score_grad, one, two = lax.optimization_barrier((tiles, score_grad, one, two))
    one, two = lax.ppermute(one, "img", LOW_PAIRS), lax.ppermute(two, "img", HIGH_PAIRS)
    d_pixels, sums, both_outputs = call(
        functools.partial(back_two_body, channels),
        [((images, channels, pix), F32), ((8, wide), F32), ((images, rows, width), BF)],
        [
            vm((padded, pix), F32),
            vm((wide, 128), F32),
            vm((images, padded, rows), BF),
            dma((3,)),
        ],
        (score_grad, weights_low, query_pix, both, pix_rows, par, output, got_output),
        "vvavvvan",
        "back_two",
        2 * cross,
    )
    (tile,) = call(
        functools.partial(back_join_two_body, channels),
        [((padded, lanes), BF)],
        [vm((chips, padded, lanes), BF), dma((chips,))],
        (tiles[0], *around(tiles[1:]), sums),
        "n" * chips + "v",
        "back_join_two",
        1,
    )
    tile, one, two = lax.optimization_barrier((tile, one, two))

    one, two = image_second(
        *call(
            second_add_body,
            [((quarter, 128), BF)] * 2,
            adds,
            (both_keep, got_send, one, two),
            "anvv",
            "second_add",
            1,
        )
    )
    tiles = [tile] + around([tile] * (chips - 1))
    last_rows = width + padded + 32 + 16
    d_lat, d_lat_low, keep, send = call(
        functools.partial(tail_body, channels),
        [
            ((rows, width), F32),
            ((rows, width), BF),
            ((last_rows, 128), BF),
            ((last_rows, 128), BF),
        ],
        [
            vm((rows, width), BF),
            vm((width, width), BF),
            vm((rows, width), F32),
            vm((padded, rows), BF),
            vm((padded, width), BF),
            vm((16, width), F32),
            vm((rows, width), BF),
            vm((rows, width), BF),
            vm((rows, width), F32),
            vm((2, rows, 128), F32),
            vm((2, 8, width), F32),
            vm((32, width), F32),
            dma,
            dma,
            dma,
            dma((chips,)),
        ],
        (
            *tiles,
            latents,
            w_query,
            d_after,
            query,
            w_key,
            norm_gains,
            norm_shifts,
            small_grads,
        ),
        "n" * chips + "aanhhhhh",
        "tail",
        3 * unit,
    )
    keep, send, d_lat_low, one, two = lax.optimization_barrier((keep, send, d_lat_low, one, two))
    got_one, got_two = image_third(one, two)
    part = last_rows // 4
    got_lat = swapped(d_lat_low)

    def partners(tiles):
        return [
            lax.ppermute(t, "img", [(i, i ^ (step + 1)) for i in range(4)])
            for step, t in enumerate(tiles)
        ]

    tiles = call(
        last_add_body,
        [((part, 128), BF)] * 4,
        [],
        (keep, swapped(send)),
        "vv",
        "last_add",
        1,
    )
    tiles, got_lat = lax.optimization_barrier((tiles, got_lat))
    arrived = partners(tiles[1:])
    square = (width, 128)
    first, pieces, shapes = 0, [], []
    for across in (1, 1, 1, 3, 1, 1, 1):
        pieces.append((first, width, across))
        shapes.append((width, 128 * across))
        first += width * across
    pieces += [(first, padded, 1), (first + channels, 1, 1)]
    shapes += [(channels, 128), (1, 128)]
    both_latents, *main = call(
        functools.partial(unpack_main_body, pieces),
        [((images, rows, width), F32)] + [(s, F32) for s in shapes],
        [vm((4 * one.shape[0], 128), BF), vm((32, 128), F32), dma((4,))],
        (one, two, got_one, got_two, d_lat, got_lat),
        "nnnnvv",
        "unpack_main",
        1,
    )
    d_pixels = jnp.transpose(d_pixels, (0, 2, 1))
    arrived, both_latents, d_pixels = lax.optimization_barrier((arrived, both_latents, d_pixels))
    (tile,) = call(
        last_sum_body,
        [((part, 128), BF)],
        [vm((4, part, 128), BF), dma((4,))],
        (tiles[0], *arrived),
        "nnnn",
        "last_sum",
        1,
    )
    parts = partners([tile] * 3)
    at = width + padded
    rest = call(
        functools.partial(
            unpack_last_body,
            [
                (0, width, 1),
                (width, padded, 1),
                (at, 4, 1),
                (at + 4, 4, 1),
                (at + 8, 9, 1),
                (at + 32, 1, 3),
                (at + 35, 1, 3),
            ],
        ),
        [
            (s, F32)
            for s in (square, (channels, 128), (4, 128), (4, 128), (9, 128), (1, 384), (1, 384))
        ],
        [vm((last_rows, 128), BF), vm((32, 128), F32), dma((4,))],
        (tile, *parts),
        "nnnn",
        "unpack_last",
        1,
    )
    return (
        both_outputs,
        both_latents,
        d_pixels,
        rest[0],
        rest[1],
        main[7],
        main[8][0],
        main[6],
        main[5],
        main[4],
        main[3],
        main[2],
        main[1],
        main[0],
        rest[2],
        rest[3],
        rest[4],
        rest[5][0, :channels],
        rest[6][0, :channels],
    )


def on_device(*args):
    rows, width = args[0].shape[1:]
    chips = lax.axis_size("chip")
    if (width // chips) % 256 == 0 and width // chips == 256 and (rows // chips) % 128 == 0:
        return on_device_fast(*args)
    return on_device_slow(*args)


def solution(mesh):
    images, pieces = mesh.devices.shape
    split = Mesh(mesh.devices.reshape(images, pieces // 2, 2), ("img", "chip", "core"))
    latent = P("img", None, None)
    weight = P(None, PIX)
    placed = (latent, P("img", PIX, None), P("img", PIX), latent) + (P(),) * 16
    return jax.shard_map(
        on_device,
        mesh=split,
        in_specs=placed,
        out_specs=(latent, latent, P("img", PIX, None), weight, weight, weight, P(PIX))
        + (weight,) * 10
        + (P(), P()),
        check_vma=False,
    )
```

```python
import functools

import jax
import jax.numpy as jnp
from jax import lax
from jax.experimental import pallas as pl
from jax.experimental.pallas import tpu as pltpu
from jax.sharding import Mesh
from jax.sharding import PartitionSpec as P

HEADS = 8
EPSILON = 1e-05
LOG_TWO = 0.6931471805599453
FLOOR_VALUE = -1e30
BF = jnp.bfloat16
F32 = jnp.float32
SWAP = [(0, 1), (1, 0)]
PIX = ("chip", "core")


def dot(a, b, ca, cb):
    return lax.dot_general(a, b, (((ca,), (cb,)), ((), ())), preferred_element_type=F32)


def layer_norm(values, norm_gain, norm_shift):
    centre = values - jnp.mean(values, axis=-1, keepdims=True)
    inverse = lax.rsqrt(jnp.mean(centre * centre, axis=-1, keepdims=True) + EPSILON)
    unit_rows = centre * inverse
    return (unit_rows * norm_gain + norm_shift, unit_rows, inverse)


def row_total(values):
    return jnp.sum(values, axis=tuple(range(values.ndim - 1)))


def norm_back(grad, unit_rows, inverse, norm_gain):
    scaled = grad * norm_gain
    d_values = inverse * (
        scaled
        - jnp.mean(scaled, axis=-1, keepdims=True)
        - unit_rows * jnp.mean(scaled * unit_rows, axis=-1, keepdims=True)
    )
    return (d_values, row_total(grad * unit_rows), row_total(grad))


def gelu_exact(values):
    return jax.nn.gelu(values, approximate=False)


def three_parts(values):
    high = values.astype(BF).astype(F32)
    rest = values - high
    middle = rest.astype(BF).astype(F32)
    return (high, middle, rest - middle)


ROOT_HALF = 0.7071067811865476
ROOT_TWO_PI = 0.3989422804014327


def trunk_core(
    channels,
    span,
    qkv_span,
    chip_start,
    qkv_start,
    flip,
    waits,
    lat,
    mean,
    stats,
    cot,
    gains,
    shifts,
    biases,
    result,
    d_after,
    pack,
    small,
    keep_h,
    send_h,
    wv,
    wo,
    w1,
    w2,
    wq,
    ws,
    w3,
    w4,
    att,
    dg1,
    h1,
    x2,
    qkv,
    wl,
    inv_total,
    sl,
    x3,
    dg4,
    h4,
    acc,
    low,
    low_two,
    normed,
    stat,
    sums,
    stage,
    spare_sem,
    store_sem,
):
    rows, width = lat.shape
    head_dim = width // HEADS
    head_scale = head_dim ** (-0.5)
    x1 = d_after
    def over_rows(step, most=512):
        block = min(most, rows)
        if block == rows:
            step(pl.ds(0, rows))
            return

        def run(i, carry):
            step(pl.ds(pl.multiple_of(i * block, block), block))
            return carry

        lax.fori_loop(0, rows // block, run, 0)

    def vector(ref, i):
        return ref[i : i + 1, :].astype(F32)

    def add_sum(at, value):
        sums[at] += jnp.sum(value.reshape(-1, 8, width), axis=0)

    def clear(*ats):
        for at in ats:
            sums[at] = jnp.zeros((8, width), F32)

    def flush(at, row):
        small[row : row + 1, :] = jnp.sum(sums[at], axis=0, keepdims=True)

    def norm_forward(x, i):
        g, s = vector(gains, i), vector(shifts, i)

        def step(at):
            v = x[at, :]
            m = jnp.mean(v, axis=1, keepdims=True)
            c = v - m
            iv = lax.rsqrt(jnp.mean(c * c, axis=1, keepdims=True) + EPSILON)
            normed[at, :] = (c * iv * g + s).astype(BF)
            stat[i - 1, 0, at, :] = jnp.broadcast_to(m, (m.shape[0], 128))
            stat[i - 1, 1, at, :] = jnp.broadcast_to(iv, (m.shape[0], 128))

        over_rows(step)

    def norm_again(x, i):
        g, s = vector(gains, i), vector(shifts, i)

        def step(at):
            m, iv = stat[i - 1, 0, at, 0:1], stat[i - 1, 1, at, 0:1]
            normed[at, :] = ((x[at, :] - m) * iv * g + s).astype(BF)

        over_rows(step)

    def norm_backward(x, skip, i, gain_row, shift_row, bias_row):
        g = vector(gains, i)
        clear(0, 1, 2)

        def step(at):
            m, iv = stat[i - 1, 0, at, 0:1], stat[i - 1, 1, at, 0:1]
            unit = (x[at, :] - m) * iv
            grad = acc[at, :]
            scaled = grad * g
            mean_one = jnp.mean(scaled, axis=1, keepdims=True)
            mean_two = jnp.mean(scaled * unit, axis=1, keepdims=True)
            total = skip[at, :].astype(F32) + iv * (scaled - mean_one - unit * mean_two)
            add_sum(0, grad * unit)
            add_sum(1, grad)
            add_sum(2, total)
            x[at, :] = total
            low_two[at, :] = total.astype(BF)

        over_rows(step)
        flush(0, gain_row)
        flush(1, shift_row)
        flush(2, bias_row)

    def hidden(bias_row, h, dg):
        b = vector(biases, bias_row)

        def step(at):
            v = acc[at, :] + b
            cdf = 0.5 * (1.0 + lax.erf(v * ROOT_HALF))
            h[at, :] = (v * cdf).astype(BF)
            dg[at, :] = cdf + v * (jnp.exp(-0.5 * v * v) * ROOT_TWO_PI)

        over_rows(step)

    def hidden_back(dg, bias_row):
        clear(0)

        def step(at):
            d = acc[at, :] * dg[at, :]
            add_sum(0, d)
            low[at, :] = d.astype(BF)

        over_rows(step)
        flush(0, bias_row)

    pending = [[], []]
    state = {"slot": 0, "row": 0}

    def emit(x, dy, start, span, ca, beside=None):
        count = x.shape[1 - ca]
        half = span // 2
        for t in range(half // 128):
            slot = state["slot"]
            state["slot"] = 1 - slot
            for waiting in pending[slot]:
                waiting.wait()
            pending[slot] = []
            mine = dy[:, pl.ds(pl.multiple_of(start + flip * half + t * 128, 128), 128)]
            other = dy[:, pl.ds(pl.multiple_of(start + (1 - flip) * half + t * 128, 128), 128)]
            both = jnp.concatenate([mine, other], axis=1)
            stage[slot, :count, :] = dot(x[...], both, ca, 0).astype(BF)
            if beside is not None and t == half // 128 - 1:
                beside()
            target = pl.ds(state["row"] + t * count, count)
            for side, out in enumerate((keep_h, send_h)):
                src = stage.at[slot, pl.ds(0, count), pl.ds(side * 128, 128)]
                copy = pltpu.make_async_copy(src, out.at[target, :], store_sem.at[slot, side])
                copy.start()
                pending[slot].append(copy)
        state["row"] += count * (half // 128)

    waits[0]()
    att[...] = dot(mean[...], wv[...], 0, 0).astype(BF)
    waits[1]()
    acc[...] = dot(att[...], wo[...], 1, 0)
    out_bias = vector(biases, 1)

    def after_cross(at):
        x1[at, :] = lat[at, :].astype(F32) + acc[at, :] + out_bias

    over_rows(after_cross)
    waits[9]()
    norm_forward(x1, 1)
    waits[2]()
    acc[...] = dot(normed[...], w1[...], 1, 0)
    hidden(2, h1, dg1)
    waits[3]()
    x2[...] = x1[...] + dot(h1[...], w2[...], 1, 0) + vector(biases, 3)
    norm_forward(x2, 2)
    waits[4]()
    qkv[:, :width] = (
        (dot(normed[...], wq[:, :width], 1, 0) + vector(biases, 4)) * head_scale
    ).astype(BF)
    qkv[:, width : 2 * width] = dot(normed[...], wq[:, width : 2 * width], 1, 0).astype(BF)
    qkv[:, 2 * width :] = (
        dot(normed[...], wq[:, 2 * width :], 1, 0) + vector(biases, 5)
    ).astype(BF)
    ones = jnp.ones((rows, head_dim), BF)

    def head_at(h, part):
        return pl.ds(pl.multiple_of(h * head_dim + part * width, head_dim), head_dim)

    def head_forward(h, carry):
        scores = dot(qkv[:, head_at(h, 0)], qkv[:, head_at(h, 1)], 1, 1)
        top = jnp.max(scores, axis=1, keepdims=True)
        shift = LOG_TWO * jnp.floor(top / LOG_TWO)
        weights = jnp.exp(scores - shift).astype(BF)
        wl[h] = weights
        value = jnp.concatenate([qkv[:, head_at(h, 2)], ones], axis=1)
        both = dot(weights, value, 1, 0)
        over = 1.0 / both[:, head_dim:]
        inv_total[:, head_at(h, 0)] = over
        sl[:, head_at(h, 0)] = (both[:, :head_dim] * over).astype(BF)
        return carry

    lax.fori_loop(0, HEADS, head_forward, 0, unroll=True)
    waits[5]()
    x3[...] = x2[...] + dot(sl[...], ws[...], 1, 0) + vector(biases, 6)
    norm_forward(x3, 3)
    waits[6]()
    acc[...] = dot(normed[...], w3[...], 1, 0)
    hidden(7, h4, dg4)
    waits[7]()
    low[...] = (x3[...] + dot(h4[...], w4[...], 1, 0) + vector(biases, 8)).astype(BF)
    result_copy = pltpu.make_async_copy(low, result, spare_sem)
    result_copy.start()

    waits[8]()
    clear(0)

    def cot_sum(at):
        add_sum(0, cot[at, :].astype(F32))

    over_rows(cot_sum)
    flush(0, 13)
    acc[...] = dot(cot[...], w4[...], 1, 1)
    result_copy.wait()
    emit(h4, cot, chip_start, span, 0, lambda: hidden_back(dg4, 12))
    acc[...] = dot(low[...], w3[...], 1, 1)
    emit(normed, low, chip_start, span, 0, lambda: norm_backward(x3, cot, 3, 2, 5, 11))
    acc[...] = dot(low_two[...], ws[...], 1, 1)
    clear(0, 1)

    def head_backward(h, carry):
        head = head_at(h, 0)
        query, keys, value = qkv[:, head], qkv[:, head_at(h, 1)], qkv[:, head_at(h, 2)]
        grad = acc[:, head] * inv_total[:, head]
        numer_grad = grad.astype(BF)
        total_part = (-(grad * sl[:, head].astype(F32))).astype(BF)
        weights = wl[h]
        d_weights = dot(
            jnp.concatenate([numer_grad, total_part], axis=1),
            jnp.concatenate([value, ones], axis=1),
            1,
            1,
        )
        score_grad = (d_weights * weights.astype(F32)).astype(BF)
        d_value = dot(weights, numer_grad, 0, 0)
        d_query = dot(score_grad, keys, 1, 0) * head_scale
        d_keys = dot(score_grad, query, 0, 0)
        qkv[:, head] = d_query.astype(BF)
        qkv[:, head_at(h, 1)] = d_keys.astype(BF)
        qkv[:, head_at(h, 2)] = d_value.astype(BF)
        sums[0, :, head] = jnp.sum(d_query.reshape(-1, 8, head_dim), axis=0)
        sums[1, :, head] = jnp.sum(d_value.reshape(-1, 8, head_dim), axis=0)
        return carry

    def heads_backward():
        lax.fori_loop(0, HEADS, head_backward, 0, unroll=True)

    emit(sl, low_two, chip_start, span, 0, heads_backward)
    flush(0, 9)
    flush(1, 10)
    norm_again(x2, 2)
    acc[...] = dot(qkv[...], wq[...], 1, 1)
    emit(normed, qkv, qkv_start, qkv_span, 0, lambda: norm_backward(x2, x3, 2, 1, 4, 8))
    acc[...] = dot(low_two[...], w2[...], 1, 1)

    def early_hidden():
        hidden_back(dg1, 7)
        norm_again(x1, 1)

    emit(h1, low_two, chip_start, span, 0, early_hidden)
    acc[...] = dot(low[...], w1[...], 1, 1)
    emit(normed, low, chip_start, span, 0, lambda: norm_backward(x1, x2, 1, 0, 3, 6))
    low[...] = dot(low_two[...], wo[...], 1, 1).astype(BF)
    emit(att, low_two, chip_start, span, 0)
    emit(mean, low, chip_start, span, 1)
    grad_pix = dot(wv[...], low[...], 1, 1)
    over = stats[0:1, :]
    row = lax.broadcasted_iota(jnp.int32, grad_pix.shape, 0)
    line = jnp.sum(jnp.where(row == channels, grad_pix, 0.0), axis=0, keepdims=True)
    line = (line - jnp.sum(grad_pix * mean[...].astype(F32), axis=0, keepdims=True)) * over
    high = line.astype(BF).astype(F32)
    packed = jnp.where(row < channels, grad_pix * over, 0.0)
    extras = [high, line - high, stats[1:2, :], stats[2:3, :], stats[3:4, :]]
    for at, extra in enumerate(extras):
        packed = jnp.where(row == channels + at, extra, packed)
    pack[...] = packed.astype(BF)
    for slot in range(2):
        for waiting in pending[slot]:
            waiting.wait()


def trunk_slow_body(channels, span, qkv_span, place, lat, mean, stats, cot, gains, shifts, biases, *refs):
    load_sem, store_sem = refs[-2:]
    loads = []
    for at in range(8):
        copy = pltpu.make_async_copy(refs[at], refs[14 + at], load_sem.at[at])
        copy.start()
        loads.append(copy.wait)
    loads += [lambda: None, lambda: None]
    trunk_core(
        channels, span, qkv_span, place[0], place[1], place[2], loads, lat, mean, stats, cot,
        gains, shifts, biases, *refs[8:-2], load_sem.at[0], store_sem
    )


def trunk_fast_body(channels, chips, *refs):
    tiles, refs = refs[:chips], refs[chips:]
    lat_h, cot_h, gains, shifts, biases, value, kv_bias = refs[:7]
    weights_h, refs = refs[7:14], refs[14:]
    lat, mean, raw, stats, tail, load_sem, store_sem = refs[-7:]
    cot = lat
    wv = refs[6]
    place = places()
    chip, core = place[0], place[1]
    tile_copies = tiles_in(place, raw, tiles, load_sem.at[pl.ds(9, chips)])
    loads = []
    pairs = [(lat_h.at[core], lat)]
    pairs += [(weights_h[at], refs[7 + at]) for at in range(7)]
    for at, (src, dst) in enumerate(pairs):
        copy = pltpu.make_async_copy(src, dst, load_sem.at[at])
        copy.start()
        loads.append(copy.wait)
    cot_copy = pltpu.make_async_copy(cot_h.at[core], cot, load_sem.at[8])
    loads += [cot_copy.wait, cot_copy.start]
    fill_rows(wv, value, tail, kv_bias[...].astype(F32))
    for copy in tile_copies:
        copy.wait()
    full = raw[...].astype(F32)
    mean[...] = jnp.where(row_of(full) <= channels, full, 0.0).astype(BF)
    total = (
        full[channels + 1 : channels + 2]
        + full[channels + 2 : channels + 3]
        + full[channels + 3 : channels + 4]
    )
    stats[0:1, :] = 1.0 / total
    for at in range(3):
        stats[at + 1 : at + 2, :] = full[channels + 4 + at : channels + 5 + at]
    trunk_core(
        channels, 256, 768, chip * 256, chip * 768, core, loads, lat, mean, stats, cot,
        gains, shifts, biases, *refs[:-7], load_sem.at[0], store_sem
    )


def trunk_scratch(rows, width, padded):
    big = pltpu.VMEM((rows, width), F32)
    half = pltpu.VMEM((rows, width), BF)
    square = pltpu.VMEM((width, width), BF)
    return [
        pltpu.VMEM((padded, width), BF),
        square,
        square,
        square,
        pltpu.VMEM((width, 3 * width), BF),
        square,
        square,
        square,
        half,
        big,
        half,
        big,
        pltpu.VMEM((rows, 3 * width), BF),
        pltpu.VMEM((HEADS, rows, rows), BF),
        big,
        half,
        big,
        big,
        half,
        big,
        half,
        half,
        half,
        pltpu.VMEM((3, 2, rows, 128), F32),
        pltpu.VMEM((3, 8, width), F32),
        pltpu.VMEM((2, width, 256), BF),
    ]


def trunk_outs(rows, width, padded, sent):
    return [
        ((rows, width), BF),
        ((rows, width), F32),
        ((padded, rows), BF),
        ((16, width), F32),
        ((sent, 128), BF),
        ((sent, 128), BF),
    ]


def trunk_slow(place, lat, mean, stats, cot, gains, shifts, biases, weights, channels, span, qkv_span):
    rows, width = lat.shape
    padded = mean.shape[0]
    sent = width * (6 * (span // 256) + qkv_span // 256) + padded * (span // 256)
    return call(
        functools.partial(trunk_slow_body, channels, span, qkv_span),
        trunk_outs(rows, width, padded, sent),
        trunk_scratch(rows, width, padded)
        + [pltpu.SemaphoreType.DMA((8,)), pltpu.SemaphoreType.DMA((2, 2))],
        (place, lat, mean, stats, cot, gains, shifts, biases, *weights),
        "s" + "v" * 7 + "n" * 8,
        "trunk",
        60 * rows * width * width,
        "avvvaa",
        58,
    )


def trunk(
    tiles, latents, cotangent, gains, shifts, biases, value, kv_bias, weights, channels, padded
):
    _, rows, width = latents.shape
    sent = -(-(9 * width + padded) // 64) * 64
    vm = pltpu.VMEM
    return call(
        functools.partial(trunk_fast_body, channels, len(tiles)),
        trunk_outs(rows, width, padded, sent),
        trunk_scratch(rows, width, padded)
        + [
            vm((rows, width), BF),
            vm((padded, rows), BF),
            vm((padded, rows), BF),
            vm((8, rows), F32),
            vm((16, width), F32),
            pltpu.SemaphoreType.DMA((9 + len(tiles),)),
            pltpu.SemaphoreType.DMA((2, 2)),
        ],
        (*tiles, latents, cotangent, gains, shifts, biases, value, kv_bias, *weights),
        "n" * len(tiles) + "aahhhhv" + "a" * 7,
        "trunk",
        60 * rows * width * width,
        "avvvaa",
        58,
    )


def shifted(devices, step):
    return [(i, (i + step) % devices) for i in range(devices)]


def exchange(tiles, axis):
    devices = tiles.shape[0]
    if devices == 1:
        return tiles
    place = lax.axis_index(axis)
    got = [lax.dynamic_index_in_dim(tiles, place, 0, keepdims=False)]
    for step in range(1, devices):
        tile = lax.dynamic_index_in_dim(tiles, (place + step) % devices, 0, keepdims=False)
        got.append(lax.ppermute(tile, axis, shifted(devices, step)))
    return jnp.stack(got)


def gather(tile, axis):
    devices = lax.axis_size(axis)
    place = lax.axis_index(axis)
    got = [tile]
    for step in range(1, devices):
        got.append(lax.ppermute(tile, axis, shifted(devices, step)))
    stacked = jnp.stack(got)
    order = (place - jnp.arange(devices)) % devices
    return jnp.stack([lax.dynamic_index_in_dim(stacked, order[i], 0, keepdims=False) for i in range(devices)])


def in_tiles(rows, devices):
    return jnp.moveaxis(rows.reshape(rows.shape[0], devices, -1), 1, 0)


def from_tiles(tiles):
    return jnp.moveaxis(tiles, 0, 1).reshape(tiles.shape[1], -1)


def image_parts(rows):
    count = rows.shape[0]
    quarter = -(-count // 64) * 16
    tiles = jnp.pad(rows, ((0, 4 * quarter - count), (0, 0))).reshape(4, quarter, -1)
    return tiles


LOW_PAIRS = [(0, 1), (1, 0), (2, 3), (3, 2)]
HIGH_PAIRS = [(0, 2), (2, 0), (1, 3), (3, 1)]


def pick(pair, at):
    return jnp.where(at == 0, pair[0], pair[1])


def plus(a, b):
    return (a.astype(F32) + b.astype(F32)).astype(BF)


def image_places():
    place = lax.axis_index("img")
    return place // 2, place % 2


def image_first(rows):
    high, low = image_places()
    tiles = image_parts(rows)
    one, two = tiles[:2], tiles[2:]
    got_one = lax.ppermute(pick(one, 1 - low), "img", LOW_PAIRS)
    got_two = lax.ppermute(pick(two, 1 - high), "img", HIGH_PAIRS)
    return plus(pick(one, low), got_one), plus(pick(two, high), got_two)


def image_second(one, two):
    got_one = lax.ppermute(one, "img", HIGH_PAIRS)
    got_two = lax.ppermute(two, "img", LOW_PAIRS)
    return plus(one, got_one), plus(two, got_two)


def image_third(one, two):
    return lax.ppermute(one, "img", LOW_PAIRS), lax.ppermute(two, "img", HIGH_PAIRS)


def image_whole(one, two, got_one, got_two, count):
    high, low = image_places()
    whole = jnp.concatenate(
        [
            jnp.where(low == 0, one, got_one),
            jnp.where(low == 0, got_one, one),
            jnp.where(high == 0, two, got_two),
            jnp.where(high == 0, got_two, two),
        ]
    )
    return whole[:count]


def image_sum(rows):
    one, two = image_second(*image_first(rows))
    return image_whole(one, two, *image_third(one, two), rows.shape[0])


def on_device_slow(
    latents,
    pixels,
    keep_mask,
    cotangent,
    w_query,
    w_key,
    w_value,
    kv_bias,
    w_out,
    w_first,
    w_second,
    w_qkv,
    w_self_out,
    w_third,
    w_fourth,
    norm_gains,
    norm_shifts,
    proj_biases,
    pix_gain,
    pix_shift,
):
    width = latents.shape[-1]
    rows = latents.shape[1]
    channels = pixels.shape[-1]
    padded = -(-(channels + 8) // 16) * 16
    cross_scale = width ** (-0.5)
    chips = lax.axis_size("chip")
    chip = lax.axis_index("chip")
    core = lax.axis_index("core")
    piece = width // (chips * 2)

    def columns(values):
        span = values.shape[-1] // chips
        return lax.dynamic_slice_in_dim(values, chip * span, span, values.ndim - 1)

    def mine(values):
        return lax.dynamic_index_in_dim(values, core, 0, keepdims=False)

    def other(values):
        return lax.dynamic_index_in_dim(values, 1 - core, 0, keepdims=False)

    def swapped(values):
        return lax.ppermute(values, "core", SWAP)

    gains = norm_gains.astype(F32)
    shifts = norm_shifts.astype(F32)
    biases = proj_biases.astype(F32)
    pixel_gain = pix_gain.astype(F32)
    pixel_shift = pix_shift.astype(F32)
    key_rows = jnp.pad(w_key, ((0, padded - channels), (0, 0)))
    value_rows = jnp.concatenate(
        [w_value, kv_bias[None], jnp.zeros((padded - channels - 1, width), BF)]
    )

    q_normed, _, _ = layer_norm(latents.astype(F32), gains[0], shifts[0])
    q_normed_low = q_normed.astype(BF)
    query = (
        (dot(q_normed_low.reshape(-1, width), w_query, 1, 0) + biases[0]) * cross_scale
    ).astype(BF)
    query_pix = jnp.stack(
        [dot(key_rows, query[:rows], 1, 1), dot(key_rows, query[rows:], 1, 1)]
    ).astype(BF)
    p_normed, p_unit, p_inverse = layer_norm(pixels.astype(F32), pixel_gain, pixel_shift)
    lane = jnp.arange(padded)
    ones_lanes = ((lane == channels) | (lane == channels + 1)).astype(BF)
    pix_low = jnp.pad(p_normed.astype(BF), ((0, 0), (0, 0), (0, padded - channels))) + ones_lanes
    kept_pixels = keep_mask[:, :, None] > 0
    scores = jnp.einsum("bpc,bci->bpi", pix_low, query_pix, preferred_element_type=F32)
    local_top = jnp.max(jnp.where(kept_pixels, scores, FLOOR_VALUE), axis=1)
    level = jnp.floor(local_top / LOG_TWO)
    first_weights = jnp.where(
        kept_pixels, jnp.exp(scores - (level * LOG_TWO)[:, None, :]), 0.0
    ).astype(BF)
    local_numer = jnp.einsum("bpc,bpi->bci", pix_low, first_weights, preferred_element_type=F32)

    def packed(body, extras):
        lead = jnp.concatenate([body] + [e[None, :] for e in extras]).astype(BF)
        return jnp.pad(lead, ((0, padded - lead.shape[0]), (0, 0)))

    def fwd_pack(numer, level):
        total = numer[channels]
        return packed(numer[:channels], three_parts(total)[:2] + three_parts(level))

    def fwd_unpack(pack):
        pack = pack.astype(F32)
        total = pack[channels] + pack[channels + 1]
        level = pack[channels + 2] + pack[channels + 3] + pack[channels + 4]
        return (jnp.concatenate([pack[:channels], total[None]]), level)

    def joined(parts):
        top = parts[0][1]
        for _, level in parts[1:]:
            top = jnp.maximum(top, level)
        return (sum(body * jnp.exp2(level - top)[None, :] for body, level in parts), top)

    sent = swapped(fwd_pack(other(local_numer), other(level)))
    body, top = joined([(mine(local_numer)[: channels + 1], mine(level)), fwd_unpack(sent)])
    got = exchange(in_tiles(fwd_pack(body, top), chips), "chip")
    body, top = joined([fwd_unpack(got[i]) for i in range(chips)])
    mean_tile = packed(
        body[:channels] / body[channels], three_parts(body[channels]) + three_parts(top)
    )
    mean_all = from_tiles(gather(mean_tile, "chip")).astype(F32)
    cross_total = mean_all[channels] + mean_all[channels + 1] + mean_all[channels + 2]
    cross_level = mean_all[channels + 3] + mean_all[channels + 4] + mean_all[channels + 5]
    row = jnp.arange(padded)[:, None]
    mean_pix = jnp.where(row < channels, mean_all, jnp.where(row == channels, 1.0, 0.0))
    mean_low = mean_pix.astype(BF)

    _, q_unit, q_inverse = layer_norm(mine(latents).astype(F32), gains[0], shifts[0])
    fast = piece % 128 == 0
    if fast:
        span, qkv_span = 2 * piece, 6 * piece
        starts = (chip * span, chip * qkv_span)
        flip = core
    else:
        span, qkv_span = 256, 256
        starts = tuple(
            jnp.minimum(chip * size // chips // 128 * 128, size - 256) for size in (width, 3 * width)
        )
        flip = 0 * core
    place = jnp.stack([starts[0], starts[1], flip]).astype(jnp.int32)
    stats = jnp.concatenate(
        [
            (1.0 / cross_total)[None],
            mean_all[channels + 3 : channels + 6],
            jnp.zeros((4, rows), F32),
        ]
    )
    output, d_after, own_pack, small_grads, keep, send = trunk_slow(
        place,
        mine(latents),
        mean_low,
        stats,
        mine(cotangent),
        norm_gains,
        norm_shifts,
        proj_biases,
        [value_rows, w_out, w_first, w_second, w_qkv, w_self_out, w_third, w_fourth],
        channels,
        span,
        qkv_span,
    )
    def flat(arrays):
        return jnp.concatenate(
            [a.reshape(a.shape[0], -1, piece).swapaxes(0, 1).reshape(-1, piece) for a in arrays]
        ).astype(BF)

    def split(grads):
        keep, send = [], []
        for g in grads:
            half = g.shape[-1] // 2
            keep.append(lax.dynamic_slice_in_dim(g, core * half, half, 1))
            send.append(lax.dynamic_slice_in_dim(g, (1 - core) * half, half, 1))
        return flat(keep), flat(send)

    squares = [(width, piece)] * 3
    spans = squares + [(width, 3 * piece)] + squares + [(padded, piece)]
    if not fast:
        blocks, at = [], 0
        for r, c in spans:
            size = c * chips * 2
            block = jnp.concatenate([keep[at : at + r], send[at : at + r]], axis=1)
            offset = chip * 2 * c - (starts[1] if size > width else starts[0])
            blocks.append(lax.dynamic_slice_in_dim(block, offset, 2 * c, 1))
            at += r
        keep, send = split(blocks)
    got_pack, got_send = lax.optimization_barrier((swapped(own_pack), swapped(send)))
    both_cores = plus(keep, got_send)
    got_pack, both_cores = lax.optimization_barrier((got_pack, both_cores))
    one, two = image_first(both_cores)
    both = jnp.where(core == 0, jnp.stack([own_pack, got_pack]), jnp.stack([got_pack, own_pack]))

    levels = jnp.sum(both[:, channels + 2 : channels + 5].astype(F32), axis=1)
    weights = jnp.where(kept_pixels, jnp.exp(scores - (levels * LOG_TWO)[:, None, :]), 0.0)
    grad_rows = jnp.where(row[None] < channels + 2, both, jnp.zeros((), BF))
    d_weights = jnp.einsum("bpc,bci->bpi", pix_low, grad_rows, preferred_element_type=F32)
    score_grad = (d_weights * weights).astype(BF)
    query_part = jnp.einsum("bpc,bpi->bci", pix_low, score_grad, preferred_element_type=F32)
    d_pix_normed = jnp.einsum(
        "bpi,bci->bpc", score_grad, query_pix, preferred_element_type=F32
    ) + jnp.einsum("bpi,bci->bpc", weights.astype(BF), grad_rows, preferred_element_type=F32)
    d_pix_normed = d_pix_normed[..., :channels]
    scaled = d_pix_normed * pixel_gain
    d_pixels = p_inverse * (
        scaled
        - jnp.mean(scaled, axis=-1, keepdims=True)
        - p_unit * jnp.mean(scaled * p_unit, axis=-1, keepdims=True)
    )
    pix_sums = jnp.stack(
        [jnp.sum(d_pix_normed * p_unit, axis=1), jnp.sum(d_pix_normed, axis=1)], axis=1
    )
    pix_sums = jnp.pad(pix_sums, ((0, 0), (0, 0), (0, rows - channels)))

    def bwd_pack(body, sums):
        high, low, _ = three_parts(sums)
        return packed(body[:channels], [high[0], low[0], high[1], low[1]])

    def bwd_unpack(pack):
        pack = pack.astype(F32)
        sums = jnp.stack(
            [pack[channels] + pack[channels + 1], pack[channels + 2] + pack[channels + 3]]
        )
        return (pack[:channels], sums)

    query_part, pix_sums, one, two = lax.optimization_barrier((query_part, pix_sums, one, two))
    one, two = image_second(one, two)
    sent = swapped(bwd_pack(other(query_part), other(pix_sums)))
    body_two, sums_two = bwd_unpack(sent)
    body, sums = (mine(query_part)[:channels] + body_two, mine(pix_sums) + sums_two)
    got = exchange(in_tiles(bwd_pack(body, sums), chips), "chip")
    got = [bwd_unpack(got[i]) for i in range(chips)]
    body, sums = (sum(g[0] for g in got), sum(g[1] for g in got))
    body, sums, one, two = lax.optimization_barrier((body, sums, one, two))
    got_one, got_two = image_third(one, two)
    all_parts = from_tiles(gather(bwd_pack(body, sums), "chip"))
    _, sums = bwd_unpack(all_parts)
    query_sum = jnp.where(row < channels, all_parts, jnp.zeros((), BF))

    d_query = dot(query_sum, key_rows, 0, 0) * cross_scale
    d_query_low = d_query.astype(BF)
    own_normed = mine(q_normed_low)
    own_query = lax.dynamic_slice_in_dim(query, core * rows, rows, 0)
    d_w_query = dot(own_normed, columns(d_query_low), 0, 0)
    d_w_key = dot(query_sum, columns(own_query), 1, 0)
    d_q_normed = dot(d_query_low, w_query, 1, 1)
    d_q_in, d_gain_zero, d_shift_zero = norm_back(d_q_normed, q_unit, q_inverse, gains[0])
    d_latents_own = d_after + d_q_in

    def two_images(own):
        got = swapped(own.astype(BF)).astype(own.dtype)
        return jnp.where(core == 0, jnp.stack([own, got]), jnp.stack([got, own]))

    def unpacked(whole, spans):
        outs, at = [], 0
        for r, c in spans:
            count = r * (c // piece)
            part = whole[at : at + count].reshape(c // piece, r, piece).swapaxes(0, 1).reshape(r, c)
            outs.append(part.astype(F32))
            at += count
        return outs

    def reduced(keep, send, spans):
        return unpacked(image_sum(plus(keep, swapped(send))), spans)

    small = jnp.concatenate(
        [
            d_gain_zero[None],
            small_grads[0:3],
            d_shift_zero[None],
            small_grads[3:6],
            row_total(d_query)[None],
            small_grads[6:14],
        ]
    )
    sum_lanes = -(-channels // piece) * piece
    pix_rows = sums[:, :sum_lanes].reshape(-1, piece)
    pix_rows = jnp.concatenate([pix_rows, pix_rows], axis=1)
    last_spans = [(width, piece), (padded, piece), (small.shape[0], piece), (pix_rows.shape[0], piece)]
    keep, send = split([d_w_query, d_w_key, columns(small), pix_rows])
    keep, send, got_one, got_two = lax.optimization_barrier((keep, send, got_one, got_two))
    last = reduced(keep, send, last_spans)
    main = unpacked(image_whole(one, two, got_one, got_two, both_cores.shape[0]), spans)
    d_small = last[2]
    pix_out = last[3].reshape(2, sum_lanes)
    return (
        two_images(output.astype(BF)),
        two_images(d_latents_own),
        d_pixels,
        last[0],
        last[1][:channels],
        main[7][:channels],
        main[7][channels],
        main[6],
        main[5],
        main[4],
        main[3],
        main[2],
        main[1],
        main[0],
        d_small[0:4],
        d_small[4:8],
        d_small[8:17],
        pix_out[0, :channels],
        pix_out[1, :channels],
    )


VMEM_MIB = {
    "look": 28,
    "join_one": 6,
    "join_two": 6,
    "back_one": 20,
    "back_join_one": 6,
    "back_two": 24,
    "back_join_two": 6,
    "tail": 24,
    "last_add": 8,
    "first_add": 8,
    "second_add": 8,
    "last_sum": 6,
    "unpack_main": 24,
    "latents": 10,
    "unpack_last": 8,
}
LOWEST_LEVEL = -16777216.0


def row_of(value):
    return lax.broadcasted_iota(jnp.int32, value.shape, 0)


def with_rows(body, first, extras):
    row = row_of(body)
    for at, extra in enumerate(extras):
        body = jnp.where(row == first + at, extra, body)
    return body


def pack_sum(body, channels, level):
    total = body[channels : channels + 1]
    extras = three_parts(total)[:2] + three_parts(level)
    return with_rows(body, channels, extras).astype(BF)


def unpack_sum(pack, channels):
    pack = pack.astype(F32)
    total = pack[channels : channels + 1] + pack[channels + 1 : channels + 2]
    level = (
        pack[channels + 2 : channels + 3]
        + pack[channels + 3 : channels + 4]
        + pack[channels + 4 : channels + 5]
    )
    return with_rows(pack, channels, [total]), level


def join_sums(parts):
    top = parts[0][1]
    for _, level in parts[1:]:
        top = jnp.maximum(top, level)
    body = None
    for part, level in parts:
        scaled = part * jnp.exp2(level - top)
        body = scaled if body is None else body + scaled
    return body, top


def fill_rows(dst, src, tail, extra=None):
    count = src.shape[0]
    base = count // 16 * 16
    dst[:base, :] = src[:base, :]
    tail[...] = jnp.zeros_like(tail)
    tail[: count - base, :] = src[base:count, :].astype(F32)
    if extra is not None:
        tail[count - base : count - base + 1, :] = extra
    dst[base : base + 16, :] = tail[...].astype(BF)


def pixel_units(pix, image, xs, channels):
    xs[:channels, :] = pix[:, image, :].astype(F32)
    x = xs[...]
    inside = row_of(x) < channels
    mean = jnp.sum(x, axis=0, keepdims=True) * (1.0 / channels)
    c = jnp.where(inside, x - mean, 0.0)
    iv = lax.rsqrt(jnp.sum(c * c, axis=0, keepdims=True) * (1.0 / channels) + EPSILON)
    return c * iv, iv, inside


def look_body(
    channels,
    lat_h,
    pix_h,
    mask,
    pix_gain,
    pix_shift,
    gains,
    shifts,
    biases,
    wk_in,
    wq_h,
    keep,
    send,
    par,
    qp_h,
    q_h,
    pn_h,
    wq,
    held,
    turn,
    normed,
    qs,
    wk,
    xs,
    tail,
    qp_out,
    pn_out,
    bodies,
    pix,
    sem,
    out_sem,
):
    images, rows, width = lat_h.shape
    core = places()[1]
    lat_copies = [
        pltpu.make_async_copy(lat_h.at[image], held.at[image], out_sem.at[image])
        for image in range(images)
    ]
    for lat_copy in lat_copies:
        lat_copy.start()
    pix_copy = pltpu.make_async_copy(pix_h, pix, out_sem.at[2])
    pix_copy.start()
    copy = pltpu.make_async_copy(wq_h, wq, sem)
    copy.start()
    turn[...] = jnp.zeros_like(turn)
    turn[0:1, :channels] = pix_gain[...].astype(F32).reshape(1, channels)
    turn[1:2, :channels] = pix_shift[...].astype(F32).reshape(1, channels)
    par[...] = turn[...].T[: par.shape[0]]
    g, s = gains[0:1, :].astype(F32), shifts[0:1, :].astype(F32)

    fill_rows(wk, wk_in, tail)
    xs[...] = jnp.zeros_like(xs)
    for image in range(images):
        lat_copies[image].wait()
        v = held[image].astype(F32)
        c = v - jnp.mean(v, axis=1, keepdims=True)
        iv = lax.rsqrt(jnp.mean(c * c, axis=1, keepdims=True) + EPSILON)
        normed[image] = (c * iv * g + s).astype(BF)
    copy.wait()
    bias = biases[0:1, :].astype(F32)

    def per_image(image):
        qs[image] = ((dot(normed[image], wq[...], 1, 0) + bias) * width ** (-0.5)).astype(BF)
        scored = dot(wk[...], qs[image], 1, 1)
        qp_out[image] = with_rows(scored, channels + 2, [jnp.ones((1, rows), F32)]).astype(BF)
        unit, _, _ = pixel_units(pix, image, xs, channels)
        n = unit * par[:, 0:1] + par[:, 1:2]
        off = jnp.where(mask[pl.ds(image, 1), :] > 0, 0.0, FLOOR_VALUE)
        one = jnp.ones_like(off)
        pn_out[image] = with_rows(n, channels, [one, one, off]).astype(BF)
        scores = dot(pn_out[image], qp_out[image], 0, 0)
        top = jnp.max(scores, axis=0, keepdims=True)
        level = jnp.maximum(jnp.floor(top / LOG_TWO), LOWEST_LEVEL)
        weights = jnp.exp(scores - level * LOG_TWO).astype(BF)
        body = dot(pn_out[image], weights, 1, 0)
        bodies[image] = with_rows(body, channels + 1, [level])

    pix_copy.wait()
    for image in range(images):
        per_image(image)
    keep[...] = bodies[core]
    other = bodies[1 - core]
    send[...] = pack_sum(other, channels, other[channels + 1 : channels + 2])
    copies = [
        pltpu.make_async_copy(qs.at[core], q_h, out_sem.at[0]),
        pltpu.make_async_copy(qp_out, qp_h, out_sem.at[1]),
        pltpu.make_async_copy(pn_out, pn_h, out_sem.at[2]),
    ]
    for out in copies:
        out.start()
    for out in copies:
        out.wait()


def tiles_out(place, whole, outs):
    chips = len(outs)
    lanes = outs[0].shape[1]
    for step in range(chips):
        at = lax.rem(place[0] + step, chips)
        outs[step][...] = whole[:, pl.ds(pl.multiple_of(at * lanes, lanes), lanes)]


def tiles_in(place, whole, tiles, sem):
    chips = len(tiles)
    lanes = tiles[0].shape[1]
    copies = []
    for step in range(chips):
        at = lax.rem(place[0] + chips - step, chips)
        target = whole.at[:, pl.ds(pl.multiple_of(at * lanes, lanes), lanes)]
        copies.append(pltpu.make_async_copy(tiles[step], target, sem.at[step]))
        copies[-1].start()
    return copies


def places():
    return lax.axis_index("chip"), lax.axis_index("core"), lax.axis_index("img")


def join_one_body(channels, keep, got, *refs):
    outs, whole = refs[:-1], refs[-1]
    place = places()
    own = keep[...]
    body, top = join_sums(
        [(own, own[channels + 1 : channels + 2]), unpack_sum(got[...], channels)]
    )
    whole[...] = pack_sum(body, channels, top)
    tiles_out(place, whole, outs)


def load_all(tiles, held, sem):
    copies = [
        pltpu.make_async_copy(tile, held.at[at], sem.at[at]) for at, tile in enumerate(tiles)
    ]
    for copy in copies:
        copy.start()
    for copy in copies:
        copy.wait()
    return [held[at] for at in range(len(tiles))]


def join_two_body(channels, *refs):
    tiles, out, held, sem = refs[:-3], refs[-3], refs[-2], refs[-1]
    body, top = join_sums([unpack_sum(t, channels) for t in load_all(tiles, held, sem)])
    total = body[channels : channels + 1]
    extras = (jnp.ones_like(total),) + three_parts(total) + three_parts(top)
    out[...] = with_rows(body / total, channels, extras).astype(BF)


def back_one_body(
    channels, own, got, qp_h, pn_h, keep, send, both, score_grad, weights_low, pair, qp_in, pn, bodies, sem
):
    images, padded, rows = qp_in.shape
    core = places()[1]
    pairs = [(pn_h, pn), (qp_h, qp_in), (own, pair.at[core]), (got, pair.at[1 - core])]
    copies = [pltpu.make_async_copy(s, d, sem.at[at]) for at, (s, d) in enumerate(pairs)]
    for copy in copies:
        copy.start()
    for copy in copies:
        copy.wait()

    def per_image(image):
        pack = pair[image].astype(F32)
        level = (
            pack[channels + 2 : channels + 3]
            + pack[channels + 3 : channels + 4]
            + pack[channels + 4 : channels + 5]
        )
        grads = jnp.where(row_of(pack) < channels + 2, pack, 0.0).astype(BF)
        both[image] = grads
        scores = dot(pn[image], qp_in[image], 0, 0)
        weights = jnp.exp(scores - level * LOG_TWO)
        weights_low[image] = weights.astype(BF)
        score_grad[image] = (dot(pn[image], grads, 0, 0) * weights).astype(BF)
        bodies[image] = dot(pn[image], score_grad[image], 1, 0)

    for image in range(images):
        per_image(image)
    keep[...] = bodies[core]
    send[...] = bodies[1 - core].astype(BF)


def back_join_one_body(keep, got, *refs):
    outs, whole = refs[:-1], refs[-1]
    place = places()
    whole[...] = (keep[...] + got[...].astype(F32)).astype(BF)
    tiles_out(place, whole, outs)


def back_two_body(
    channels, score_grad, weights_low, qp_h, both, pix, par, out_own, out_got,
    d_pix, sums, out_both, xs, turn, qp, sem
):
    images = pix.shape[1]
    padded = qp.shape[1]
    core = places()[1]
    pairs = [(qp_h, qp), (out_own, out_both.at[core]), (out_got, out_both.at[1 - core])]
    copies = [pltpu.make_async_copy(s, d, sem.at[at]) for at, (s, d) in enumerate(pairs)]
    for copy in copies:
        copy.start()
    copies[0].wait()
    xs[...] = jnp.zeros_like(xs)

    def per_image(image, carry):
        dn = dot(qp[image], score_grad[image], 1, 1) + dot(both[image], weights_low[image], 1, 1)
        unit, iv, inside = pixel_units(pix, image, xs, channels)
        grad = jnp.where(inside, dn, 0.0)
        scaled = grad * par[:, 0:1]
        one = jnp.sum(scaled, axis=0, keepdims=True) * (1.0 / channels)
        two = jnp.sum(scaled * unit, axis=0, keepdims=True) * (1.0 / channels)
        d_pix[:, image, :] = (iv * (scaled - one - unit * two))[:channels]
        d_gain = jnp.sum(grad * unit, axis=1, keepdims=True)
        d_shift = jnp.sum(grad, axis=1, keepdims=True)
        return carry[0] + d_gain, carry[1] + d_shift

    zero = jnp.zeros((padded, 1), F32)
    d_gain, d_shift = zero, zero
    for image in range(images):
        d_gain, d_shift = per_image(image, (d_gain, d_shift))
    turn[...] = jnp.zeros_like(turn)
    lane = lax.broadcasted_iota(jnp.int32, (padded, 128), 1)
    turn[:padded, :] = jnp.where(lane == 0, d_gain, jnp.where(lane == 1, d_shift, 0.0))
    sums[...] = turn[...].T[:8]
    copies[1].wait()
    copies[2].wait()


def back_join_two_body(channels, *refs):
    tiles, (sums, out, held, sem) = refs[:-4], refs[-4:]
    body = None
    for tile in load_all(tiles, held, sem):
        body = tile.astype(F32) if body is None else body + tile.astype(F32)
    lanes = out.shape[1]
    count = sums.shape[1] // lanes
    extras = [sums[r : r + 1, j * lanes : (j + 1) * lanes] for r in range(2) for j in range(count)]
    out[...] = with_rows(body, channels, extras).astype(BF)


def tail_body(channels, *refs):
    chips = len(refs) - 28
    place = places()
    tiles = refs[:chips]
    (
        lat_h,
        wq_h,
        d_after_h,
        query,
        wk_in,
        gains,
        shifts,
        small_in,
        d_lat,
        d_lat_low,
        keep,
        send,
        lat,
        wq,
        d_after,
        part,
        wk,
        tail,
        normed,
        low,
        acc,
        stat,
        sums,
        small,
        lat_sem,
        wq_sem,
        after_sem,
        tile_sem,
    ) = refs[chips:]
    rows, width = query.shape
    padded = part.shape[0]
    chip, core = place[0], place[1]
    copies = [
        pltpu.make_async_copy(lat_h.at[core], lat, lat_sem),
        pltpu.make_async_copy(wq_h, wq, wq_sem),
        pltpu.make_async_copy(d_after_h, d_after, after_sem),
    ]
    tile_copies = tiles_in(place, part, tiles, tile_sem)
    for copy in copies:
        copy.start()
    fill_rows(wk, wk_in, tail)
    for copy in tile_copies:
        copy.wait()
    base = channels // 16 * 16
    tail[:, :rows] = part[base : base + 16, :].astype(F32)
    extra_rows = tail[channels - base : channels - base + 6, :rows]
    lanes = tiles[0].shape[1]
    pix_rows = extra_rows[:, :lanes]
    for at in range(1, chips):
        pix_rows = pix_rows + extra_rows[:, at * lanes : (at + 1) * lanes]
    part_value = part[...]
    clean = jnp.where(row_of(part_value) < channels, part_value.astype(F32), 0.0).astype(BF)
    part[...] = clean
    d_query = dot(part[...], wk[...], 0, 0) * width ** (-0.5)
    low[...] = d_query.astype(BF)
    bias_row = jnp.sum(jnp.sum(d_query.reshape(-1, 8, width), axis=0), axis=0, keepdims=True)
    copies[0].wait()
    g, s = gains[0:1, :].astype(F32), shifts[0:1, :].astype(F32)

    v = lat[...].astype(F32)
    m = jnp.mean(v, axis=1, keepdims=True)
    c = v - m
    iv = lax.rsqrt(jnp.mean(c * c, axis=1, keepdims=True) + EPSILON)
    normed[...] = (c * iv * g + s).astype(BF)
    stat[0] = jnp.broadcast_to(m, (rows, 128))
    stat[1] = jnp.broadcast_to(iv, (rows, 128))

    def put(first, value):
        count = value.shape[0]

        @pl.when(core == 0)
        def _():
            keep[first : first + count, :] = value[:, :128]
            send[first : first + count, :] = value[:, 128:]

        @pl.when(core != 0)
        def _():
            send[first : first + count, :] = value[:, :128]
            keep[first : first + count, :] = value[:, 128:]

    cols = pl.ds(pl.multiple_of(chip * 256, 256), 256)
    put(0, dot(normed[...], low[:, cols], 0, 0).astype(BF))
    put(width, dot(part[...], query[:, cols], 1, 0).astype(BF))
    copies[1].wait()
    acc[...] = dot(low[...], wq[...], 1, 1)
    copies[2].wait()

    m, iv = stat[0, :, 0:1], stat[1, :, 0:1]
    unit = (lat[...].astype(F32) - m) * iv
    grad = acc[...]
    scaled = grad * g
    first_mean = jnp.mean(scaled, axis=1, keepdims=True)
    second_mean = jnp.mean(scaled * unit, axis=1, keepdims=True)
    total = d_after[...] + iv * (scaled - first_mean - unit * second_mean)
    d_lat[...] = total
    d_lat_low[...] = total.astype(BF)
    sums[0] = jnp.sum((grad * unit).reshape(-1, 8, width), axis=0)
    sums[1] = jnp.sum(grad.reshape(-1, 8, width), axis=0)
    small[...] = jnp.zeros_like(small)
    small[0:1, :] = jnp.sum(sums[0], axis=0, keepdims=True)
    small[1:4, :] = small_in[0:3, :]
    small[4:5, :] = jnp.sum(sums[1], axis=0, keepdims=True)
    small[5:8, :] = small_in[3:6, :]
    small[8:9, :] = bias_row
    small[9:17, :] = small_in[6:14, :]
    put(width + padded, small[:, cols].astype(BF))
    tail[...] = jnp.zeros_like(tail)
    tail[0:6, :lanes] = pix_rows
    spread = tail[:, :128].astype(BF)
    first = width + padded + small.shape[0]
    keep[first : first + 16, :] = spread
    send[first : first + 16, :] = spread


def first_add_body(keep_h, got_h, one, two, keep, got, sem):
    img = places()[2]
    quarter = one.shape[0]
    spots = [1 - lax.rem(img, 2), 3 - lax.div(img, 2)]
    copies = []
    for at, spot in enumerate(spots):
        source = pl.ds(pl.multiple_of(spot * quarter, 16), quarter)
        copies.append(pltpu.make_async_copy(keep_h.at[source, :], keep.at[at], sem.at[at, 0]))
        copies.append(pltpu.make_async_copy(got_h.at[source, :], got.at[at], sem.at[at, 1]))
    for copy in copies:
        copy.start()
    for at, out in enumerate((one, two)):
        copies[2 * at].wait()
        copies[2 * at + 1].wait()
        out[...] = (keep[at].astype(F32) + got[at].astype(F32)).astype(BF)


def second_add_body(keep_h, got_h, more_one, more_two, one, two, keep, got, sem):
    img = places()[2]
    quarter = one.shape[0]
    spots = [lax.rem(img, 2), 2 + lax.div(img, 2)]
    copies = []
    for at, spot in enumerate(spots):
        source = pl.ds(pl.multiple_of(spot * quarter, 16), quarter)
        copies.append(pltpu.make_async_copy(keep_h.at[source, :], keep.at[at], sem.at[at, 0]))
        copies.append(pltpu.make_async_copy(got_h.at[source, :], got.at[at], sem.at[at, 1]))
    for copy in copies:
        copy.start()
    for at, (more, out) in enumerate(((more_one, one), (more_two, two))):
        copies[2 * at].wait()
        copies[2 * at + 1].wait()
        total = keep[at].astype(F32) + got[at].astype(F32) + more[...].astype(F32)
        out[...] = total.astype(BF)


def last_add_body(keep, got, *outs):
    img = places()[2]
    part = outs[0].shape[0]
    for step, out in enumerate(outs):
        at = pl.ds(pl.multiple_of((img ^ step) * part, 16), part)
        out[...] = (keep[at, :].astype(F32) + got[at, :].astype(F32)).astype(BF)


def last_sum_body(*refs):
    tiles, (out, held, sem) = refs[:-3], refs[-3:]
    body = None
    for tile in load_all(tiles, held, sem):
        body = tile.astype(F32) if body is None else body + tile.astype(F32)
    out[...] = body.astype(BF)


def give(outs, pieces, whole, some):
    for out, (first, count, across) in zip(outs, pieces):
        for j in range(across):
            at = first + j * count
            rows = out.shape[0]
            if rows > 16:
                out[:, j * 128 : (j + 1) * 128] = whole[at : at + rows, :].astype(F32)
            else:
                base = min(at // 16 * 16, whole.shape[0] - 32)
                some[...] = whole[base : base + 32, :].astype(F32)
                out[:, j * 128 : (j + 1) * 128] = some[at - base : at - base + rows, :]


def fetch(parts, spots, whole, sem):
    part = parts[0].shape[0]
    copies = []
    for at, spot in enumerate(spots):
        target = whole.at[pl.ds(pl.multiple_of(spot * part, 16), part), :]
        copies.append(pltpu.make_async_copy(parts[at], target, sem.at[at]))
        copies[-1].start()
    for copy in copies:
        copy.wait()


def unpack_last_body(pieces, *refs):
    parts, outs, (whole, some, sem) = refs[:4], refs[4:-3], refs[-3:]
    img = places()[2]
    fetch(parts, [img ^ step for step in range(4)], whole, sem)
    give(outs, pieces, whole, some)


def latents_body(own, got, both):
    core = places()[1]
    both[core] = own[...]
    both[1 - core] = got[...].astype(F32)


def unpack_main_body(pieces, *refs):
    parts, outs, (whole, some, sem) = refs[:4], refs[4:-3], refs[-3:]
    img = places()[2]
    high, low = lax.div(img, 2), lax.rem(img, 2)
    fetch(parts, [low, 2 + high, 1 - low, 3 - high], whole, sem)
    give(outs, pieces, whole, some)


def call(body, outs, scratch, args, spaces, name, flops, out_spaces=None, vmem=None):
    vmem = vmem or VMEM_MIB[name]
    where = {
        "v": pl.BlockSpec(memory_space=pltpu.VMEM),
        "a": pl.BlockSpec(memory_space=pltpu.HBM),
        "n": pl.BlockSpec(memory_space=pl.ANY),
        "h": pl.BlockSpec(memory_space=pltpu.VMEM),
        "s": pl.BlockSpec(memory_space=pltpu.SMEM),
    }
    out_spaces = out_spaces or "v" * len(outs)
    args = [
        pltpu.with_memory_space_constraint(arg, pltpu.HBM) if s in "ah" else arg
        for arg, s in zip(args, spaces)
    ]
    return pl.pallas_call(
        body,
        out_shape=[
            pltpu.HBM(*o) if s == "a" else jax.ShapeDtypeStruct(*o) for o, s in zip(outs, out_spaces)
        ],
        in_specs=[where[s] for s in spaces],
        out_specs=[where[s] for s in out_spaces],
        scratch_shapes=scratch,
        compiler_params=pltpu.CompilerParams(vmem_limit_bytes=vmem << 20),
        cost_estimate=pl.CostEstimate(flops=flops, transcendentals=0, bytes_accessed=8 << 20),
        name=name,
    )(*args)


def on_device_fast(
    latents,
    pixels,
    keep_mask,
    cotangent,
    w_query,
    w_key,
    w_value,
    kv_bias,
    w_out,
    w_first,
    w_second,
    w_qkv,
    w_self_out,
    w_third,
    w_fourth,
    norm_gains,
    norm_shifts,
    proj_biases,
    pix_gain,
    pix_shift,
):
    images, rows, width = latents.shape
    _, pix, channels = pixels.shape
    padded = -(-(channels + 8) // 16) * 16
    wide = -(-(channels + 8) // 128) * 128
    chips = lax.axis_size("chip")
    lanes = rows // chips
    vm = pltpu.VMEM
    dma = pltpu.SemaphoreType.DMA
    pix_rows = jnp.transpose(pixels, (2, 0, 1))
    unit = 2 * rows * width * width
    cross = 2 * rows * pix * wide * images

    def swapped(values):
        return lax.ppermute(values, "core", SWAP)

    def around(tiles):
        return [
            lax.ppermute(t, "chip", shifted(chips, step + 1)) for step, t in enumerate(tiles)
        ]

    keep, send, par, query_pix, query, pix_normed = call(
        functools.partial(look_body, channels),
        [
            ((padded, rows), F32),
            ((padded, rows), BF),
            ((padded, 128), F32),
            ((images, padded, rows), BF),
            ((rows, width), BF),
            ((images, padded, pix), BF),
        ],
        [
            vm((width, width), BF),
            vm((images, rows, width), BF),
            vm((128, wide), F32),
            vm((images, rows, width), BF),
            vm((images, rows, width), BF),
            vm((padded, width), BF),
            vm((padded, pix), F32),
            vm((16, width), F32),
            vm((images, padded, rows), BF),
            vm((images, padded, pix), BF),
            vm((images, padded, rows), F32),
            vm((channels, images, pix), BF),
            dma,
            dma((3,)),
        ],
        (
            latents,
            pix_rows,
            keep_mask,
            pix_gain,
            pix_shift,
            norm_gains,
            norm_shifts,
            proj_biases,
            w_key,
            w_query,
        ),
        "aahhhhhhha",
        "look",
        3 * unit + 2 * cross,
        "vvvaaa",
    )
    tiles = call(
        functools.partial(join_one_body, channels),
        [((padded, lanes), BF)] * chips,
        [vm((padded, rows), BF)],
        (keep, swapped(send)),
        "vv",
        "join_one",
        1,
    )
    (tile,) = call(
        functools.partial(join_two_body, channels),
        [((padded, lanes), BF)],
        [vm((chips, padded, lanes), BF), dma((chips,))],
        (tiles[0], *around(tiles[1:])),
        "n" * chips,
        "join_two",
        1,
    )
    tiles = [tile] + around([tile] * (chips - 1))
    output, d_after, own_pack, small_grads, keep, send = trunk(
        tiles,
        latents,
        cotangent,
        norm_gains,
        norm_shifts,
        proj_biases,
        w_value,
        kv_bias[None],
        [w_out, w_first, w_second, w_qkv, w_self_out, w_third, w_fourth],
        channels,
        padded,
    )
    got_pack, send = lax.optimization_barrier((swapped(own_pack), send))
    got_send = swapped(send)
    both_keep = keep
    keep, send, both, score_grad, weights_low = call(
        functools.partial(back_one_body, channels),
        [
            ((padded, rows), F32),
            ((padded, rows), BF),
            ((images, padded, rows), BF),
            ((images, pix, rows), BF),
            ((images, pix, rows), BF),
        ],
        [
            vm((images, padded, rows), BF),
            vm((images, padded, rows), BF),
            vm((images, padded, pix), BF),
            vm((images, padded, rows), F32),
            dma((4,)),
        ],
        (own_pack, got_pack, query_pix, pix_normed),
        "anaa",
        "back_one",
        3 * cross,
    )
    keep, send, got_send = lax.optimization_barrier((keep, send, got_send))
    quarter = both_keep.shape[0] // 4
    adds = [vm((2, quarter, 128), BF), vm((2, quarter, 128), BF), dma((2, 2))]
    one, two = call(
        first_add_body,
        [((quarter, 128), BF)] * 2,
        adds,
        (both_keep, got_send),
        "an",
        "first_add",
        1,
    )
    got_output = swapped(output)
    tiles = call(
        back_join_one_body,
        [((padded, lanes), BF)] * chips,
        [vm((padded, rows), BF)],
        (keep, swapped(send)),
        "vv",
        "back_join_one",
        1,
    )
    tiles, score_grad, one, two = lax.optimization_barrier((tiles, score_grad, one, two))
    one, two = lax.ppermute(one, "img", LOW_PAIRS), lax.ppermute(two, "img", HIGH_PAIRS)
    d_pixels, sums, both_outputs = call(
        functools.partial(back_two_body, channels),
        [((channels, images, pix), F32), ((8, wide), F32), ((images, rows, width), BF)],
        [
            vm((padded, pix), F32),
            vm((wide, 128), F32),
            vm((images, padded, rows), BF),
            dma((3,)),
        ],
        (score_grad, weights_low, query_pix, both, pix_rows, par, output, got_output),
        "vvavhhan",
        "back_two",
        2 * cross,
    )
    (tile,) = call(
        functools.partial(back_join_two_body, channels),
        [((padded, lanes), BF)],
        [vm((chips, padded, lanes), BF), dma((chips,))],
        (tiles[0], *around(tiles[1:]), sums),
        "n" * chips + "v",
        "back_join_two",
        1,
    )
    tile, one, two = lax.optimization_barrier((tile, one, two))

    one, two = image_second(
        *call(
            second_add_body,
            [((quarter, 128), BF)] * 2,
            adds,
            (both_keep, got_send, one, two),
            "anvv",
            "second_add",
            1,
        )
    )
    tiles = [tile] + around([tile] * (chips - 1))
    last_rows = width + padded + 32 + 16
    d_lat, d_lat_low, keep, send = call(
        functools.partial(tail_body, channels),
        [
            ((rows, width), F32),
            ((rows, width), BF),
            ((last_rows, 128), BF),
            ((last_rows, 128), BF),
        ],
        [
            vm((rows, width), BF),
            vm((width, width), BF),
            vm((rows, width), F32),
            vm((padded, rows), BF),
            vm((padded, width), BF),
            vm((16, width), F32),
            vm((rows, width), BF),
            vm((rows, width), BF),
            vm((rows, width), F32),
            vm((2, rows, 128), F32),
            vm((2, 8, width), F32),
            vm((32, width), F32),
            dma,
            dma,
            dma,
            dma((chips,)),
        ],
        (
            *tiles,
            latents,
            w_query,
            d_after,
            query,
            w_key,
            norm_gains,
            norm_shifts,
            small_grads,
        ),
        "n" * chips + "aanhhhhh",
        "tail",
        3 * unit,
    )
    keep, send, d_lat_low, one, two = lax.optimization_barrier((keep, send, d_lat_low, one, two))
    got_one, got_two = image_third(one, two)
    part = last_rows // 4
    got_lat = swapped(d_lat_low)

    def partners(tiles):
        return [
            lax.ppermute(t, "img", [(i, i ^ (step + 1)) for i in range(4)])
            for step, t in enumerate(tiles)
        ]

    tiles = call(
        last_add_body,
        [((part, 128), BF)] * 4,
        [],
        (keep, swapped(send)),
        "vv",
        "last_add",
        1,
    )
    tiles, got_lat = lax.optimization_barrier((tiles, got_lat))
    arrived = partners(tiles[1:])
    square = (width, 128)
    first, pieces, shapes = 0, [], []
    for across in (1, 1, 1, 3, 1, 1, 1):
        pieces.append((first, width, across))
        shapes.append((width, 128 * across))
        first += width * across
    pieces += [(first, padded, 1), (first + channels, 1, 1)]
    shapes += [(channels, 128), (1, 128)]
    main = call(
        functools.partial(unpack_main_body, pieces),
        [(s, F32) for s in shapes],
        [vm((4 * one.shape[0], 128), BF), vm((32, 128), F32), dma((4,))],
        (one, two, got_one, got_two),
        "nnnn",
        "unpack_main",
        1,
    )
    d_pixels = jnp.transpose(d_pixels, (1, 2, 0))
    (both_latents,) = call(
        latents_body,
        [((images, rows, width), F32)],
        [],
        (d_lat, got_lat),
        "vv",
        "latents",
        1,
    )
    arrived, both_latents, d_pixels = lax.optimization_barrier((arrived, both_latents, d_pixels))
    (tile,) = call(
        last_sum_body,
        [((part, 128), BF)],
        [vm((4, part, 128), BF), dma((4,))],
        (tiles[0], *arrived),
        "nnnn",
        "last_sum",
        1,
    )
    parts = partners([tile] * 3)
    parts, main = lax.optimization_barrier((parts, main))
    at = width + padded
    rest = call(
        functools.partial(
            unpack_last_body,
            [
                (0, width, 1),
                (width, padded, 1),
                (at, 4, 1),
                (at + 4, 4, 1),
                (at + 8, 9, 1),
                (at + 32, 1, 3),
                (at + 35, 1, 3),
            ],
        ),
        [
            (s, F32)
            for s in (square, (channels, 128), (4, 128), (4, 128), (9, 128), (1, 384), (1, 384))
        ],
        [vm((last_rows, 128), BF), vm((32, 128), F32), dma((4,))],
        (tile, *parts),
        "nnnn",
        "unpack_last",
        1,
    )
    return (
        both_outputs,
        both_latents,
        d_pixels,
        rest[0],
        rest[1],
        main[7],
        main[8][0],
        main[6],
        main[5],
        main[4],
        main[3],
        main[2],
        main[1],
        main[0],
        rest[2],
        rest[3],
        rest[4],
        rest[5][0, :channels],
        rest[6][0, :channels],
    )


def on_device(*args):
    rows, width = args[0].shape[1:]
    chips = lax.axis_size("chip")
    if (width // chips) % 256 == 0 and width // chips == 256 and (rows // chips) % 128 == 0:
        return on_device_fast(*args)
    return on_device_slow(*args)


def solution(mesh):
    images, pieces = mesh.devices.shape
    split = Mesh(mesh.devices.reshape(images, pieces // 2, 2), ("img", "chip", "core"))
    latent = P("img", None, None)
    weight = P(None, PIX)
    placed = (latent, P("img", PIX, None), P("img", PIX), latent) + (P(),) * 16
    return jax.shard_map(
        on_device,
        mesh=split,
        in_specs=placed,
        out_specs=(latent, latent, P("img", PIX, None), weight, weight, weight, P(PIX))
        + (weight,) * 10
        + (P(), P()),
        check_vma=False,
    )
```

```python
import functools

import jax
import jax.numpy as jnp
from jax import lax
from jax.experimental import pallas as pl
from jax.experimental.pallas import tpu as pltpu
from jax.sharding import Mesh
from jax.sharding import PartitionSpec as P

HEADS = 8
EPSILON = 1e-05
LOG_TWO = 0.6931471805599453
FLOOR_VALUE = -1e30
BF = jnp.bfloat16
F32 = jnp.float32
SWAP = [(0, 1), (1, 0)]
PIX = ("chip", "core")


def dot(a, b, ca, cb):
    return lax.dot_general(a, b, (((ca,), (cb,)), ((), ())), preferred_element_type=F32)


def layer_norm(values, norm_gain, norm_shift):
    centre = values - jnp.mean(values, axis=-1, keepdims=True)
    inverse = lax.rsqrt(jnp.mean(centre * centre, axis=-1, keepdims=True) + EPSILON)
    unit_rows = centre * inverse
    return (unit_rows * norm_gain + norm_shift, unit_rows, inverse)


def row_total(values):
    return jnp.sum(values, axis=tuple(range(values.ndim - 1)))


def norm_back(grad, unit_rows, inverse, norm_gain):
    scaled = grad * norm_gain
    d_values = inverse * (
        scaled
        - jnp.mean(scaled, axis=-1, keepdims=True)
        - unit_rows * jnp.mean(scaled * unit_rows, axis=-1, keepdims=True)
    )
    return (d_values, row_total(grad * unit_rows), row_total(grad))


def gelu_exact(values):
    return jax.nn.gelu(values, approximate=False)


def three_parts(values):
    high = values.astype(BF).astype(F32)
    rest = values - high
    middle = rest.astype(BF).astype(F32)
    return (high, middle, rest - middle)


ROOT_HALF = 0.7071067811865476
ROOT_TWO_PI = 0.3989422804014327


def trunk_core(
    channels,
    span,
    qkv_span,
    chip_start,
    qkv_start,
    flip,
    waits,
    lat,
    mean,
    stats,
    cot,
    gains,
    shifts,
    biases,
    result,
    d_after,
    pack,
    small,
    keep_h,
    send_h,
    wv,
    wo,
    w1,
    w2,
    wq,
    ws,
    w3,
    w4,
    att,
    dg1,
    h1,
    x2,
    qkv,
    wl,
    inv_total,
    sl,
    x3,
    dg4,
    h4,
    acc,
    low,
    low_two,
    normed,
    stat,
    sums,
    stage,
    spare_sem,
    store_sem,
):
    rows, width = lat.shape
    head_dim = width // HEADS
    head_scale = head_dim ** (-0.5)
    x1 = d_after
    def over_rows(step, most=512):
        block = min(most, rows)
        if block == rows:
            step(pl.ds(0, rows))
            return

        def run(i, carry):
            step(pl.ds(pl.multiple_of(i * block, block), block))
            return carry

        lax.fori_loop(0, rows // block, run, 0)

    def vector(ref, i):
        return ref[i : i + 1, :].astype(F32)

    def add_sum(at, value):
        sums[at] += jnp.sum(value.reshape(-1, 8, width), axis=0)

    def clear(*ats):
        for at in ats:
            sums[at] = jnp.zeros((8, width), F32)

    def flush(at, row):
        small[row : row + 1, :] = jnp.sum(sums[at], axis=0, keepdims=True)

    def norm_forward(x, i):
        g, s = vector(gains, i), vector(shifts, i)

        def step(at):
            v = x[at, :]
            m = jnp.mean(v, axis=1, keepdims=True)
            c = v - m
            iv = lax.rsqrt(jnp.mean(c * c, axis=1, keepdims=True) + EPSILON)
            normed[at, :] = (c * iv * g + s).astype(BF)
            stat[i - 1, 0, at, :] = jnp.broadcast_to(m, (m.shape[0], 128))
            stat[i - 1, 1, at, :] = jnp.broadcast_to(iv, (m.shape[0], 128))

        over_rows(step)

    def norm_again(x, i):
        g, s = vector(gains, i), vector(shifts, i)

        def step(at):
            m, iv = stat[i - 1, 0, at, 0:1], stat[i - 1, 1, at, 0:1]
            normed[at, :] = ((x[at, :] - m) * iv * g + s).astype(BF)

        over_rows(step)

    def norm_backward(x, skip, i, gain_row, shift_row, bias_row):
        g = vector(gains, i)
        clear(0, 1, 2)

        def step(at):
            m, iv = stat[i - 1, 0, at, 0:1], stat[i - 1, 1, at, 0:1]
            unit = (x[at, :] - m) * iv
            grad = acc[at, :]
            scaled = grad * g
            mean_one = jnp.mean(scaled, axis=1, keepdims=True)
            mean_two = jnp.mean(scaled * unit, axis=1, keepdims=True)
            total = skip[at, :].astype(F32) + iv * (scaled - mean_one - unit * mean_two)
            add_sum(0, grad * unit)
            add_sum(1, grad)
            add_sum(2, total)
            x[at, :] = total
            low_two[at, :] = total.astype(BF)

        over_rows(step)
        flush(0, gain_row)
        flush(1, shift_row)
        flush(2, bias_row)

    def hidden(bias_row, h, dg):
        b = vector(biases, bias_row)

        def step(at):
            v = acc[at, :] + b
            cdf = 0.5 * (1.0 + lax.erf(v * ROOT_HALF))
            h[at, :] = (v * cdf).astype(BF)
            dg[at, :] = cdf + v * (jnp.exp(-0.5 * v * v) * ROOT_TWO_PI)

        over_rows(step)

    def hidden_back(dg, bias_row):
        clear(0)

        def step(at):
            d = acc[at, :] * dg[at, :]
            add_sum(0, d)
            low[at, :] = d.astype(BF)

        over_rows(step)
        flush(0, bias_row)

    pending = [[], []]
    state = {"slot": 0, "row": 0}

    def emit(x, dy, start, span, ca, beside=None):
        count = x.shape[1 - ca]
        half = span // 2
        for t in range(half // 128):
            slot = state["slot"]
            state["slot"] = 1 - slot
            for waiting in pending[slot]:
                waiting.wait()
            pending[slot] = []
            mine = dy[:, pl.ds(pl.multiple_of(start + flip * half + t * 128, 128), 128)]
            other = dy[:, pl.ds(pl.multiple_of(start + (1 - flip) * half + t * 128, 128), 128)]
            both = jnp.concatenate([mine, other], axis=1)
            stage[slot, :count, :] = dot(x[...], both, ca, 0).astype(BF)
            if beside is not None and t == half // 128 - 1:
                beside()
            target = pl.ds(state["row"] + t * count, count)
            for side, out in enumerate((keep_h, send_h)):
                src = stage.at[slot, pl.ds(0, count), pl.ds(side * 128, 128)]
                copy = pltpu.make_async_copy(src, out.at[target, :], store_sem.at[slot, side])
                copy.start()
                pending[slot].append(copy)
        state["row"] += count * (half // 128)

    waits[0]()
    att[...] = dot(mean[...], wv[...], 0, 0).astype(BF)
    waits[1]()
    acc[...] = dot(att[...], wo[...], 1, 0)
    out_bias = vector(biases, 1)

    def after_cross(at):
        x1[at, :] = lat[at, :].astype(F32) + acc[at, :] + out_bias

    over_rows(after_cross)
    waits[9]()
    norm_forward(x1, 1)
    waits[2]()
    acc[...] = dot(normed[...], w1[...], 1, 0)
    hidden(2, h1, dg1)
    waits[3]()
    x2[...] = x1[...] + dot(h1[...], w2[...], 1, 0) + vector(biases, 3)
    norm_forward(x2, 2)
    waits[4]()
    qkv[:, :width] = (
        (dot(normed[...], wq[:, :width], 1, 0) + vector(biases, 4)) * head_scale
    ).astype(BF)
    qkv[:, width : 2 * width] = dot(normed[...], wq[:, width : 2 * width], 1, 0).astype(BF)
    qkv[:, 2 * width :] = (
        dot(normed[...], wq[:, 2 * width :], 1, 0) + vector(biases, 5)
    ).astype(BF)
    ones = jnp.ones((rows, head_dim), BF)

    def head_at(h, part):
        return pl.ds(pl.multiple_of(h * head_dim + part * width, head_dim), head_dim)

    def head_forward(h, carry):
        scores = dot(qkv[:, head_at(h, 0)], qkv[:, head_at(h, 1)], 1, 1)
        top = jnp.max(scores, axis=1, keepdims=True)
        shift = LOG_TWO * jnp.floor(top / LOG_TWO)
        weights = jnp.exp(scores - shift).astype(BF)
        wl[h] = weights
        value = jnp.concatenate([qkv[:, head_at(h, 2)], ones], axis=1)
        both = dot(weights, value, 1, 0)
        over = 1.0 / both[:, head_dim:]
        inv_total[:, head_at(h, 0)] = over
        sl[:, head_at(h, 0)] = (both[:, :head_dim] * over).astype(BF)
        return carry

    lax.fori_loop(0, HEADS, head_forward, 0, unroll=True)
    waits[5]()
    x3[...] = x2[...] + dot(sl[...], ws[...], 1, 0) + vector(biases, 6)
    norm_forward(x3, 3)
    waits[6]()
    acc[...] = dot(normed[...], w3[...], 1, 0)
    hidden(7, h4, dg4)
    waits[7]()
    low[...] = (x3[...] + dot(h4[...], w4[...], 1, 0) + vector(biases, 8)).astype(BF)
    result_copy = pltpu.make_async_copy(low, result, spare_sem)
    result_copy.start()

    waits[8]()
    clear(0)

    def cot_sum(at):
        add_sum(0, cot[at, :].astype(F32))

    over_rows(cot_sum)
    flush(0, 13)
    acc[...] = dot(cot[...], w4[...], 1, 1)
    result_copy.wait()
    emit(h4, cot, chip_start, span, 0, lambda: hidden_back(dg4, 12))
    acc[...] = dot(low[...], w3[...], 1, 1)
    emit(normed, low, chip_start, span, 0, lambda: norm_backward(x3, cot, 3, 2, 5, 11))
    acc[...] = dot(low_two[...], ws[...], 1, 1)
    clear(0, 1)

    def head_backward(h, carry):
        head = head_at(h, 0)
        query, keys, value = qkv[:, head], qkv[:, head_at(h, 1)], qkv[:, head_at(h, 2)]
        grad = acc[:, head] * inv_total[:, head]
        numer_grad = grad.astype(BF)
        total_part = (-(grad * sl[:, head].astype(F32))).astype(BF)
        weights = wl[h]
        d_weights = dot(
            jnp.concatenate([numer_grad, total_part], axis=1),
            jnp.concatenate([value, ones], axis=1),
            1,
            1,
        )
        score_grad = (d_weights * weights.astype(F32)).astype(BF)
        d_value = dot(weights, numer_grad, 0, 0)
        d_query = dot(score_grad, keys, 1, 0) * head_scale
        d_keys = dot(score_grad, query, 0, 0)
        qkv[:, head] = d_query.astype(BF)
        qkv[:, head_at(h, 1)] = d_keys.astype(BF)
        qkv[:, head_at(h, 2)] = d_value.astype(BF)
        sums[0, :, head] = jnp.sum(d_query.reshape(-1, 8, head_dim), axis=0)
        sums[1, :, head] = jnp.sum(d_value.reshape(-1, 8, head_dim), axis=0)
        return carry

    def heads_backward():
        lax.fori_loop(0, HEADS, head_backward, 0, unroll=True)

    emit(sl, low_two, chip_start, span, 0, heads_backward)
    flush(0, 9)
    flush(1, 10)
    norm_again(x2, 2)
    acc[...] = dot(qkv[...], wq[...], 1, 1)
    emit(normed, qkv, qkv_start, qkv_span, 0, lambda: norm_backward(x2, x3, 2, 1, 4, 8))
    acc[...] = dot(low_two[...], w2[...], 1, 1)

    def early_hidden():
        hidden_back(dg1, 7)
        norm_again(x1, 1)

    emit(h1, low_two, chip_start, span, 0, early_hidden)
    acc[...] = dot(low[...], w1[...], 1, 1)
    emit(normed, low, chip_start, span, 0, lambda: norm_backward(x1, x2, 1, 0, 3, 6))
    low[...] = dot(low_two[...], wo[...], 1, 1).astype(BF)
    emit(att, low_two, chip_start, span, 0)
    emit(mean, low, chip_start, span, 1)
    grad_pix = dot(wv[...], low[...], 1, 1)
    over = stats[0:1, :]
    row = lax.broadcasted_iota(jnp.int32, grad_pix.shape, 0)
    line = jnp.sum(jnp.where(row == channels, grad_pix, 0.0), axis=0, keepdims=True)
    line = (line - jnp.sum(grad_pix * mean[...].astype(F32), axis=0, keepdims=True)) * over
    high = line.astype(BF).astype(F32)
    packed = jnp.where(row < channels, grad_pix * over, 0.0)
    extras = [high, line - high, stats[1:2, :], stats[2:3, :], stats[3:4, :]]
    for at, extra in enumerate(extras):
        packed = jnp.where(row == channels + at, extra, packed)
    pack[...] = packed.astype(BF)
    for slot in range(2):
        for waiting in pending[slot]:
            waiting.wait()


def trunk_slow_body(channels, span, qkv_span, place, lat, mean, stats, cot, gains, shifts, biases, *refs):
    load_sem, store_sem = refs[-2:]
    loads = []
    for at in range(8):
        copy = pltpu.make_async_copy(refs[at], refs[14 + at], load_sem.at[at])
        copy.start()
        loads.append(copy.wait)
    loads += [lambda: None, lambda: None]
    trunk_core(
        channels, span, qkv_span, place[0], place[1], place[2], loads, lat, mean, stats, cot,
        gains, shifts, biases, *refs[8:-2], load_sem.at[0], store_sem
    )


def trunk_fast_body(channels, chips, *refs):
    tiles, refs = refs[:chips], refs[chips:]
    lat_h, cot_h, gains, shifts, biases, value, kv_bias = refs[:7]
    weights_h, refs = refs[7:14], refs[14:]
    lat, mean, raw, stats, tail, load_sem, store_sem = refs[-7:]
    cot = lat
    wv = refs[6]
    place = places()
    chip, core = place[0], place[1]
    tile_copies = [pltpu.make_async_copy(tiles[0], raw, load_sem.at[9])]
    tile_copies[0].start()
    loads = []
    pairs = [(lat_h.at[core], lat)]
    pairs += [(weights_h[at], refs[7 + at]) for at in range(7)]
    for at, (src, dst) in enumerate(pairs):
        copy = pltpu.make_async_copy(src, dst, load_sem.at[at])
        copy.start()
        loads.append(copy.wait)
    cot_copy = pltpu.make_async_copy(cot_h.at[core], cot, load_sem.at[8])
    loads += [cot_copy.wait, cot_copy.start]
    fill_rows(wv, value, tail, kv_bias[...].astype(F32))
    for copy in tile_copies:
        copy.wait()
    full = raw[...].astype(F32)
    mean[...] = jnp.where(row_of(full) <= channels, full, 0.0).astype(BF)
    total = (
        full[channels + 1 : channels + 2]
        + full[channels + 2 : channels + 3]
        + full[channels + 3 : channels + 4]
    )
    stats[0:1, :] = 1.0 / total
    for at in range(3):
        stats[at + 1 : at + 2, :] = full[channels + 4 + at : channels + 5 + at]
    trunk_core(
        channels, 256, 768, chip * 256, chip * 768, core, loads, lat, mean, stats, cot,
        gains, shifts, biases, *refs[:-7], load_sem.at[0], store_sem
    )


def trunk_scratch(rows, width, padded):
    big = pltpu.VMEM((rows, width), F32)
    half = pltpu.VMEM((rows, width), BF)
    square = pltpu.VMEM((width, width), BF)
    return [
        pltpu.VMEM((padded, width), BF),
        square,
        square,
        square,
        pltpu.VMEM((width, 3 * width), BF),
        square,
        square,
        square,
        half,
        big,
        half,
        big,
        pltpu.VMEM((rows, 3 * width), BF),
        pltpu.VMEM((HEADS, rows, rows), BF),
        big,
        half,
        big,
        big,
        half,
        big,
        half,
        half,
        half,
        pltpu.VMEM((3, 2, rows, 128), F32),
        pltpu.VMEM((3, 8, width), F32),
        pltpu.VMEM((2, width, 256), BF),
    ]


def trunk_outs(rows, width, padded, sent):
    return [
        ((rows, width), BF),
        ((rows, width), F32),
        ((padded, rows), BF),
        ((16, width), F32),
        ((sent, 128), BF),
        ((sent, 128), BF),
    ]


def trunk_slow(place, lat, mean, stats, cot, gains, shifts, biases, weights, channels, span, qkv_span):
    rows, width = lat.shape
    padded = mean.shape[0]
    sent = width * (6 * (span // 256) + qkv_span // 256) + padded * (span // 256)
    return call(
        functools.partial(trunk_slow_body, channels, span, qkv_span),
        trunk_outs(rows, width, padded, sent),
        trunk_scratch(rows, width, padded)
        + [pltpu.SemaphoreType.DMA((8,)), pltpu.SemaphoreType.DMA((2, 2))],
        (place, lat, mean, stats, cot, gains, shifts, biases, *weights),
        "s" + "v" * 7 + "n" * 8,
        "trunk",
        60 * rows * width * width,
        "avvvaa",
        58,
    )


def trunk(
    tiles, latents, cotangent, gains, shifts, biases, value, kv_bias, weights, channels, padded
):
    _, rows, width = latents.shape
    sent = -(-(9 * width + padded) // 64) * 64
    vm = pltpu.VMEM
    return call(
        functools.partial(trunk_fast_body, channels, len(tiles)),
        trunk_outs(rows, width, padded, sent),
        trunk_scratch(rows, width, padded)
        + [
            vm((rows, width), BF),
            vm((padded, rows), BF),
            vm((padded, rows), BF),
            vm((8, rows), F32),
            vm((16, width), F32),
            pltpu.SemaphoreType.DMA((9 + len(tiles),)),
            pltpu.SemaphoreType.DMA((2, 2)),
        ],
        (*tiles, latents, cotangent, gains, shifts, biases, value, kv_bias, *weights),
        "a" * len(tiles) + "aahhhhv" + "a" * 7,
        "trunk",
        60 * rows * width * width,
        "avvvaa",
        58,
    )


def shifted(devices, step):
    return [(i, (i + step) % devices) for i in range(devices)]


def exchange(tiles, axis):
    devices = tiles.shape[0]
    if devices == 1:
        return tiles
    place = lax.axis_index(axis)
    got = [lax.dynamic_index_in_dim(tiles, place, 0, keepdims=False)]
    for step in range(1, devices):
        tile = lax.dynamic_index_in_dim(tiles, (place + step) % devices, 0, keepdims=False)
        got.append(lax.ppermute(tile, axis, shifted(devices, step)))
    return jnp.stack(got)


def gather(tile, axis):
    devices = lax.axis_size(axis)
    place = lax.axis_index(axis)
    got = [tile]
    for step in range(1, devices):
        got.append(lax.ppermute(tile, axis, shifted(devices, step)))
    stacked = jnp.stack(got)
    order = (place - jnp.arange(devices)) % devices
    return jnp.stack([lax.dynamic_index_in_dim(stacked, order[i], 0, keepdims=False) for i in range(devices)])


def in_tiles(rows, devices):
    return jnp.moveaxis(rows.reshape(rows.shape[0], devices, -1), 1, 0)


def from_tiles(tiles):
    return jnp.moveaxis(tiles, 0, 1).reshape(tiles.shape[1], -1)


def image_parts(rows):
    count = rows.shape[0]
    quarter = -(-count // 64) * 16
    tiles = jnp.pad(rows, ((0, 4 * quarter - count), (0, 0))).reshape(4, quarter, -1)
    return tiles


LOW_PAIRS = [(0, 1), (1, 0), (2, 3), (3, 2)]
HIGH_PAIRS = [(0, 2), (2, 0), (1, 3), (3, 1)]


def pick(pair, at):
    return jnp.where(at == 0, pair[0], pair[1])


def plus(a, b):
    return (a.astype(F32) + b.astype(F32)).astype(BF)


def image_places():
    place = lax.axis_index("img")
    return place // 2, place % 2


def image_first(rows):
    high, low = image_places()
    tiles = image_parts(rows)
    one, two = tiles[:2], tiles[2:]
    got_one = lax.ppermute(pick(one, 1 - low), "img", LOW_PAIRS)
    got_two = lax.ppermute(pick(two, 1 - high), "img", HIGH_PAIRS)
    return plus(pick(one, low), got_one), plus(pick(two, high), got_two)


def image_second(one, two):
    got_one = lax.ppermute(one, "img", HIGH_PAIRS)
    got_two = lax.ppermute(two, "img", LOW_PAIRS)
    return plus(one, got_one), plus(two, got_two)


def image_third(one, two):
    return lax.ppermute(one, "img", LOW_PAIRS), lax.ppermute(two, "img", HIGH_PAIRS)


def image_whole(one, two, got_one, got_two, count):
    high, low = image_places()
    whole = jnp.concatenate(
        [
            jnp.where(low == 0, one, got_one),
            jnp.where(low == 0, got_one, one),
            jnp.where(high == 0, two, got_two),
            jnp.where(high == 0, got_two, two),
        ]
    )
    return whole[:count]


def image_sum(rows):
    one, two = image_second(*image_first(rows))
    return image_whole(one, two, *image_third(one, two), rows.shape[0])


def on_device_slow(
    latents,
    pixels,
    keep_mask,
    cotangent,
    w_query,
    w_key,
    w_value,
    kv_bias,
    w_out,
    w_first,
    w_second,
    w_qkv,
    w_self_out,
    w_third,
    w_fourth,
    norm_gains,
    norm_shifts,
    proj_biases,
    pix_gain,
    pix_shift,
):
    width = latents.shape[-1]
    rows = latents.shape[1]
    channels = pixels.shape[-1]
    padded = -(-(channels + 8) // 16) * 16
    cross_scale = width ** (-0.5)
    chips = lax.axis_size("chip")
    chip = lax.axis_index("chip")
    core = lax.axis_index("core")
    piece = width // (chips * 2)

    def columns(values):
        span = values.shape[-1] // chips
        return lax.dynamic_slice_in_dim(values, chip * span, span, values.ndim - 1)

    def mine(values):
        return lax.dynamic_index_in_dim(values, core, 0, keepdims=False)

    def other(values):
        return lax.dynamic_index_in_dim(values, 1 - core, 0, keepdims=False)

    def swapped(values):
        return lax.ppermute(values, "core", SWAP)

    gains = norm_gains.astype(F32)
    shifts = norm_shifts.astype(F32)
    biases = proj_biases.astype(F32)
    pixel_gain = pix_gain.astype(F32)
    pixel_shift = pix_shift.astype(F32)
    key_rows = jnp.pad(w_key, ((0, padded - channels), (0, 0)))
    value_rows = jnp.concatenate(
        [w_value, kv_bias[None], jnp.zeros((padded - channels - 1, width), BF)]
    )

    q_normed, _, _ = layer_norm(latents.astype(F32), gains[0], shifts[0])
    q_normed_low = q_normed.astype(BF)
    query = (
        (dot(q_normed_low.reshape(-1, width), w_query, 1, 0) + biases[0]) * cross_scale
    ).astype(BF)
    query_pix = jnp.stack(
        [dot(key_rows, query[:rows], 1, 1), dot(key_rows, query[rows:], 1, 1)]
    ).astype(BF)
    p_normed, p_unit, p_inverse = layer_norm(pixels.astype(F32), pixel_gain, pixel_shift)
    lane = jnp.arange(padded)
    ones_lanes = ((lane == channels) | (lane == channels + 1)).astype(BF)
    pix_low = jnp.pad(p_normed.astype(BF), ((0, 0), (0, 0), (0, padded - channels))) + ones_lanes
    kept_pixels = keep_mask[:, :, None] > 0
    scores = jnp.einsum("bpc,bci->bpi", pix_low, query_pix, preferred_element_type=F32)
    local_top = jnp.max(jnp.where(kept_pixels, scores, FLOOR_VALUE), axis=1)
    level = jnp.floor(local_top / LOG_TWO)
    first_weights = jnp.where(
        kept_pixels, jnp.exp(scores - (level * LOG_TWO)[:, None, :]), 0.0
    ).astype(BF)
    local_numer = jnp.einsum("bpc,bpi->bci", pix_low, first_weights, preferred_element_type=F32)

    def packed(body, extras):
        lead = jnp.concatenate([body] + [e[None, :] for e in extras]).astype(BF)
        return jnp.pad(lead, ((0, padded - lead.shape[0]), (0, 0)))

    def fwd_pack(numer, level):
        total = numer[channels]
        return packed(numer[:channels], three_parts(total)[:2] + three_parts(level))

    def fwd_unpack(pack):
        pack = pack.astype(F32)
        total = pack[channels] + pack[channels + 1]
        level = pack[channels + 2] + pack[channels + 3] + pack[channels + 4]
        return (jnp.concatenate([pack[:channels], total[None]]), level)

    def joined(parts):
        top = parts[0][1]
        for _, level in parts[1:]:
            top = jnp.maximum(top, level)
        return (sum(body * jnp.exp2(level - top)[None, :] for body, level in parts), top)

    sent = swapped(fwd_pack(other(local_numer), other(level)))
    body, top = joined([(mine(local_numer)[: channels + 1], mine(level)), fwd_unpack(sent)])
    got = exchange(in_tiles(fwd_pack(body, top), chips), "chip")
    body, top = joined([fwd_unpack(got[i]) for i in range(chips)])
    mean_tile = packed(
        body[:channels] / body[channels], three_parts(body[channels]) + three_parts(top)
    )
    mean_all = from_tiles(gather(mean_tile, "chip")).astype(F32)
    cross_total = mean_all[channels] + mean_all[channels + 1] + mean_all[channels + 2]
    cross_level = mean_all[channels + 3] + mean_all[channels + 4] + mean_all[channels + 5]
    row = jnp.arange(padded)[:, None]
    mean_pix = jnp.where(row < channels, mean_all, jnp.where(row == channels, 1.0, 0.0))
    mean_low = mean_pix.astype(BF)

    _, q_unit, q_inverse = layer_norm(mine(latents).astype(F32), gains[0], shifts[0])
    fast = piece % 128 == 0
    if fast:
        span, qkv_span = 2 * piece, 6 * piece
        starts = (chip * span, chip * qkv_span)
        flip = core
    else:
        span, qkv_span = 256, 256
        starts = tuple(
            jnp.minimum(chip * size // chips // 128 * 128, size - 256) for size in (width, 3 * width)
        )
        flip = 0 * core
    place = jnp.stack([starts[0], starts[1], flip]).astype(jnp.int32)
    stats = jnp.concatenate(
        [
            (1.0 / cross_total)[None],
            mean_all[channels + 3 : channels + 6],
            jnp.zeros((4, rows), F32),
        ]
    )
    output, d_after, own_pack, small_grads, keep, send = trunk_slow(
        place,
        mine(latents),
        mean_low,
        stats,
        mine(cotangent),
        norm_gains,
        norm_shifts,
        proj_biases,
        [value_rows, w_out, w_first, w_second, w_qkv, w_self_out, w_third, w_fourth],
        channels,
        span,
        qkv_span,
    )
    def flat(arrays):
        return jnp.concatenate(
            [a.reshape(a.shape[0], -1, piece).swapaxes(0, 1).reshape(-1, piece) for a in arrays]
        ).astype(BF)

    def split(grads):
        keep, send = [], []
        for g in grads:
            half = g.shape[-1] // 2
            keep.append(lax.dynamic_slice_in_dim(g, core * half, half, 1))
            send.append(lax.dynamic_slice_in_dim(g, (1 - core) * half, half, 1))
        return flat(keep), flat(send)

    squares = [(width, piece)] * 3
    spans = squares + [(width, 3 * piece)] + squares + [(padded, piece)]
    if not fast:
        blocks, at = [], 0
        for r, c in spans:
            size = c * chips * 2
            block = jnp.concatenate([keep[at : at + r], send[at : at + r]], axis=1)
            offset = chip * 2 * c - (starts[1] if size > width else starts[0])
            blocks.append(lax.dynamic_slice_in_dim(block, offset, 2 * c, 1))
            at += r
        keep, send = split(blocks)
    got_pack, got_send = lax.optimization_barrier((swapped(own_pack), swapped(send)))
    both_cores = plus(keep, got_send)
    got_pack, both_cores = lax.optimization_barrier((got_pack, both_cores))
    one, two = image_first(both_cores)
    both = jnp.where(core == 0, jnp.stack([own_pack, got_pack]), jnp.stack([got_pack, own_pack]))

    levels = jnp.sum(both[:, channels + 2 : channels + 5].astype(F32), axis=1)
    weights = jnp.where(kept_pixels, jnp.exp(scores - (levels * LOG_TWO)[:, None, :]), 0.0)
    grad_rows = jnp.where(row[None] < channels + 2, both, jnp.zeros((), BF))
    d_weights = jnp.einsum("bpc,bci->bpi", pix_low, grad_rows, preferred_element_type=F32)
    score_grad = (d_weights * weights).astype(BF)
    query_part = jnp.einsum("bpc,bpi->bci", pix_low, score_grad, preferred_element_type=F32)
    d_pix_normed = jnp.einsum(
        "bpi,bci->bpc", score_grad, query_pix, preferred_element_type=F32
    ) + jnp.einsum("bpi,bci->bpc", weights.astype(BF), grad_rows, preferred_element_type=F32)
    d_pix_normed = d_pix_normed[..., :channels]
    scaled = d_pix_normed * pixel_gain
    d_pixels = p_inverse * (
        scaled
        - jnp.mean(scaled, axis=-1, keepdims=True)
        - p_unit * jnp.mean(scaled * p_unit, axis=-1, keepdims=True)
    )
    pix_sums = jnp.stack(
        [jnp.sum(d_pix_normed * p_unit, axis=1), jnp.sum(d_pix_normed, axis=1)], axis=1
    )
    pix_sums = jnp.pad(pix_sums, ((0, 0), (0, 0), (0, rows - channels)))

    def bwd_pack(body, sums):
        high, low, _ = three_parts(sums)
        return packed(body[:channels], [high[0], low[0], high[1], low[1]])

    def bwd_unpack(pack):
        pack = pack.astype(F32)
        sums = jnp.stack(
            [pack[channels] + pack[channels + 1], pack[channels + 2] + pack[channels + 3]]
        )
        return (pack[:channels], sums)

    query_part, pix_sums, one, two = lax.optimization_barrier((query_part, pix_sums, one, two))
    one, two = image_second(one, two)
    sent = swapped(bwd_pack(other(query_part), other(pix_sums)))
    body_two, sums_two = bwd_unpack(sent)
    body, sums = (mine(query_part)[:channels] + body_two, mine(pix_sums) + sums_two)
    got = exchange(in_tiles(bwd_pack(body, sums), chips), "chip")
    got = [bwd_unpack(got[i]) for i in range(chips)]
    body, sums = (sum(g[0] for g in got), sum(g[1] for g in got))
    body, sums, one, two = lax.optimization_barrier((body, sums, one, two))
    got_one, got_two = image_third(one, two)
    all_parts = from_tiles(gather(bwd_pack(body, sums), "chip"))
    _, sums = bwd_unpack(all_parts)
    query_sum = jnp.where(row < channels, all_parts, jnp.zeros((), BF))

    d_query = dot(query_sum, key_rows, 0, 0) * cross_scale
    d_query_low = d_query.astype(BF)
    own_normed = mine(q_normed_low)
    own_query = lax.dynamic_slice_in_dim(query, core * rows, rows, 0)
    d_w_query = dot(own_normed, columns(d_query_low), 0, 0)
    d_w_key = dot(query_sum, columns(own_query), 1, 0)
    d_q_normed = dot(d_query_low, w_query, 1, 1)
    d_q_in, d_gain_zero, d_shift_zero = norm_back(d_q_normed, q_unit, q_inverse, gains[0])
    d_latents_own = d_after + d_q_in

    def two_images(own):
        got = swapped(own.astype(BF)).astype(own.dtype)
        return jnp.where(core == 0, jnp.stack([own, got]), jnp.stack([got, own]))

    def unpacked(whole, spans):
        outs, at = [], 0
        for r, c in spans:
            count = r * (c // piece)
            part = whole[at : at + count].reshape(c // piece, r, piece).swapaxes(0, 1).reshape(r, c)
            outs.append(part.astype(F32))
            at += count
        return outs

    def reduced(keep, send, spans):
        return unpacked(image_sum(plus(keep, swapped(send))), spans)

    small = jnp.concatenate(
        [
            d_gain_zero[None],
            small_grads[0:3],
            d_shift_zero[None],
            small_grads[3:6],
            row_total(d_query)[None],
            small_grads[6:14],
        ]
    )
    sum_lanes = -(-channels // piece) * piece
    pix_rows = sums[:, :sum_lanes].reshape(-1, piece)
    pix_rows = jnp.concatenate([pix_rows, pix_rows], axis=1)
    last_spans = [(width, piece), (padded, piece), (small.shape[0], piece), (pix_rows.shape[0], piece)]
    keep, send = split([d_w_query, d_w_key, columns(small), pix_rows])
    keep, send, got_one, got_two = lax.optimization_barrier((keep, send, got_one, got_two))
    last = reduced(keep, send, last_spans)
    main = unpacked(image_whole(one, two, got_one, got_two, both_cores.shape[0]), spans)
    d_small = last[2]
    pix_out = last[3].reshape(2, sum_lanes)
    return (
        two_images(output.astype(BF)),
        two_images(d_latents_own),
        d_pixels,
        last[0],
        last[1][:channels],
        main[7][:channels],
        main[7][channels],
        main[6],
        main[5],
        main[4],
        main[3],
        main[2],
        main[1],
        main[0],
        d_small[0:4],
        d_small[4:8],
        d_small[8:17],
        pix_out[0, :channels],
        pix_out[1, :channels],
    )


VMEM_MIB = {
    "look": 28,
    "join_one": 6,
    "join_two": 6,
    "gather": 6,
    "back_one": 20,
    "back_join_one": 6,
    "back_two": 24,
    "back_join_two": 6,
    "tail": 24,
    "last_add": 8,
    "first_add": 8,
    "second_add": 8,
    "last_sum": 6,
    "unpack_main": 24,
    "latents": 10,
    "unpack_last": 8,
}
LOWEST_LEVEL = -16777216.0


def row_of(value):
    return lax.broadcasted_iota(jnp.int32, value.shape, 0)


def with_rows(body, first, extras):
    row = row_of(body)
    for at, extra in enumerate(extras):
        body = jnp.where(row == first + at, extra, body)
    return body


def pack_sum(body, channels, level):
    total = body[channels : channels + 1]
    extras = three_parts(total)[:2] + three_parts(level)
    return with_rows(body, channels, extras).astype(BF)


def unpack_sum(pack, channels):
    pack = pack.astype(F32)
    total = pack[channels : channels + 1] + pack[channels + 1 : channels + 2]
    level = (
        pack[channels + 2 : channels + 3]
        + pack[channels + 3 : channels + 4]
        + pack[channels + 4 : channels + 5]
    )
    return with_rows(pack, channels, [total]), level


def join_sums(parts):
    top = parts[0][1]
    for _, level in parts[1:]:
        top = jnp.maximum(top, level)
    body = None
    for part, level in parts:
        scaled = part * jnp.exp2(level - top)
        body = scaled if body is None else body + scaled
    return body, top


def fill_rows(dst, src, tail, extra=None):
    count = src.shape[0]
    base = count // 16 * 16
    dst[:base, :] = src[:base, :]
    tail[...] = jnp.zeros_like(tail)
    tail[: count - base, :] = src[base:count, :].astype(F32)
    if extra is not None:
        tail[count - base : count - base + 1, :] = extra
    dst[base : base + 16, :] = tail[...].astype(BF)


def pixel_units(pix, image, xs, channels):
    xs[:channels, :] = pix[:, image, :].astype(F32)
    x = xs[...]
    inside = row_of(x) < channels
    mean = jnp.sum(x, axis=0, keepdims=True) * (1.0 / channels)
    c = jnp.where(inside, x - mean, 0.0)
    iv = lax.rsqrt(jnp.sum(c * c, axis=0, keepdims=True) * (1.0 / channels) + EPSILON)
    return c * iv, iv, inside


def look_body(
    channels,
    lat_h,
    pix_h,
    mask,
    pix_gain,
    pix_shift,
    gains,
    shifts,
    biases,
    wk_in,
    wq_h,
    keep,
    send,
    par,
    qp_h,
    q_h,
    pn_h,
    wq,
    held,
    turn,
    normed,
    qs,
    wk,
    xs,
    tail,
    qp_out,
    pn_out,
    bodies,
    pix,
    sem,
    out_sem,
):
    images, rows, width = lat_h.shape
    core = places()[1]
    lat_copies = [
        pltpu.make_async_copy(lat_h.at[image], held.at[image], out_sem.at[image])
        for image in range(images)
    ]
    for lat_copy in lat_copies:
        lat_copy.start()
    pix_copy = pltpu.make_async_copy(pix_h, pix, out_sem.at[2])
    pix_copy.start()
    copy = pltpu.make_async_copy(wq_h, wq, sem)
    copy.start()
    turn[...] = jnp.zeros_like(turn)
    turn[0:1, :channels] = pix_gain[...].astype(F32).reshape(1, channels)
    turn[1:2, :channels] = pix_shift[...].astype(F32).reshape(1, channels)
    par[...] = turn[...].T[: par.shape[0]]
    g, s = gains[0:1, :].astype(F32), shifts[0:1, :].astype(F32)

    fill_rows(wk, wk_in, tail)
    xs[...] = jnp.zeros_like(xs)
    for image in range(images):
        lat_copies[image].wait()
        v = held[image].astype(F32)
        c = v - jnp.mean(v, axis=1, keepdims=True)
        iv = lax.rsqrt(jnp.mean(c * c, axis=1, keepdims=True) + EPSILON)
        normed[image] = (c * iv * g + s).astype(BF)
    copy.wait()
    bias = biases[0:1, :].astype(F32)

    def per_image(image):
        qs[image] = ((dot(normed[image], wq[...], 1, 0) + bias) * width ** (-0.5)).astype(BF)
        scored = dot(wk[...], qs[image], 1, 1)
        qp_out[image] = with_rows(scored, channels + 2, [jnp.ones((1, rows), F32)]).astype(BF)
        unit, _, _ = pixel_units(pix, image, xs, channels)
        n = unit * par[:, 0:1] + par[:, 1:2]
        off = jnp.where(mask[pl.ds(image, 1), :] > 0, 0.0, FLOOR_VALUE)
        one = jnp.ones_like(off)
        pn_out[image] = with_rows(n, channels, [one, one, off]).astype(BF)
        scores = dot(pn_out[image], qp_out[image], 0, 0)
        top = jnp.max(scores, axis=0, keepdims=True)
        level = jnp.maximum(jnp.floor(top / LOG_TWO), LOWEST_LEVEL)
        weights = jnp.exp(scores - level * LOG_TWO).astype(BF)
        body = dot(pn_out[image], weights, 1, 0)
        bodies[image] = with_rows(body, channels + 1, [level])

    pix_copy.wait()
    for image in range(images):
        per_image(image)
    keep[...] = bodies[core]
    other = bodies[1 - core]
    send[...] = pack_sum(other, channels, other[channels + 1 : channels + 2])
    copies = [
        pltpu.make_async_copy(qs.at[core], q_h, out_sem.at[0]),
        pltpu.make_async_copy(qp_out, qp_h, out_sem.at[1]),
        pltpu.make_async_copy(pn_out, pn_h, out_sem.at[2]),
    ]
    for out in copies:
        out.start()
    for out in copies:
        out.wait()


def tiles_out(place, whole, outs):
    chips = len(outs)
    lanes = outs[0].shape[1]
    for step in range(chips):
        at = lax.rem(place[0] + step, chips)
        outs[step][...] = whole[:, pl.ds(pl.multiple_of(at * lanes, lanes), lanes)]


def tiles_in(place, whole, tiles, sem):
    chips = len(tiles)
    lanes = tiles[0].shape[1]
    copies = []
    for step in range(chips):
        at = lax.rem(place[0] + chips - step, chips)
        target = whole.at[:, pl.ds(pl.multiple_of(at * lanes, lanes), lanes)]
        copies.append(pltpu.make_async_copy(tiles[step], target, sem.at[step]))
        copies[-1].start()
    return copies


def places():
    return lax.axis_index("chip"), lax.axis_index("core"), lax.axis_index("img")


def join_one_body(channels, keep, got, *refs):
    outs, whole = refs[:-1], refs[-1]
    place = places()
    own = keep[...]
    body, top = join_sums(
        [(own, own[channels + 1 : channels + 2]), unpack_sum(got[...], channels)]
    )
    whole[...] = pack_sum(body, channels, top)
    tiles_out(place, whole, outs)


def load_all(tiles, held, sem):
    copies = [
        pltpu.make_async_copy(tile, held.at[at], sem.at[at]) for at, tile in enumerate(tiles)
    ]
    for copy in copies:
        copy.start()
    for copy in copies:
        copy.wait()
    return [held[at] for at in range(len(tiles))]


def join_two_body(channels, *refs):
    tiles, out, held, sem = refs[:-3], refs[-3], refs[-2], refs[-1]
    body, top = join_sums([unpack_sum(t, channels) for t in load_all(tiles, held, sem)])
    total = body[channels : channels + 1]
    extras = (jnp.ones_like(total),) + three_parts(total) + three_parts(top)
    out[...] = with_rows(body / total, channels, extras).astype(BF)


def gather_body(*refs):
    tiles, whole, sem = refs[:-2], refs[-2], refs[-1]
    for copy in tiles_in(places(), whole, tiles, sem):
        copy.wait()


def back_one_body(
    channels, own, got, qp_h, pn_h, keep, send, both, score_grad, weights_low, pair, qp_in, pn, bodies, sem
):
    images, padded, rows = qp_in.shape
    core = places()[1]
    pairs = [(pn_h, pn), (qp_h, qp_in), (own, pair.at[core]), (got, pair.at[1 - core])]
    copies = [pltpu.make_async_copy(s, d, sem.at[at]) for at, (s, d) in enumerate(pairs)]
    for copy in copies:
        copy.start()
    for copy in copies:
        copy.wait()

    def per_image(image):
        pack = pair[image].astype(F32)
        level = (
            pack[channels + 2 : channels + 3]
            + pack[channels + 3 : channels + 4]
            + pack[channels + 4 : channels + 5]
        )
        grads = jnp.where(row_of(pack) < channels + 2, pack, 0.0).astype(BF)
        both[image] = grads
        scores = dot(pn[image], qp_in[image], 0, 0)
        weights = jnp.exp(scores - level * LOG_TWO)
        weights_low[image] = weights.astype(BF)
        score_grad[image] = (dot(pn[image], grads, 0, 0) * weights).astype(BF)
        bodies[image] = dot(pn[image], score_grad[image], 1, 0)

    for image in range(images):
        per_image(image)
    keep[...] = bodies[core]
    send[...] = bodies[1 - core].astype(BF)


def back_join_one_body(keep, got, *refs):
    outs, whole = refs[:-1], refs[-1]
    place = places()
    whole[...] = (keep[...] + got[...].astype(F32)).astype(BF)
    tiles_out(place, whole, outs)


def back_two_body(
    channels, score_grad, weights_low, qp_h, both, pix, par, out_own, out_got,
    d_pix, sums, out_both, xs, turn, qp, sem
):
    images = pix.shape[1]
    padded = qp.shape[1]
    core = places()[1]
    pairs = [(qp_h, qp), (out_own, out_both.at[core]), (out_got, out_both.at[1 - core])]
    copies = [pltpu.make_async_copy(s, d, sem.at[at]) for at, (s, d) in enumerate(pairs)]
    for copy in copies:
        copy.start()
    copies[0].wait()
    xs[...] = jnp.zeros_like(xs)

    def per_image(image, carry):
        dn = dot(qp[image], score_grad[image], 1, 1) + dot(both[image], weights_low[image], 1, 1)
        unit, iv, inside = pixel_units(pix, image, xs, channels)
        grad = jnp.where(inside, dn, 0.0)
        scaled = grad * par[:, 0:1]
        one = jnp.sum(scaled, axis=0, keepdims=True) * (1.0 / channels)
        two = jnp.sum(scaled * unit, axis=0, keepdims=True) * (1.0 / channels)
        d_pix[:, image, :] = (iv * (scaled - one - unit * two))[:channels]
        d_gain = jnp.sum(grad * unit, axis=1, keepdims=True)
        d_shift = jnp.sum(grad, axis=1, keepdims=True)
        return carry[0] + d_gain, carry[1] + d_shift

    zero = jnp.zeros((padded, 1), F32)
    d_gain, d_shift = zero, zero
    for image in range(images):
        d_gain, d_shift = per_image(image, (d_gain, d_shift))
    turn[...] = jnp.zeros_like(turn)
    lane = lax.broadcasted_iota(jnp.int32, (padded, 128), 1)
    turn[:padded, :] = jnp.where(lane == 0, d_gain, jnp.where(lane == 1, d_shift, 0.0))
    sums[...] = turn[...].T[:8]
    copies[1].wait()
    copies[2].wait()


def back_join_two_body(channels, *refs):
    tiles, (sums, out, held, sem) = refs[:-4], refs[-4:]
    body = None
    for tile in load_all(tiles, held, sem):
        body = tile.astype(F32) if body is None else body + tile.astype(F32)
    lanes = out.shape[1]
    count = sums.shape[1] // lanes
    extras = [sums[r : r + 1, j * lanes : (j + 1) * lanes] for r in range(2) for j in range(count)]
    out[...] = with_rows(body, channels, extras).astype(BF)


def tail_body(channels, *refs):
    chips = len(refs) - 28
    place = places()
    tiles = refs[:chips]
    (
        lat_h,
        wq_h,
        d_after_h,
        query,
        wk_in,
        gains,
        shifts,
        small_in,
        d_lat,
        d_lat_low,
        keep,
        send,
        lat,
        wq,
        d_after,
        part,
        wk,
        tail,
        normed,
        low,
        acc,
        stat,
        sums,
        small,
        lat_sem,
        wq_sem,
        after_sem,
        tile_sem,
    ) = refs[chips:]
    rows, width = query.shape
    padded = part.shape[0]
    chip, core = place[0], place[1]
    copies = [
        pltpu.make_async_copy(lat_h.at[core], lat, lat_sem),
        pltpu.make_async_copy(wq_h, wq, wq_sem),
        pltpu.make_async_copy(d_after_h, d_after, after_sem),
    ]
    tile_copies = tiles_in(place, part, tiles, tile_sem)
    for copy in copies:
        copy.start()
    fill_rows(wk, wk_in, tail)
    for copy in tile_copies:
        copy.wait()
    base = channels // 16 * 16
    tail[:, :rows] = part[base : base + 16, :].astype(F32)
    extra_rows = tail[channels - base : channels - base + 6, :rows]
    lanes = tiles[0].shape[1]
    pix_rows = extra_rows[:, :lanes]
    for at in range(1, chips):
        pix_rows = pix_rows + extra_rows[:, at * lanes : (at + 1) * lanes]
    part_value = part[...]
    clean = jnp.where(row_of(part_value) < channels, part_value.astype(F32), 0.0).astype(BF)
    part[...] = clean
    d_query = dot(part[...], wk[...], 0, 0) * width ** (-0.5)
    low[...] = d_query.astype(BF)
    bias_row = jnp.sum(jnp.sum(d_query.reshape(-1, 8, width), axis=0), axis=0, keepdims=True)
    copies[0].wait()
    g, s = gains[0:1, :].astype(F32), shifts[0:1, :].astype(F32)

    v = lat[...].astype(F32)
    m = jnp.mean(v, axis=1, keepdims=True)
    c = v - m
    iv = lax.rsqrt(jnp.mean(c * c, axis=1, keepdims=True) + EPSILON)
    normed[...] = (c * iv * g + s).astype(BF)
    stat[0] = jnp.broadcast_to(m, (rows, 128))
    stat[1] = jnp.broadcast_to(iv, (rows, 128))

    def put(first, value):
        count = value.shape[0]

        @pl.when(core == 0)
        def _():
            keep[first : first + count, :] = value[:, :128]
            send[first : first + count, :] = value[:, 128:]

        @pl.when(core != 0)
        def _():
            send[first : first + count, :] = value[:, :128]
            keep[first : first + count, :] = value[:, 128:]

    cols = pl.ds(pl.multiple_of(chip * 256, 256), 256)
    put(0, dot(normed[...], low[:, cols], 0, 0).astype(BF))
    put(width, dot(part[...], query[:, cols], 1, 0).astype(BF))
    copies[1].wait()
    acc[...] = dot(low[...], wq[...], 1, 1)
    copies[2].wait()

    m, iv = stat[0, :, 0:1], stat[1, :, 0:1]
    unit = (lat[...].astype(F32) - m) * iv
    grad = acc[...]
    scaled = grad * g
    first_mean = jnp.mean(scaled, axis=1, keepdims=True)
    second_mean = jnp.mean(scaled * unit, axis=1, keepdims=True)
    total = d_after[...] + iv * (scaled - first_mean - unit * second_mean)
    d_lat[...] = total
    d_lat_low[...] = total.astype(BF)
    sums[0] = jnp.sum((grad * unit).reshape(-1, 8, width), axis=0)
    sums[1] = jnp.sum(grad.reshape(-1, 8, width), axis=0)
    small[...] = jnp.zeros_like(small)
    small[0:1, :] = jnp.sum(sums[0], axis=0, keepdims=True)
    small[1:4, :] = small_in[0:3, :]
    small[4:5, :] = jnp.sum(sums[1], axis=0, keepdims=True)
    small[5:8, :] = small_in[3:6, :]
    small[8:9, :] = bias_row
    small[9:17, :] = small_in[6:14, :]
    put(width + padded, small[:, cols].astype(BF))
    tail[...] = jnp.zeros_like(tail)
    tail[0:6, :lanes] = pix_rows
    spread = tail[:, :128].astype(BF)
    first = width + padded + small.shape[0]
    keep[first : first + 16, :] = spread
    send[first : first + 16, :] = spread


def first_add_body(keep_h, got_h, one, two, keep, got, sem):
    img = places()[2]
    quarter = one.shape[0]
    spots = [1 - lax.rem(img, 2), 3 - lax.div(img, 2)]
    copies = []
    for at, spot in enumerate(spots):
        source = pl.ds(pl.multiple_of(spot * quarter, 16), quarter)
        copies.append(pltpu.make_async_copy(keep_h.at[source, :], keep.at[at], sem.at[at, 0]))
        copies.append(pltpu.make_async_copy(got_h.at[source, :], got.at[at], sem.at[at, 1]))
    for copy in copies:
        copy.start()
    for at, out in enumerate((one, two)):
        copies[2 * at].wait()
        copies[2 * at + 1].wait()
        out[...] = (keep[at].astype(F32) + got[at].astype(F32)).astype(BF)


def second_add_body(keep_h, got_h, more_one, more_two, one, two, keep, got, sem):
    img = places()[2]
    quarter = one.shape[0]
    spots = [lax.rem(img, 2), 2 + lax.div(img, 2)]
    copies = []
    for at, spot in enumerate(spots):
        source = pl.ds(pl.multiple_of(spot * quarter, 16), quarter)
        copies.append(pltpu.make_async_copy(keep_h.at[source, :], keep.at[at], sem.at[at, 0]))
        copies.append(pltpu.make_async_copy(got_h.at[source, :], got.at[at], sem.at[at, 1]))
    for copy in copies:
        copy.start()
    for at, (more, out) in enumerate(((more_one, one), (more_two, two))):
        copies[2 * at].wait()
        copies[2 * at + 1].wait()
        total = keep[at].astype(F32) + got[at].astype(F32) + more[...].astype(F32)
        out[...] = total.astype(BF)


def last_add_body(keep, got, *outs):
    img = places()[2]
    part = outs[0].shape[0]
    for step, out in enumerate(outs):
        at = pl.ds(pl.multiple_of((img ^ step) * part, 16), part)
        out[...] = (keep[at, :].astype(F32) + got[at, :].astype(F32)).astype(BF)


def last_sum_body(*refs):
    tiles, (out, held, sem) = refs[:-3], refs[-3:]
    body = None
    for tile in load_all(tiles, held, sem):
        body = tile.astype(F32) if body is None else body + tile.astype(F32)
    out[...] = body.astype(BF)


def give(outs, pieces, whole, some):
    for out, (first, count, across) in zip(outs, pieces):
        for j in range(across):
            at = first + j * count
            rows = out.shape[0]
            if len(out.shape) == 1:
                base = min(first // 16 * 16, whole.shape[0] - 32)
                some[...] = whole[base : base + 32, :].astype(F32)
                at = first - base
                row = jnp.concatenate([some[at + k : at + k + 1, :] for k in range(3)], axis=1)
                out[...] = row.reshape(384)[:rows]
            elif rows > 16:
                out[:, j * 128 : (j + 1) * 128] = whole[at : at + rows, :].astype(F32)
            else:
                base = min(at // 16 * 16, whole.shape[0] - 32)
                some[...] = whole[base : base + 32, :].astype(F32)
                out[:, j * 128 : (j + 1) * 128] = some[at - base : at - base + rows, :]


def fetch(parts, spots, whole, sem):
    part = parts[0].shape[0]
    copies = []
    for at, spot in enumerate(spots):
        target = whole.at[pl.ds(pl.multiple_of(spot * part, 16), part), :]
        copies.append(pltpu.make_async_copy(parts[at], target, sem.at[at]))
        copies[-1].start()
    for copy in copies:
        copy.wait()


def unpack_last_body(pieces, *refs):
    parts, outs, (whole, some, sem) = refs[:4], refs[4:-3], refs[-3:]
    img = places()[2]
    fetch(parts, [img ^ step for step in range(4)], whole, sem)
    give(outs, pieces, whole, some)


def latents_body(own, got, both):
    core = places()[1]
    both[core] = own[...]
    both[1 - core] = got[...].astype(F32)


def unpack_main_body(pieces, *refs):
    parts, outs, (whole, some, sem) = refs[:4], refs[4:-3], refs[-3:]
    img = places()[2]
    high, low = lax.div(img, 2), lax.rem(img, 2)
    fetch(parts, [low, 2 + high, 1 - low, 3 - high], whole, sem)
    give(outs, pieces, whole, some)


def call(body, outs, scratch, args, spaces, name, flops, out_spaces=None, vmem=None):
    vmem = vmem or VMEM_MIB[name]
    where = {
        "v": pl.BlockSpec(memory_space=pltpu.VMEM),
        "a": pl.BlockSpec(memory_space=pltpu.HBM),
        "n": pl.BlockSpec(memory_space=pl.ANY),
        "h": pl.BlockSpec(memory_space=pltpu.VMEM),
        "s": pl.BlockSpec(memory_space=pltpu.SMEM),
    }
    out_spaces = out_spaces or "v" * len(outs)
    args = [
        pltpu.with_memory_space_constraint(arg, pltpu.HBM) if s in "ah" else arg
        for arg, s in zip(args, spaces)
    ]
    return pl.pallas_call(
        body,
        out_shape=[
            pltpu.HBM(*o) if s == "a" else jax.ShapeDtypeStruct(*o) for o, s in zip(outs, out_spaces)
        ],
        in_specs=[where[s] for s in spaces],
        out_specs=[where[s] for s in out_spaces],
        scratch_shapes=scratch,
        compiler_params=pltpu.CompilerParams(vmem_limit_bytes=vmem << 20),
        cost_estimate=pl.CostEstimate(flops=flops, transcendentals=0, bytes_accessed=8 << 20),
        name=name,
    )(*args)


def on_device_fast(
    latents,
    pixels,
    keep_mask,
    cotangent,
    w_query,
    w_key,
    w_value,
    kv_bias,
    w_out,
    w_first,
    w_second,
    w_qkv,
    w_self_out,
    w_third,
    w_fourth,
    norm_gains,
    norm_shifts,
    proj_biases,
    pix_gain,
    pix_shift,
):
    images, rows, width = latents.shape
    _, pix, channels = pixels.shape
    padded = -(-(channels + 8) // 16) * 16
    wide = -(-(channels + 8) // 128) * 128
    chips = lax.axis_size("chip")
    lanes = rows // chips
    vm = pltpu.VMEM
    dma = pltpu.SemaphoreType.DMA
    pix_rows = jnp.transpose(pixels, (2, 0, 1))
    unit = 2 * rows * width * width
    cross = 2 * rows * pix * wide * images

    def swapped(values):
        return lax.ppermute(values, "core", SWAP)

    def around(tiles):
        return [
            lax.ppermute(t, "chip", shifted(chips, step + 1)) for step, t in enumerate(tiles)
        ]

    keep, send, par, query_pix, query, pix_normed = call(
        functools.partial(look_body, channels),
        [
            ((padded, rows), F32),
            ((padded, rows), BF),
            ((padded, 128), F32),
            ((images, padded, rows), BF),
            ((rows, width), BF),
            ((images, padded, pix), BF),
        ],
        [
            vm((width, width), BF),
            vm((images, rows, width), BF),
            vm((128, wide), F32),
            vm((images, rows, width), BF),
            vm((images, rows, width), BF),
            vm((padded, width), BF),
            vm((padded, pix), F32),
            vm((16, width), F32),
            vm((images, padded, rows), BF),
            vm((images, padded, pix), BF),
            vm((images, padded, rows), F32),
            vm((channels, images, pix), BF),
            dma,
            dma((3,)),
        ],
        (
            latents,
            pix_rows,
            keep_mask,
            pix_gain,
            pix_shift,
            norm_gains,
            norm_shifts,
            proj_biases,
            w_key,
            w_query,
        ),
        "aahhhhhhha",
        "look",
        3 * unit + 2 * cross,
        "vvvaaa",
    )
    tiles = call(
        functools.partial(join_one_body, channels),
        [((padded, lanes), BF)] * chips,
        [vm((padded, rows), BF)],
        (keep, swapped(send)),
        "vv",
        "join_one",
        1,
    )
    (tile,) = call(
        functools.partial(join_two_body, channels),
        [((padded, lanes), BF)],
        [vm((chips, padded, lanes), BF), dma((chips,))],
        (tiles[0], *around(tiles[1:])),
        "n" * chips,
        "join_two",
        1,
    )
    (tile,) = call(
        gather_body,
        [((padded, rows), BF)],
        [dma((chips,))],
        (tile, *around([tile] * (chips - 1))),
        "n" * chips,
        "gather",
        1,
        "a",
    )
    output, d_after, own_pack, small_grads, keep, send = trunk(
        [tile],
        latents,
        cotangent,
        norm_gains,
        norm_shifts,
        proj_biases,
        w_value,
        kv_bias[None],
        [w_out, w_first, w_second, w_qkv, w_self_out, w_third, w_fourth],
        channels,
        padded,
    )
    got_pack, send = lax.optimization_barrier((swapped(own_pack), send))
    got_send = swapped(send)
    both_keep = keep
    keep, send, both, score_grad, weights_low = call(
        functools.partial(back_one_body, channels),
        [
            ((padded, rows), F32),
            ((padded, rows), BF),
            ((images, padded, rows), BF),
            ((images, pix, rows), BF),
            ((images, pix, rows), BF),
        ],
        [
            vm((images, padded, rows), BF),
            vm((images, padded, rows), BF),
            vm((images, padded, pix), BF),
            vm((images, padded, rows), F32),
            dma((4,)),
        ],
        (own_pack, got_pack, query_pix, pix_normed),
        "anaa",
        "back_one",
        3 * cross,
    )
    keep, send, got_send = lax.optimization_barrier((keep, send, got_send))
    quarter = both_keep.shape[0] // 4
    adds = [vm((2, quarter, 128), BF), vm((2, quarter, 128), BF), dma((2, 2))]
    one, two = call(
        first_add_body,
        [((quarter, 128), BF)] * 2,
        adds,
        (both_keep, got_send),
        "an",
        "first_add",
        1,
    )
    got_output = swapped(output)
    tiles = call(
        back_join_one_body,
        [((padded, lanes), BF)] * chips,
        [vm((padded, rows), BF)],
        (keep, swapped(send)),
        "vv",
        "back_join_one",
        1,
    )
    tiles, score_grad, one, two = lax.optimization_barrier((tiles, score_grad, one, two))
    one, two = lax.ppermute(one, "img", LOW_PAIRS), lax.ppermute(two, "img", HIGH_PAIRS)
    d_pixels, sums, both_outputs = call(
        functools.partial(back_two_body, channels),
        [((channels, images, pix), F32), ((8, wide), F32), ((images, rows, width), BF)],
        [
            vm((padded, pix), F32),
            vm((wide, 128), F32),
            vm((images, padded, rows), BF),
            dma((3,)),
        ],
        (score_grad, weights_low, query_pix, both, pix_rows, par, output, got_output),
        "vvavhhan",
        "back_two",
        2 * cross,
    )
    (tile,) = call(
        functools.partial(back_join_two_body, channels),
        [((padded, lanes), BF)],
        [vm((chips, padded, lanes), BF), dma((chips,))],
        (tiles[0], *around(tiles[1:]), sums),
        "n" * chips + "v",
        "back_join_two",
        1,
    )
    tile, one, two = lax.optimization_barrier((tile, one, two))

    one, two = image_second(
        *call(
            second_add_body,
            [((quarter, 128), BF)] * 2,
            adds,
            (both_keep, got_send, one, two),
            "anvv",
            "second_add",
            1,
        )
    )
    tiles = [tile] + around([tile] * (chips - 1))
    last_rows = width + padded + 32 + 16
    d_lat, d_lat_low, keep, send = call(
        functools.partial(tail_body, channels),
        [
            ((rows, width), F32),
            ((rows, width), BF),
            ((last_rows, 128), BF),
            ((last_rows, 128), BF),
        ],
        [
            vm((rows, width), BF),
            vm((width, width), BF),
            vm((rows, width), F32),
            vm((padded, rows), BF),
            vm((padded, width), BF),
            vm((16, width), F32),
            vm((rows, width), BF),
            vm((rows, width), BF),
            vm((rows, width), F32),
            vm((2, rows, 128), F32),
            vm((2, 8, width), F32),
            vm((32, width), F32),
            dma,
            dma,
            dma,
            dma((chips,)),
        ],
        (
            *tiles,
            latents,
            w_query,
            d_after,
            query,
            w_key,
            norm_gains,
            norm_shifts,
            small_grads,
        ),
        "n" * chips + "aanhhhhh",
        "tail",
        3 * unit,
    )
    keep, send, d_lat_low, one, two = lax.optimization_barrier((keep, send, d_lat_low, one, two))
    got_one, got_two = image_third(one, two)
    part = last_rows // 4
    got_lat = swapped(d_lat_low)

    def partners(tiles):
        return [
            lax.ppermute(t, "img", [(i, i ^ (step + 1)) for i in range(4)])
            for step, t in enumerate(tiles)
        ]

    tiles = call(
        last_add_body,
        [((part, 128), BF)] * 4,
        [],
        (keep, swapped(send)),
        "vv",
        "last_add",
        1,
    )
    tiles, got_lat = lax.optimization_barrier((tiles, got_lat))
    arrived = partners(tiles[1:])
    square = (width, 128)
    first, pieces, shapes = 0, [], []
    for across in (1, 1, 1, 3, 1, 1, 1):
        pieces.append((first, width, across))
        shapes.append((width, 128 * across))
        first += width * across
    pieces += [(first, padded, 1), (first + channels, 1, 1)]
    shapes += [(channels, 128), (1, 128)]
    main = call(
        functools.partial(unpack_main_body, pieces),
        [(s, F32) for s in shapes],
        [vm((4 * one.shape[0], 128), BF), vm((32, 128), F32), dma((4,))],
        (one, two, got_one, got_two),
        "nnnn",
        "unpack_main",
        1,
    )
    d_pixels = jnp.transpose(d_pixels, (1, 2, 0))
    (both_latents,) = call(
        latents_body,
        [((images, rows, width), F32)],
        [],
        (d_lat, got_lat),
        "vv",
        "latents",
        1,
    )
    arrived, both_latents, d_pixels = lax.optimization_barrier((arrived, both_latents, d_pixels))
    (tile,) = call(
        last_sum_body,
        [((part, 128), BF)],
        [vm((4, part, 128), BF), dma((4,))],
        (tiles[0], *arrived),
        "nnnn",
        "last_sum",
        1,
    )
    parts = partners([tile] * 3)
    parts, main = lax.optimization_barrier((parts, main))
    at = width + padded
    rest = call(
        functools.partial(
            unpack_last_body,
            [
                (0, width, 1),
                (width, padded, 1),
                (at, 4, 1),
                (at + 4, 4, 1),
                (at + 8, 9, 1),
                (at + 32, 1, 1),
                (at + 35, 1, 1),
            ],
        ),
        [
            (s, F32)
            for s in (square, (channels, 128), (4, 128), (4, 128), (9, 128), (channels,), (channels,))
        ],
        [vm((last_rows, 128), BF), vm((32, 128), F32), dma((4,))],
        (tile, *parts),
        "nnnn",
        "unpack_last",
        1,
    )
    return (
        both_outputs,
        both_latents,
        d_pixels,
        rest[0],
        rest[1],
        main[7],
        main[8][0],
        main[6],
        main[5],
        main[4],
        main[3],
        main[2],
        main[1],
        main[0],
        rest[2],
        rest[3],
        rest[4],
        rest[5],
        rest[6],
    )


def on_device(*args):
    rows, width = args[0].shape[1:]
    chips = lax.axis_size("chip")
    if (width // chips) % 256 == 0 and width // chips == 256 and (rows // chips) % 128 == 0:
        return on_device_fast(*args)
    return on_device_slow(*args)


def solution(mesh):
    images, pieces = mesh.devices.shape
    split = Mesh(mesh.devices.reshape(images, pieces // 2, 2), ("img", "chip", "core"))
    latent = P("img", None, None)
    weight = P(None, PIX)
    placed = (latent, P("img", PIX, None), P("img", PIX), latent) + (P(),) * 16
    return jax.shard_map(
        on_device,
        mesh=split,
        in_specs=placed,
        out_specs=(latent, latent, P("img", PIX, None), weight, weight, weight, P(PIX))
        + (weight,) * 10
        + (P(), P()),
        check_vma=False,
    )
```

```python
import functools

import jax
import jax.numpy as jnp
from jax import lax
from jax.experimental import pallas as pl
from jax.experimental.pallas import tpu as pltpu
from jax.sharding import Mesh
from jax.sharding import PartitionSpec as P

HEADS = 8
EPSILON = 1e-05
LOG_TWO = 0.6931471805599453
FLOOR_VALUE = -1e30
BF = jnp.bfloat16
F32 = jnp.float32
SWAP = [(0, 1), (1, 0)]
PIX = ("chip", "core")


def dot(a, b, ca, cb):
    return lax.dot_general(a, b, (((ca,), (cb,)), ((), ())), preferred_element_type=F32)


def layer_norm(values, norm_gain, norm_shift):
    centre = values - jnp.mean(values, axis=-1, keepdims=True)
    inverse = lax.rsqrt(jnp.mean(centre * centre, axis=-1, keepdims=True) + EPSILON)
    unit_rows = centre * inverse
    return (unit_rows * norm_gain + norm_shift, unit_rows, inverse)


def row_total(values):
    return jnp.sum(values, axis=tuple(range(values.ndim - 1)))


def norm_back(grad, unit_rows, inverse, norm_gain):
    scaled = grad * norm_gain
    d_values = inverse * (
        scaled
        - jnp.mean(scaled, axis=-1, keepdims=True)
        - unit_rows * jnp.mean(scaled * unit_rows, axis=-1, keepdims=True)
    )
    return (d_values, row_total(grad * unit_rows), row_total(grad))


def gelu_exact(values):
    return jax.nn.gelu(values, approximate=False)


def three_parts(values):
    high = values.astype(BF).astype(F32)
    rest = values - high
    middle = rest.astype(BF).astype(F32)
    return (high, middle, rest - middle)


ROOT_HALF = 0.7071067811865476
ROOT_TWO_PI = 0.3989422804014327


def trunk_core(
    channels,
    span,
    qkv_span,
    chip_start,
    qkv_start,
    flip,
    waits,
    lat,
    mean,
    stats,
    cot,
    gains,
    shifts,
    biases,
    result,
    d_after,
    pack,
    small,
    keep_h,
    send_h,
    wv,
    wo,
    w1,
    w2,
    wq,
    ws,
    w3,
    w4,
    att,
    dg1,
    h1,
    x2,
    qkv,
    wl,
    inv_total,
    sl,
    x3,
    dg4,
    h4,
    acc,
    low,
    low_two,
    normed,
    stat,
    sums,
    stage,
    spare_sem,
    store_sem,
):
    rows, width = lat.shape
    head_dim = width // HEADS
    head_scale = head_dim ** (-0.5)
    x1 = d_after
    def over_rows(step, most=512):
        block = min(most, rows)
        if block == rows:
            step(pl.ds(0, rows))
            return

        def run(i, carry):
            step(pl.ds(pl.multiple_of(i * block, block), block))
            return carry

        lax.fori_loop(0, rows // block, run, 0)

    def vector(ref, i):
        return ref[i : i + 1, :].astype(F32)

    def add_sum(at, value):
        sums[at] += jnp.sum(value.reshape(-1, 8, width), axis=0)

    def clear(*ats):
        for at in ats:
            sums[at] = jnp.zeros((8, width), F32)

    def flush(at, row):
        small[row : row + 1, :] = jnp.sum(sums[at], axis=0, keepdims=True)

    def norm_forward(x, i):
        g, s = vector(gains, i), vector(shifts, i)

        def step(at):
            v = x[at, :]
            m = jnp.mean(v, axis=1, keepdims=True)
            c = v - m
            iv = lax.rsqrt(jnp.mean(c * c, axis=1, keepdims=True) + EPSILON)
            normed[at, :] = (c * iv * g + s).astype(BF)
            stat[i - 1, 0, at, :] = jnp.broadcast_to(m, (m.shape[0], 128))
            stat[i - 1, 1, at, :] = jnp.broadcast_to(iv, (m.shape[0], 128))

        over_rows(step)

    def norm_again(x, i):
        g, s = vector(gains, i), vector(shifts, i)

        def step(at):
            m, iv = stat[i - 1, 0, at, 0:1], stat[i - 1, 1, at, 0:1]
            normed[at, :] = ((x[at, :] - m) * iv * g + s).astype(BF)

        over_rows(step)

    def norm_backward(x, skip, i, gain_row, shift_row, bias_row):
        g = vector(gains, i)
        clear(0, 1, 2)

        def step(at):
            m, iv = stat[i - 1, 0, at, 0:1], stat[i - 1, 1, at, 0:1]
            unit = (x[at, :] - m) * iv
            grad = acc[at, :]
            scaled = grad * g
            mean_one = jnp.mean(scaled, axis=1, keepdims=True)
            mean_two = jnp.mean(scaled * unit, axis=1, keepdims=True)
            total = skip[at, :].astype(F32) + iv * (scaled - mean_one - unit * mean_two)
            add_sum(0, grad * unit)
            add_sum(1, grad)
            add_sum(2, total)
            x[at, :] = total
            low_two[at, :] = total.astype(BF)

        over_rows(step)
        flush(0, gain_row)
        flush(1, shift_row)
        flush(2, bias_row)

    def hidden(bias_row, h, dg):
        b = vector(biases, bias_row)

        def step(at):
            v = acc[at, :] + b
            cdf = 0.5 * (1.0 + lax.erf(v * ROOT_HALF))
            h[at, :] = (v * cdf).astype(BF)
            dg[at, :] = cdf + v * (jnp.exp(-0.5 * v * v) * ROOT_TWO_PI)

        over_rows(step)

    def hidden_back(dg, bias_row):
        clear(0)

        def step(at):
            d = acc[at, :] * dg[at, :]
            add_sum(0, d)
            low[at, :] = d.astype(BF)

        over_rows(step)
        flush(0, bias_row)

    pending = [[], []]
    state = {"slot": 0, "row": 0}

    def emit(x, dy, start, span, ca, beside=None):
        count = x.shape[1 - ca]
        half = span // 2
        for t in range(half // 128):
            slot = state["slot"]
            state["slot"] = 1 - slot
            for waiting in pending[slot]:
                waiting.wait()
            pending[slot] = []
            mine = dy[:, pl.ds(pl.multiple_of(start + flip * half + t * 128, 128), 128)]
            other = dy[:, pl.ds(pl.multiple_of(start + (1 - flip) * half + t * 128, 128), 128)]
            both = jnp.concatenate([mine, other], axis=1)
            stage[slot, :count, :] = dot(x[...], both, ca, 0).astype(BF)
            if beside is not None and t == half // 128 - 1:
                beside()
            target = pl.ds(state["row"] + t * count, count)
            for side, out in enumerate((keep_h, send_h)):
                src = stage.at[slot, pl.ds(0, count), pl.ds(side * 128, 128)]
                copy = pltpu.make_async_copy(src, out.at[target, :], store_sem.at[slot, side])
                copy.start()
                pending[slot].append(copy)
        state["row"] += count * (half // 128)

    waits[0]()
    att[...] = dot(mean[...], wv[...], 0, 0).astype(BF)
    waits[1]()
    acc[...] = dot(att[...], wo[...], 1, 0)
    out_bias = vector(biases, 1)

    def after_cross(at):
        x1[at, :] = lat[at, :].astype(F32) + acc[at, :] + out_bias

    over_rows(after_cross)
    waits[9]()
    norm_forward(x1, 1)
    waits[2]()
    acc[...] = dot(normed[...], w1[...], 1, 0)
    hidden(2, h1, dg1)
    waits[3]()
    x2[...] = x1[...] + dot(h1[...], w2[...], 1, 0) + vector(biases, 3)
    norm_forward(x2, 2)
    waits[4]()
    qkv[:, :width] = (
        (dot(normed[...], wq[:, :width], 1, 0) + vector(biases, 4)) * head_scale
    ).astype(BF)
    qkv[:, width : 2 * width] = dot(normed[...], wq[:, width : 2 * width], 1, 0).astype(BF)
    qkv[:, 2 * width :] = (
        dot(normed[...], wq[:, 2 * width :], 1, 0) + vector(biases, 5)
    ).astype(BF)
    ones = jnp.ones((rows, head_dim), BF)

    def head_at(h, part):
        return pl.ds(pl.multiple_of(h * head_dim + part * width, head_dim), head_dim)

    def head_forward(h, carry):
        scores = dot(qkv[:, head_at(h, 0)], qkv[:, head_at(h, 1)], 1, 1)
        top = jnp.max(scores, axis=1, keepdims=True)
        shift = LOG_TWO * jnp.floor(top / LOG_TWO)
        weights = jnp.exp(scores - shift).astype(BF)
        wl[h] = weights
        value = jnp.concatenate([qkv[:, head_at(h, 2)], ones], axis=1)
        both = dot(weights, value, 1, 0)
        over = 1.0 / both[:, head_dim:]
        inv_total[:, head_at(h, 0)] = over
        sl[:, head_at(h, 0)] = (both[:, :head_dim] * over).astype(BF)
        return carry

    lax.fori_loop(0, HEADS, head_forward, 0, unroll=True)
    waits[5]()
    x3[...] = x2[...] + dot(sl[...], ws[...], 1, 0) + vector(biases, 6)
    norm_forward(x3, 3)
    waits[6]()
    acc[...] = dot(normed[...], w3[...], 1, 0)
    hidden(7, h4, dg4)
    waits[7]()
    low[...] = (x3[...] + dot(h4[...], w4[...], 1, 0) + vector(biases, 8)).astype(BF)
    result_copy = pltpu.make_async_copy(low, result, spare_sem)
    result_copy.start()

    waits[8]()
    clear(0)

    def cot_sum(at):
        add_sum(0, cot[at, :].astype(F32))

    over_rows(cot_sum)
    flush(0, 13)
    acc[...] = dot(cot[...], w4[...], 1, 1)
    result_copy.wait()
    emit(h4, cot, chip_start, span, 0, lambda: hidden_back(dg4, 12))
    acc[...] = dot(low[...], w3[...], 1, 1)
    emit(normed, low, chip_start, span, 0, lambda: norm_backward(x3, cot, 3, 2, 5, 11))
    acc[...] = dot(low_two[...], ws[...], 1, 1)
    clear(0, 1)

    def head_backward(h, carry):
        head = head_at(h, 0)
        query, keys, value = qkv[:, head], qkv[:, head_at(h, 1)], qkv[:, head_at(h, 2)]
        grad = acc[:, head] * inv_total[:, head]
        numer_grad = grad.astype(BF)
        total_part = (-(grad * sl[:, head].astype(F32))).astype(BF)
        weights = wl[h]
        d_weights = dot(
            jnp.concatenate([numer_grad, total_part], axis=1),
            jnp.concatenate([value, ones], axis=1),
            1,
            1,
        )
        score_grad = (d_weights * weights.astype(F32)).astype(BF)
        d_value = dot(weights, numer_grad, 0, 0)
        d_query = dot(score_grad, keys, 1, 0) * head_scale
        d_keys = dot(score_grad, query, 0, 0)
        qkv[:, head] = d_query.astype(BF)
        qkv[:, head_at(h, 1)] = d_keys.astype(BF)
        qkv[:, head_at(h, 2)] = d_value.astype(BF)
        sums[0, :, head] = jnp.sum(d_query.reshape(-1, 8, head_dim), axis=0)
        sums[1, :, head] = jnp.sum(d_value.reshape(-1, 8, head_dim), axis=0)
        return carry

    def heads_backward():
        lax.fori_loop(0, HEADS, head_backward, 0, unroll=True)

    emit(sl, low_two, chip_start, span, 0, heads_backward)
    flush(0, 9)
    flush(1, 10)
    norm_again(x2, 2)
    acc[...] = dot(qkv[...], wq[...], 1, 1)
    emit(normed, qkv, qkv_start, qkv_span, 0, lambda: norm_backward(x2, x3, 2, 1, 4, 8))
    acc[...] = dot(low_two[...], w2[...], 1, 1)

    def early_hidden():
        hidden_back(dg1, 7)
        norm_again(x1, 1)

    emit(h1, low_two, chip_start, span, 0, early_hidden)
    acc[...] = dot(low[...], w1[...], 1, 1)
    emit(normed, low, chip_start, span, 0, lambda: norm_backward(x1, x2, 1, 0, 3, 6))
    low[...] = dot(low_two[...], wo[...], 1, 1).astype(BF)
    emit(att, low_two, chip_start, span, 0)
    emit(mean, low, chip_start, span, 1)
    grad_pix = dot(wv[...], low[...], 1, 1)
    over = stats[0:1, :]
    row = lax.broadcasted_iota(jnp.int32, grad_pix.shape, 0)
    line = jnp.sum(jnp.where(row == channels, grad_pix, 0.0), axis=0, keepdims=True)
    line = (line - jnp.sum(grad_pix * mean[...].astype(F32), axis=0, keepdims=True)) * over
    high = line.astype(BF).astype(F32)
    packed = jnp.where(row < channels, grad_pix * over, 0.0)
    extras = [high, line - high, stats[1:2, :], stats[2:3, :], stats[3:4, :]]
    for at, extra in enumerate(extras):
        packed = jnp.where(row == channels + at, extra, packed)
    pack[...] = packed.astype(BF)
    for slot in range(2):
        for waiting in pending[slot]:
            waiting.wait()


def trunk_slow_body(channels, span, qkv_span, place, lat, mean, stats, cot, gains, shifts, biases, *refs):
    load_sem, store_sem = refs[-2:]
    loads = []
    for at in range(8):
        copy = pltpu.make_async_copy(refs[at], refs[14 + at], load_sem.at[at])
        copy.start()
        loads.append(copy.wait)
    loads += [lambda: None, lambda: None]
    trunk_core(
        channels, span, qkv_span, place[0], place[1], place[2], loads, lat, mean, stats, cot,
        gains, shifts, biases, *refs[8:-2], load_sem.at[0], store_sem
    )


def trunk_fast_body(channels, chips, *refs):
    tiles, refs = refs[:chips], refs[chips:]
    lat_h, cot_h, gains, shifts, biases, value, kv_bias = refs[:7]
    weights_h, refs = refs[7:14], refs[14:]
    lat, mean, raw, stats, tail, load_sem, store_sem = refs[-7:]
    cot = lat
    wv = refs[6]
    place = places()
    chip, core = place[0], place[1]
    tile_copies = [pltpu.make_async_copy(tiles[0], raw, load_sem.at[9])]
    tile_copies[0].start()
    loads = []
    pairs = [(lat_h.at[core], lat)]
    pairs += [(weights_h[at], refs[7 + at]) for at in range(7)]
    for at, (src, dst) in enumerate(pairs):
        copy = pltpu.make_async_copy(src, dst, load_sem.at[at])
        copy.start()
        loads.append(copy.wait)
    cot_copy = pltpu.make_async_copy(cot_h.at[core], cot, load_sem.at[8])
    loads += [cot_copy.wait, cot_copy.start]
    fill_rows(wv, value, tail, kv_bias[...].astype(F32))
    for copy in tile_copies:
        copy.wait()
    full = raw[...].astype(F32)
    mean[...] = jnp.where(row_of(full) <= channels, full, 0.0).astype(BF)
    total = (
        full[channels + 1 : channels + 2]
        + full[channels + 2 : channels + 3]
        + full[channels + 3 : channels + 4]
    )
    stats[0:1, :] = 1.0 / total
    for at in range(3):
        stats[at + 1 : at + 2, :] = full[channels + 4 + at : channels + 5 + at]
    trunk_core(
        channels, 256, 768, chip * 256, chip * 768, core, loads, lat, mean, stats, cot,
        gains, shifts, biases, *refs[:-7], load_sem.at[0], store_sem
    )


def trunk_scratch(rows, width, padded):
    big = pltpu.VMEM((rows, width), F32)
    half = pltpu.VMEM((rows, width), BF)
    square = pltpu.VMEM((width, width), BF)
    return [
        pltpu.VMEM((padded, width), BF),
        square,
        square,
        square,
        pltpu.VMEM((width, 3 * width), BF),
        square,
        square,
        square,
        half,
        big,
        half,
        big,
        pltpu.VMEM((rows, 3 * width), BF),
        pltpu.VMEM((HEADS, rows, rows), BF),
        big,
        half,
        big,
        big,
        half,
        big,
        half,
        half,
        half,
        pltpu.VMEM((3, 2, rows, 128), F32),
        pltpu.VMEM((3, 8, width), F32),
        pltpu.VMEM((2, width, 256), BF),
    ]


def trunk_outs(rows, width, padded, sent):
    return [
        ((rows, width), BF),
        ((rows, width), F32),
        ((padded, rows), BF),
        ((16, width), F32),
        ((sent, 128), BF),
        ((sent, 128), BF),
    ]


def trunk_slow(place, lat, mean, stats, cot, gains, shifts, biases, weights, channels, span, qkv_span):
    rows, width = lat.shape
    padded = mean.shape[0]
    sent = width * (6 * (span // 256) + qkv_span // 256) + padded * (span // 256)
    return call(
        functools.partial(trunk_slow_body, channels, span, qkv_span),
        trunk_outs(rows, width, padded, sent),
        trunk_scratch(rows, width, padded)
        + [pltpu.SemaphoreType.DMA((8,)), pltpu.SemaphoreType.DMA((2, 2))],
        (place, lat, mean, stats, cot, gains, shifts, biases, *weights),
        "s" + "v" * 7 + "n" * 8,
        "trunk",
        60 * rows * width * width,
        "avvvaa",
        58,
    )


def trunk(
    tiles, latents, cotangent, gains, shifts, biases, value, kv_bias, weights, channels, padded
):
    _, rows, width = latents.shape
    sent = -(-(9 * width + padded) // 64) * 64
    vm = pltpu.VMEM
    return call(
        functools.partial(trunk_fast_body, channels, len(tiles)),
        trunk_outs(rows, width, padded, sent),
        trunk_scratch(rows, width, padded)
        + [
            vm((rows, width), BF),
            vm((padded, rows), BF),
            vm((padded, rows), BF),
            vm((8, rows), F32),
            vm((16, width), F32),
            pltpu.SemaphoreType.DMA((9 + len(tiles),)),
            pltpu.SemaphoreType.DMA((2, 2)),
        ],
        (*tiles, latents, cotangent, gains, shifts, biases, value, kv_bias, *weights),
        "a" * len(tiles) + "aahhhhv" + "a" * 7,
        "trunk",
        60 * rows * width * width,
        "avvvaa",
        58,
    )


def shifted(devices, step):
    return [(i, (i + step) % devices) for i in range(devices)]


def exchange(tiles, axis):
    devices = tiles.shape[0]
    if devices == 1:
        return tiles
    place = lax.axis_index(axis)
    got = [lax.dynamic_index_in_dim(tiles, place, 0, keepdims=False)]
    for step in range(1, devices):
        tile = lax.dynamic_index_in_dim(tiles, (place + step) % devices, 0, keepdims=False)
        got.append(lax.ppermute(tile, axis, shifted(devices, step)))
    return jnp.stack(got)


def gather(tile, axis):
    devices = lax.axis_size(axis)
    place = lax.axis_index(axis)
    got = [tile]
    for step in range(1, devices):
        got.append(lax.ppermute(tile, axis, shifted(devices, step)))
    stacked = jnp.stack(got)
    order = (place - jnp.arange(devices)) % devices
    return jnp.stack([lax.dynamic_index_in_dim(stacked, order[i], 0, keepdims=False) for i in range(devices)])


def in_tiles(rows, devices):
    return jnp.moveaxis(rows.reshape(rows.shape[0], devices, -1), 1, 0)


def from_tiles(tiles):
    return jnp.moveaxis(tiles, 0, 1).reshape(tiles.shape[1], -1)


def image_parts(rows):
    count = rows.shape[0]
    quarter = -(-count // 64) * 16
    tiles = jnp.pad(rows, ((0, 4 * quarter - count), (0, 0))).reshape(4, quarter, -1)
    return tiles


LOW_PAIRS = [(0, 1), (1, 0), (2, 3), (3, 2)]
HIGH_PAIRS = [(0, 2), (2, 0), (1, 3), (3, 1)]


def pick(pair, at):
    return jnp.where(at == 0, pair[0], pair[1])


def plus(a, b):
    return (a.astype(F32) + b.astype(F32)).astype(BF)


def image_places():
    place = lax.axis_index("img")
    return place // 2, place % 2


def image_first(rows):
    high, low = image_places()
    tiles = image_parts(rows)
    one, two = tiles[:2], tiles[2:]
    got_one = lax.ppermute(pick(one, 1 - low), "img", LOW_PAIRS)
    got_two = lax.ppermute(pick(two, 1 - high), "img", HIGH_PAIRS)
    return plus(pick(one, low), got_one), plus(pick(two, high), got_two)


def image_second(one, two):
    got_one = lax.ppermute(one, "img", HIGH_PAIRS)
    got_two = lax.ppermute(two, "img", LOW_PAIRS)
    return plus(one, got_one), plus(two, got_two)


def image_third(one, two):
    return lax.ppermute(one, "img", LOW_PAIRS), lax.ppermute(two, "img", HIGH_PAIRS)


def image_whole(one, two, got_one, got_two, count):
    high, low = image_places()
    whole = jnp.concatenate(
        [
            jnp.where(low == 0, one, got_one),
            jnp.where(low == 0, got_one, one),
            jnp.where(high == 0, two, got_two),
            jnp.where(high == 0, got_two, two),
        ]
    )
    return whole[:count]


def image_sum(rows):
    one, two = image_second(*image_first(rows))
    return image_whole(one, two, *image_third(one, two), rows.shape[0])


def on_device_slow(
    latents,
    pixels,
    keep_mask,
    cotangent,
    w_query,
    w_key,
    w_value,
    kv_bias,
    w_out,
    w_first,
    w_second,
    w_qkv,
    w_self_out,
    w_third,
    w_fourth,
    norm_gains,
    norm_shifts,
    proj_biases,
    pix_gain,
    pix_shift,
):
    width = latents.shape[-1]
    rows = latents.shape[1]
    channels = pixels.shape[-1]
    padded = -(-(channels + 8) // 16) * 16
    cross_scale = width ** (-0.5)
    chips = lax.axis_size("chip")
    chip = lax.axis_index("chip")
    core = lax.axis_index("core")
    piece = width // (chips * 2)

    def columns(values):
        span = values.shape[-1] // chips
        return lax.dynamic_slice_in_dim(values, chip * span, span, values.ndim - 1)

    def mine(values):
        return lax.dynamic_index_in_dim(values, core, 0, keepdims=False)

    def other(values):
        return lax.dynamic_index_in_dim(values, 1 - core, 0, keepdims=False)

    def swapped(values):
        return lax.ppermute(values, "core", SWAP)

    gains = norm_gains.astype(F32)
    shifts = norm_shifts.astype(F32)
    biases = proj_biases.astype(F32)
    pixel_gain = pix_gain.astype(F32)
    pixel_shift = pix_shift.astype(F32)
    key_rows = jnp.pad(w_key, ((0, padded - channels), (0, 0)))
    value_rows = jnp.concatenate(
        [w_value, kv_bias[None], jnp.zeros((padded - channels - 1, width), BF)]
    )

    q_normed, _, _ = layer_norm(latents.astype(F32), gains[0], shifts[0])
    q_normed_low = q_normed.astype(BF)
    query = (
        (dot(q_normed_low.reshape(-1, width), w_query, 1, 0) + biases[0]) * cross_scale
    ).astype(BF)
    query_pix = jnp.stack(
        [dot(key_rows, query[:rows], 1, 1), dot(key_rows, query[rows:], 1, 1)]
    ).astype(BF)
    p_normed, p_unit, p_inverse = layer_norm(pixels.astype(F32), pixel_gain, pixel_shift)
    lane = jnp.arange(padded)
    ones_lanes = ((lane == channels) | (lane == channels + 1)).astype(BF)
    pix_low = jnp.pad(p_normed.astype(BF), ((0, 0), (0, 0), (0, padded - channels))) + ones_lanes
    kept_pixels = keep_mask[:, :, None] > 0
    scores = jnp.einsum("bpc,bci->bpi", pix_low, query_pix, preferred_element_type=F32)
    local_top = jnp.max(jnp.where(kept_pixels, scores, FLOOR_VALUE), axis=1)
    level = jnp.floor(local_top / LOG_TWO)
    first_weights = jnp.where(
        kept_pixels, jnp.exp(scores - (level * LOG_TWO)[:, None, :]), 0.0
    ).astype(BF)
    local_numer = jnp.einsum("bpc,bpi->bci", pix_low, first_weights, preferred_element_type=F32)

    def packed(body, extras):
        lead = jnp.concatenate([body] + [e[None, :] for e in extras]).astype(BF)
        return jnp.pad(lead, ((0, padded - lead.shape[0]), (0, 0)))

    def fwd_pack(numer, level):
        total = numer[channels]
        return packed(numer[:channels], three_parts(total)[:2] + three_parts(level))

    def fwd_unpack(pack):
        pack = pack.astype(F32)
        total = pack[channels] + pack[channels + 1]
        level = pack[channels + 2] + pack[channels + 3] + pack[channels + 4]
        return (jnp.concatenate([pack[:channels], total[None]]), level)

    def joined(parts):
        top = parts[0][1]
        for _, level in parts[1:]:
            top = jnp.maximum(top, level)
        return (sum(body * jnp.exp2(level - top)[None, :] for body, level in parts), top)

    sent = swapped(fwd_pack(other(local_numer), other(level)))
    body, top = joined([(mine(local_numer)[: channels + 1], mine(level)), fwd_unpack(sent)])
    got = exchange(in_tiles(fwd_pack(body, top), chips), "chip")
    body, top = joined([fwd_unpack(got[i]) for i in range(chips)])
    mean_tile = packed(
        body[:channels] / body[channels], three_parts(body[channels]) + three_parts(top)
    )
    mean_all = from_tiles(gather(mean_tile, "chip")).astype(F32)
    cross_total = mean_all[channels] + mean_all[channels + 1] + mean_all[channels + 2]
    cross_level = mean_all[channels + 3] + mean_all[channels + 4] + mean_all[channels + 5]
    row = jnp.arange(padded)[:, None]
    mean_pix = jnp.where(row < channels, mean_all, jnp.where(row == channels, 1.0, 0.0))
    mean_low = mean_pix.astype(BF)

    _, q_unit, q_inverse = layer_norm(mine(latents).astype(F32), gains[0], shifts[0])
    fast = piece % 128 == 0
    if fast:
        span, qkv_span = 2 * piece, 6 * piece
        starts = (chip * span, chip * qkv_span)
        flip = core
    else:
        span, qkv_span = 256, 256
        starts = tuple(
            jnp.minimum(chip * size // chips // 128 * 128, size - 256) for size in (width, 3 * width)
        )
        flip = 0 * core
    place = jnp.stack([starts[0], starts[1], flip]).astype(jnp.int32)
    stats = jnp.concatenate(
        [
            (1.0 / cross_total)[None],
            mean_all[channels + 3 : channels + 6],
            jnp.zeros((4, rows), F32),
        ]
    )
    output, d_after, own_pack, small_grads, keep, send = trunk_slow(
        place,
        mine(latents),
        mean_low,
        stats,
        mine(cotangent),
        norm_gains,
        norm_shifts,
        proj_biases,
        [value_rows, w_out, w_first, w_second, w_qkv, w_self_out, w_third, w_fourth],
        channels,
        span,
        qkv_span,
    )
    def flat(arrays):
        return jnp.concatenate(
            [a.reshape(a.shape[0], -1, piece).swapaxes(0, 1).reshape(-1, piece) for a in arrays]
        ).astype(BF)

    def split(grads):
        keep, send = [], []
        for g in grads:
            half = g.shape[-1] // 2
            keep.append(lax.dynamic_slice_in_dim(g, core * half, half, 1))
            send.append(lax.dynamic_slice_in_dim(g, (1 - core) * half, half, 1))
        return flat(keep), flat(send)

    squares = [(width, piece)] * 3
    spans = squares + [(width, 3 * piece)] + squares + [(padded, piece)]
    if not fast:
        blocks, at = [], 0
        for r, c in spans:
            size = c * chips * 2
            block = jnp.concatenate([keep[at : at + r], send[at : at + r]], axis=1)
            offset = chip * 2 * c - (starts[1] if size > width else starts[0])
            blocks.append(lax.dynamic_slice_in_dim(block, offset, 2 * c, 1))
            at += r
        keep, send = split(blocks)
    got_pack, got_send = lax.optimization_barrier((swapped(own_pack), swapped(send)))
    both_cores = plus(keep, got_send)
    got_pack, both_cores = lax.optimization_barrier((got_pack, both_cores))
    one, two = image_first(both_cores)
    both = jnp.where(core == 0, jnp.stack([own_pack, got_pack]), jnp.stack([got_pack, own_pack]))

    levels = jnp.sum(both[:, channels + 2 : channels + 5].astype(F32), axis=1)
    weights = jnp.where(kept_pixels, jnp.exp(scores - (levels * LOG_TWO)[:, None, :]), 0.0)
    grad_rows = jnp.where(row[None] < channels + 2, both, jnp.zeros((), BF))
    d_weights = jnp.einsum("bpc,bci->bpi", pix_low, grad_rows, preferred_element_type=F32)
    score_grad = (d_weights * weights).astype(BF)
    query_part = jnp.einsum("bpc,bpi->bci", pix_low, score_grad, preferred_element_type=F32)
    d_pix_normed = jnp.einsum(
        "bpi,bci->bpc", score_grad, query_pix, preferred_element_type=F32
    ) + jnp.einsum("bpi,bci->bpc", weights.astype(BF), grad_rows, preferred_element_type=F32)
    d_pix_normed = d_pix_normed[..., :channels]
    scaled = d_pix_normed * pixel_gain
    d_pixels = p_inverse * (
        scaled
        - jnp.mean(scaled, axis=-1, keepdims=True)
        - p_unit * jnp.mean(scaled * p_unit, axis=-1, keepdims=True)
    )
    pix_sums = jnp.stack(
        [jnp.sum(d_pix_normed * p_unit, axis=1), jnp.sum(d_pix_normed, axis=1)], axis=1
    )
    pix_sums = jnp.pad(pix_sums, ((0, 0), (0, 0), (0, rows - channels)))

    def bwd_pack(body, sums):
        high, low, _ = three_parts(sums)
        return packed(body[:channels], [high[0], low[0], high[1], low[1]])

    def bwd_unpack(pack):
        pack = pack.astype(F32)
        sums = jnp.stack(
            [pack[channels] + pack[channels + 1], pack[channels + 2] + pack[channels + 3]]
        )
        return (pack[:channels], sums)

    query_part, pix_sums, one, two = lax.optimization_barrier((query_part, pix_sums, one, two))
    one, two = image_second(one, two)
    sent = swapped(bwd_pack(other(query_part), other(pix_sums)))
    body_two, sums_two = bwd_unpack(sent)
    body, sums = (mine(query_part)[:channels] + body_two, mine(pix_sums) + sums_two)
    got = exchange(in_tiles(bwd_pack(body, sums), chips), "chip")
    got = [bwd_unpack(got[i]) for i in range(chips)]
    body, sums = (sum(g[0] for g in got), sum(g[1] for g in got))
    body, sums, one, two = lax.optimization_barrier((body, sums, one, two))
    got_one, got_two = image_third(one, two)
    all_parts = from_tiles(gather(bwd_pack(body, sums), "chip"))
    _, sums = bwd_unpack(all_parts)
    query_sum = jnp.where(row < channels, all_parts, jnp.zeros((), BF))

    d_query = dot(query_sum, key_rows, 0, 0) * cross_scale
    d_query_low = d_query.astype(BF)
    own_normed = mine(q_normed_low)
    own_query = lax.dynamic_slice_in_dim(query, core * rows, rows, 0)
    d_w_query = dot(own_normed, columns(d_query_low), 0, 0)
    d_w_key = dot(query_sum, columns(own_query), 1, 0)
    d_q_normed = dot(d_query_low, w_query, 1, 1)
    d_q_in, d_gain_zero, d_shift_zero = norm_back(d_q_normed, q_unit, q_inverse, gains[0])
    d_latents_own = d_after + d_q_in

    def two_images(own):
        got = swapped(own.astype(BF)).astype(own.dtype)
        return jnp.where(core == 0, jnp.stack([own, got]), jnp.stack([got, own]))

    def unpacked(whole, spans):
        outs, at = [], 0
        for r, c in spans:
            count = r * (c // piece)
            part = whole[at : at + count].reshape(c // piece, r, piece).swapaxes(0, 1).reshape(r, c)
            outs.append(part.astype(F32))
            at += count
        return outs

    def reduced(keep, send, spans):
        return unpacked(image_sum(plus(keep, swapped(send))), spans)

    small = jnp.concatenate(
        [
            d_gain_zero[None],
            small_grads[0:3],
            d_shift_zero[None],
            small_grads[3:6],
            row_total(d_query)[None],
            small_grads[6:14],
        ]
    )
    sum_lanes = -(-channels // piece) * piece
    pix_rows = sums[:, :sum_lanes].reshape(-1, piece)
    pix_rows = jnp.concatenate([pix_rows, pix_rows], axis=1)
    last_spans = [(width, piece), (padded, piece), (small.shape[0], piece), (pix_rows.shape[0], piece)]
    keep, send = split([d_w_query, d_w_key, columns(small), pix_rows])
    keep, send, got_one, got_two = lax.optimization_barrier((keep, send, got_one, got_two))
    last = reduced(keep, send, last_spans)
    main = unpacked(image_whole(one, two, got_one, got_two, both_cores.shape[0]), spans)
    d_small = last[2]
    pix_out = last[3].reshape(2, sum_lanes)
    return (
        two_images(output.astype(BF)),
        two_images(d_latents_own),
        d_pixels,
        last[0],
        last[1][:channels],
        main[7][:channels],
        main[7][channels],
        main[6],
        main[5],
        main[4],
        main[3],
        main[2],
        main[1],
        main[0],
        d_small[0:4],
        d_small[4:8],
        d_small[8:17],
        pix_out[0, :channels],
        pix_out[1, :channels],
    )


VMEM_MIB = {
    "look": 28,
    "join_one": 6,
    "join_two": 6,
    "gather": 6,
    "back_one": 20,
    "back_join_one": 6,
    "back_two": 24,
    "back_join_two": 6,
    "tail": 24,
    "last_add": 8,
    "first_add": 8,
    "second_add": 8,
    "last_sum": 6,
    "unpack_main": 24,
    "latents": 10,
    "unpack_last": 8,
}
LOWEST_LEVEL = -16777216.0


def row_of(value):
    return lax.broadcasted_iota(jnp.int32, value.shape, 0)


def with_rows(body, first, extras):
    row = row_of(body)
    for at, extra in enumerate(extras):
        body = jnp.where(row == first + at, extra, body)
    return body


def pack_sum(body, channels, level):
    total = body[channels : channels + 1]
    extras = three_parts(total)[:2] + three_parts(level)
    return with_rows(body, channels, extras).astype(BF)


def unpack_sum(pack, channels):
    pack = pack.astype(F32)
    total = pack[channels : channels + 1] + pack[channels + 1 : channels + 2]
    level = (
        pack[channels + 2 : channels + 3]
        + pack[channels + 3 : channels + 4]
        + pack[channels + 4 : channels + 5]
    )
    return with_rows(pack, channels, [total]), level


def join_sums(parts):
    top = parts[0][1]
    for _, level in parts[1:]:
        top = jnp.maximum(top, level)
    body = None
    for part, level in parts:
        scaled = part * jnp.exp2(level - top)
        body = scaled if body is None else body + scaled
    return body, top


def fill_rows(dst, src, tail, extra=None):
    count = src.shape[0]
    base = count // 16 * 16
    dst[:base, :] = src[:base, :]
    tail[...] = jnp.zeros_like(tail)
    tail[: count - base, :] = src[base:count, :].astype(F32)
    if extra is not None:
        tail[count - base : count - base + 1, :] = extra
    dst[base : base + 16, :] = tail[...].astype(BF)


def pixel_units(pix, image, xs, channels):
    xs[:channels, :] = pix[:, image, :].astype(F32)
    x = xs[...]
    inside = row_of(x) < channels
    mean = jnp.sum(x, axis=0, keepdims=True) * (1.0 / channels)
    c = jnp.where(inside, x - mean, 0.0)
    iv = lax.rsqrt(jnp.sum(c * c, axis=0, keepdims=True) * (1.0 / channels) + EPSILON)
    return c * iv, iv, inside


def look_body(
    channels,
    lat_h,
    pix_h,
    mask,
    pix_gain,
    pix_shift,
    gains,
    shifts,
    biases,
    wk_in,
    wq_h,
    keep,
    send,
    par,
    qp_h,
    q_h,
    pn_h,
    wq,
    held,
    turn,
    normed,
    qs,
    wk,
    xs,
    tail,
    qp_out,
    pn_out,
    bodies,
    pix,
    sem,
    out_sem,
):
    images, rows, width = lat_h.shape
    core = places()[1]
    lat_copies = [
        pltpu.make_async_copy(lat_h.at[image], held.at[image], out_sem.at[image])
        for image in range(images)
    ]
    for lat_copy in lat_copies:
        lat_copy.start()
    pix_copy = pltpu.make_async_copy(pix_h, pix, out_sem.at[2])
    pix_copy.start()
    copy = pltpu.make_async_copy(wq_h, wq, sem)
    copy.start()
    turn[...] = jnp.zeros_like(turn)
    turn[0:1, :channels] = pix_gain[...].astype(F32).reshape(1, channels)
    turn[1:2, :channels] = pix_shift[...].astype(F32).reshape(1, channels)
    par[...] = turn[...].T[: par.shape[0]]
    g, s = gains[0:1, :].astype(F32), shifts[0:1, :].astype(F32)

    fill_rows(wk, wk_in, tail)
    xs[...] = jnp.zeros_like(xs)
    for image in range(images):
        lat_copies[image].wait()
        v = held[image].astype(F32)
        c = v - jnp.mean(v, axis=1, keepdims=True)
        iv = lax.rsqrt(jnp.mean(c * c, axis=1, keepdims=True) + EPSILON)
        normed[image] = (c * iv * g + s).astype(BF)
    copy.wait()
    bias = biases[0:1, :].astype(F32)

    def per_image(image):
        qs[image] = ((dot(normed[image], wq[...], 1, 0) + bias) * width ** (-0.5)).astype(BF)
        scored = dot(wk[...], qs[image], 1, 1)
        qp_out[image] = with_rows(scored, channels + 2, [jnp.ones((1, rows), F32)]).astype(BF)
        unit, _, _ = pixel_units(pix, image, xs, channels)
        n = unit * par[:, 0:1] + par[:, 1:2]
        off = jnp.where(mask[pl.ds(image, 1), :] > 0, 0.0, FLOOR_VALUE)
        one = jnp.ones_like(off)
        pn_out[image] = with_rows(n, channels, [one, one, off]).astype(BF)
        scores = dot(pn_out[image], qp_out[image], 0, 0)
        top = jnp.max(scores, axis=0, keepdims=True)
        level = jnp.maximum(jnp.floor(top / LOG_TWO), LOWEST_LEVEL)
        weights = jnp.exp(scores - level * LOG_TWO).astype(BF)
        body = dot(pn_out[image], weights, 1, 0)
        bodies[image] = with_rows(body, channels + 1, [level])

    pix_copy.wait()
    for image in range(images):
        per_image(image)
    keep[...] = bodies[core]
    other = bodies[1 - core]
    send[...] = pack_sum(other, channels, other[channels + 1 : channels + 2])
    copies = [
        pltpu.make_async_copy(qs.at[core], q_h, out_sem.at[0]),
        pltpu.make_async_copy(qp_out, qp_h, out_sem.at[1]),
        pltpu.make_async_copy(pn_out, pn_h, out_sem.at[2]),
    ]
    for out in copies:
        out.start()
    for out in copies:
        out.wait()


def tiles_out(place, whole, outs):
    chips = len(outs)
    lanes = outs[0].shape[1]
    for step in range(chips):
        at = lax.rem(place[0] + step, chips)
        outs[step][...] = whole[:, pl.ds(pl.multiple_of(at * lanes, lanes), lanes)]


def tiles_in(place, whole, tiles, sem):
    chips = len(tiles)
    lanes = tiles[0].shape[1]
    copies = []
    for step in range(chips):
        at = lax.rem(place[0] + chips - step, chips)
        target = whole.at[:, pl.ds(pl.multiple_of(at * lanes, lanes), lanes)]
        copies.append(pltpu.make_async_copy(tiles[step], target, sem.at[step]))
        copies[-1].start()
    return copies


def places():
    return lax.axis_index("chip"), lax.axis_index("core"), lax.axis_index("img")


def join_one_body(channels, keep, got, *refs):
    outs, whole = refs[:-1], refs[-1]
    place = places()
    own = keep[...]
    body, top = join_sums(
        [(own, own[channels + 1 : channels + 2]), unpack_sum(got[...], channels)]
    )
    whole[...] = pack_sum(body, channels, top)
    tiles_out(place, whole, outs)


def load_all(tiles, held, sem):
    copies = [
        pltpu.make_async_copy(tile, held.at[at], sem.at[at]) for at, tile in enumerate(tiles)
    ]
    for copy in copies:
        copy.start()
    for copy in copies:
        copy.wait()
    return [held[at] for at in range(len(tiles))]


def join_two_body(channels, *refs):
    tiles, out, held, sem = refs[:-3], refs[-3], refs[-2], refs[-1]
    body, top = join_sums([unpack_sum(t, channels) for t in load_all(tiles, held, sem)])
    total = body[channels : channels + 1]
    extras = (jnp.ones_like(total),) + three_parts(total) + three_parts(top)
    out[...] = with_rows(body / total, channels, extras).astype(BF)


def gather_body(*refs):
    tiles, whole, sem = refs[:-2], refs[-2], refs[-1]
    for copy in tiles_in(places(), whole, tiles, sem):
        copy.wait()


def back_one_body(
    channels, own, got, qp_h, pn_h, keep, send, both, score_grad, weights_low, pair, qp_in, pn, bodies, sem
):
    images, padded, rows = qp_in.shape
    core = places()[1]
    pairs = [(pn_h, pn), (qp_h, qp_in), (own, pair.at[core]), (got, pair.at[1 - core])]
    copies = [pltpu.make_async_copy(s, d, sem.at[at]) for at, (s, d) in enumerate(pairs)]
    for copy in copies:
        copy.start()
    for copy in copies:
        copy.wait()

    def per_image(image):
        pack = pair[image].astype(F32)
        level = (
            pack[channels + 2 : channels + 3]
            + pack[channels + 3 : channels + 4]
            + pack[channels + 4 : channels + 5]
        )
        grads = jnp.where(row_of(pack) < channels + 2, pack, 0.0).astype(BF)
        both[image] = grads
        scores = dot(pn[image], qp_in[image], 0, 0)
        weights = jnp.exp(scores - level * LOG_TWO)
        weights_low[image] = weights.astype(BF)
        score_grad[image] = (dot(pn[image], grads, 0, 0) * weights).astype(BF)
        bodies[image] = dot(pn[image], score_grad[image], 1, 0)

    for image in range(images):
        per_image(image)
    keep[...] = bodies[core]
    send[...] = bodies[1 - core].astype(BF)


def back_join_one_body(keep, got, *refs):
    outs, whole = refs[:-1], refs[-1]
    place = places()
    whole[...] = (keep[...] + got[...].astype(F32)).astype(BF)
    tiles_out(place, whole, outs)


def back_two_body(
    channels, score_grad, weights_low, qp_h, both, pix, par, out_own, out_got,
    d_pix, sums, out_both, xs, turn, qp, sem
):
    images = pix.shape[1]
    padded = qp.shape[1]
    core = places()[1]
    pairs = [(qp_h, qp), (out_own, out_both.at[core]), (out_got, out_both.at[1 - core])]
    copies = [pltpu.make_async_copy(s, d, sem.at[at]) for at, (s, d) in enumerate(pairs)]
    for copy in copies:
        copy.start()
    copies[0].wait()
    xs[...] = jnp.zeros_like(xs)

    def per_image(image, carry):
        dn = dot(qp[image], score_grad[image], 1, 1) + dot(both[image], weights_low[image], 1, 1)
        unit, iv, inside = pixel_units(pix, image, xs, channels)
        grad = jnp.where(inside, dn, 0.0)
        scaled = grad * par[:, 0:1]
        one = jnp.sum(scaled, axis=0, keepdims=True) * (1.0 / channels)
        two = jnp.sum(scaled * unit, axis=0, keepdims=True) * (1.0 / channels)
        d_pix[:, image, :] = (iv * (scaled - one - unit * two))[:channels]
        d_gain = jnp.sum(grad * unit, axis=1, keepdims=True)
        d_shift = jnp.sum(grad, axis=1, keepdims=True)
        return carry[0] + d_gain, carry[1] + d_shift

    zero = jnp.zeros((padded, 1), F32)
    d_gain, d_shift = zero, zero
    for image in range(images):
        d_gain, d_shift = per_image(image, (d_gain, d_shift))
    turn[...] = jnp.zeros_like(turn)
    lane = lax.broadcasted_iota(jnp.int32, (padded, 128), 1)
    turn[:padded, :] = jnp.where(lane == 0, d_gain, jnp.where(lane == 1, d_shift, 0.0))
    sums[...] = turn[...].T[:8]
    copies[1].wait()
    copies[2].wait()


def back_join_two_body(channels, *refs):
    tiles, (sums, out, held, sem) = refs[:-4], refs[-4:]
    body = None
    for tile in load_all(tiles, held, sem):
        body = tile.astype(F32) if body is None else body + tile.astype(F32)
    lanes = out.shape[1]
    count = sums.shape[1] // lanes
    extras = [sums[r : r + 1, j * lanes : (j + 1) * lanes] for r in range(2) for j in range(count)]
    out[...] = with_rows(body, channels, extras).astype(BF)


def tail_body(channels, *refs):
    chips = len(refs) - 28
    place = places()
    tiles = refs[:chips]
    (
        lat_h,
        wq_h,
        d_after_h,
        query,
        wk_in,
        gains,
        shifts,
        small_in,
        d_lat,
        d_lat_low,
        keep,
        send,
        lat,
        wq,
        d_after,
        part,
        wk,
        tail,
        normed,
        low,
        acc,
        stat,
        sums,
        small,
        lat_sem,
        wq_sem,
        after_sem,
        tile_sem,
    ) = refs[chips:]
    rows, width = query.shape
    padded = part.shape[0]
    chip, core = place[0], place[1]
    copies = [
        pltpu.make_async_copy(lat_h.at[core], lat, lat_sem),
        pltpu.make_async_copy(wq_h, wq, wq_sem),
        pltpu.make_async_copy(d_after_h, d_after, after_sem),
    ]
    tile_copies = tiles_in(place, part, tiles, tile_sem)
    for copy in copies:
        copy.start()
    fill_rows(wk, wk_in, tail)
    for copy in tile_copies:
        copy.wait()
    base = channels // 16 * 16
    tail[:, :rows] = part[base : base + 16, :].astype(F32)
    extra_rows = tail[channels - base : channels - base + 6, :rows]
    lanes = tiles[0].shape[1]
    pix_rows = extra_rows[:, :lanes]
    for at in range(1, chips):
        pix_rows = pix_rows + extra_rows[:, at * lanes : (at + 1) * lanes]
    part_value = part[...]
    clean = jnp.where(row_of(part_value) < channels, part_value.astype(F32), 0.0).astype(BF)
    part[...] = clean
    d_query = dot(part[...], wk[...], 0, 0) * width ** (-0.5)
    low[...] = d_query.astype(BF)
    bias_row = jnp.sum(jnp.sum(d_query.reshape(-1, 8, width), axis=0), axis=0, keepdims=True)
    copies[0].wait()
    g, s = gains[0:1, :].astype(F32), shifts[0:1, :].astype(F32)

    v = lat[...].astype(F32)
    m = jnp.mean(v, axis=1, keepdims=True)
    c = v - m
    iv = lax.rsqrt(jnp.mean(c * c, axis=1, keepdims=True) + EPSILON)
    normed[...] = (c * iv * g + s).astype(BF)
    stat[0] = jnp.broadcast_to(m, (rows, 128))
    stat[1] = jnp.broadcast_to(iv, (rows, 128))

    def sides(ref):
        start = chip * 256
        mine = ref[:, pl.ds(pl.multiple_of(start + core * 128, 128), 128)]
        other = ref[:, pl.ds(pl.multiple_of(start + (1 - core) * 128, 128), 128)]
        return jnp.concatenate([mine, other], axis=1)

    def put(first, value):
        count = value.shape[0]
        keep[first : first + count, :] = value[:, :128]
        send[first : first + count, :] = value[:, 128:]

    put(0, dot(normed[...], sides(low), 0, 0).astype(BF))
    put(width, dot(part[...], sides(query), 1, 0).astype(BF))
    copies[1].wait()
    acc[...] = dot(low[...], wq[...], 1, 1)
    copies[2].wait()

    m, iv = stat[0, :, 0:1], stat[1, :, 0:1]
    unit = (lat[...].astype(F32) - m) * iv
    grad = acc[...]
    scaled = grad * g
    first_mean = jnp.mean(scaled, axis=1, keepdims=True)
    second_mean = jnp.mean(scaled * unit, axis=1, keepdims=True)
    total = d_after[...] + iv * (scaled - first_mean - unit * second_mean)
    d_lat[...] = total
    d_lat_low[...] = total.astype(BF)
    sums[0] = jnp.sum((grad * unit).reshape(-1, 8, width), axis=0)
    sums[1] = jnp.sum(grad.reshape(-1, 8, width), axis=0)
    small[...] = jnp.zeros_like(small)
    small[0:1, :] = jnp.sum(sums[0], axis=0, keepdims=True)
    small[1:4, :] = small_in[0:3, :]
    small[4:5, :] = jnp.sum(sums[1], axis=0, keepdims=True)
    small[5:8, :] = small_in[3:6, :]
    small[8:9, :] = bias_row
    small[9:17, :] = small_in[6:14, :]
    put(width + padded, sides(small).astype(BF))
    tail[...] = jnp.zeros_like(tail)
    tail[0:6, :lanes] = pix_rows
    spread = tail[:, :128].astype(BF)
    first = width + padded + small.shape[0]
    keep[first : first + 16, :] = spread
    send[first : first + 16, :] = spread


def first_add_body(keep_h, got_h, one, two, keep, got, sem):
    img = places()[2]
    quarter = one.shape[0]
    spots = [1 - lax.rem(img, 2), 3 - lax.div(img, 2)]
    copies = []
    for at, spot in enumerate(spots):
        source = pl.ds(pl.multiple_of(spot * quarter, 16), quarter)
        copies.append(pltpu.make_async_copy(keep_h.at[source, :], keep.at[at], sem.at[at, 0]))
        copies.append(pltpu.make_async_copy(got_h.at[source, :], got.at[at], sem.at[at, 1]))
    for copy in copies:
        copy.start()
    for at, out in enumerate((one, two)):
        copies[2 * at].wait()
        copies[2 * at + 1].wait()
        out[...] = (keep[at].astype(F32) + got[at].astype(F32)).astype(BF)


def second_add_body(keep_h, got_h, more_one, more_two, one, two, keep, got, sem):
    img = places()[2]
    quarter = one.shape[0]
    spots = [lax.rem(img, 2), 2 + lax.div(img, 2)]
    copies = []
    for at, spot in enumerate(spots):
        source = pl.ds(pl.multiple_of(spot * quarter, 16), quarter)
        copies.append(pltpu.make_async_copy(keep_h.at[source, :], keep.at[at], sem.at[at, 0]))
        copies.append(pltpu.make_async_copy(got_h.at[source, :], got.at[at], sem.at[at, 1]))
    for copy in copies:
        copy.start()
    for at, (more, out) in enumerate(((more_one, one), (more_two, two))):
        copies[2 * at].wait()
        copies[2 * at + 1].wait()
        total = keep[at].astype(F32) + got[at].astype(F32) + more[...].astype(F32)
        out[...] = total.astype(BF)


def last_add_body(keep, got, *outs):
    img = places()[2]
    part = outs[0].shape[0]
    for step, out in enumerate(outs):
        at = pl.ds(pl.multiple_of((img ^ step) * part, 16), part)
        out[...] = (keep[at, :].astype(F32) + got[at, :].astype(F32)).astype(BF)


def last_sum_body(*refs):
    tiles, (out, held, sem) = refs[:-3], refs[-3:]
    body = None
    for tile in load_all(tiles, held, sem):
        body = tile.astype(F32) if body is None else body + tile.astype(F32)
    out[...] = body.astype(BF)


def give(outs, pieces, whole, some):
    for out, (first, count, across) in zip(outs, pieces):
        for j in range(across):
            at = first + j * count
            rows = out.shape[0]
            if len(out.shape) == 1:
                base = min(first // 16 * 16, whole.shape[0] - 32)
                some[...] = whole[base : base + 32, :].astype(F32)
                at = first - base
                row = jnp.concatenate([some[at + k : at + k + 1, :] for k in range(3)], axis=1)
                out[...] = row.reshape(384)[:rows]
            elif rows > 16:
                out[:, j * 128 : (j + 1) * 128] = whole[at : at + rows, :].astype(F32)
            else:
                base = min(at // 16 * 16, whole.shape[0] - 32)
                some[...] = whole[base : base + 32, :].astype(F32)
                out[:, j * 128 : (j + 1) * 128] = some[at - base : at - base + rows, :]


def fetch(parts, spots, whole, sem):
    part = parts[0].shape[0]
    copies = []
    for at, spot in enumerate(spots):
        target = whole.at[pl.ds(pl.multiple_of(spot * part, 16), part), :]
        copies.append(pltpu.make_async_copy(parts[at], target, sem.at[at]))
        copies[-1].start()
    for copy in copies:
        copy.wait()


def unpack_last_body(pieces, *refs):
    parts, outs, (whole, some, sem) = refs[:4], refs[4:-3], refs[-3:]
    img = places()[2]
    fetch(parts, [img ^ step for step in range(4)], whole, sem)
    give(outs, pieces, whole, some)


def latents_body(own, got, both):
    core = places()[1]
    both[core] = own[...]
    both[1 - core] = got[...].astype(F32)


def unpack_main_body(pieces, *refs):
    parts, outs, (whole, some, sem) = refs[:4], refs[4:-3], refs[-3:]
    img = places()[2]
    high, low = lax.div(img, 2), lax.rem(img, 2)
    fetch(parts, [low, 2 + high, 1 - low, 3 - high], whole, sem)
    give(outs, pieces, whole, some)


def call(body, outs, scratch, args, spaces, name, flops, out_spaces=None, vmem=None):
    vmem = vmem or VMEM_MIB[name]
    where = {
        "v": pl.BlockSpec(memory_space=pltpu.VMEM),
        "a": pl.BlockSpec(memory_space=pltpu.HBM),
        "n": pl.BlockSpec(memory_space=pl.ANY),
        "h": pl.BlockSpec(memory_space=pltpu.VMEM),
        "s": pl.BlockSpec(memory_space=pltpu.SMEM),
    }
    out_spaces = out_spaces or "v" * len(outs)
    args = [
        pltpu.with_memory_space_constraint(arg, pltpu.HBM) if s in "ah" else arg
        for arg, s in zip(args, spaces)
    ]
    return pl.pallas_call(
        body,
        out_shape=[
            pltpu.HBM(*o) if s == "a" else jax.ShapeDtypeStruct(*o) for o, s in zip(outs, out_spaces)
        ],
        in_specs=[where[s] for s in spaces],
        out_specs=[where[s] for s in out_spaces],
        scratch_shapes=scratch,
        compiler_params=pltpu.CompilerParams(vmem_limit_bytes=vmem << 20),
        cost_estimate=pl.CostEstimate(flops=flops, transcendentals=0, bytes_accessed=8 << 20),
        name=name,
    )(*args)


def on_device_fast(
    latents,
    pixels,
    keep_mask,
    cotangent,
    w_query,
    w_key,
    w_value,
    kv_bias,
    w_out,
    w_first,
    w_second,
    w_qkv,
    w_self_out,
    w_third,
    w_fourth,
    norm_gains,
    norm_shifts,
    proj_biases,
    pix_gain,
    pix_shift,
):
    images, rows, width = latents.shape
    _, pix, channels = pixels.shape
    padded = -(-(channels + 8) // 16) * 16
    wide = -(-(channels + 8) // 128) * 128
    chips = lax.axis_size("chip")
    lanes = rows // chips
    vm = pltpu.VMEM
    dma = pltpu.SemaphoreType.DMA
    pix_rows = jnp.transpose(pixels, (2, 0, 1))
    unit = 2 * rows * width * width
    cross = 2 * rows * pix * wide * images

    def swapped(values):
        return lax.ppermute(values, "core", SWAP)

    def around(tiles):
        return [
            lax.ppermute(t, "chip", shifted(chips, step + 1)) for step, t in enumerate(tiles)
        ]

    keep, send, par, query_pix, query, pix_normed = call(
        functools.partial(look_body, channels),
        [
            ((padded, rows), F32),
            ((padded, rows), BF),
            ((padded, 128), F32),
            ((images, padded, rows), BF),
            ((rows, width), BF),
            ((images, padded, pix), BF),
        ],
        [
            vm((width, width), BF),
            vm((images, rows, width), BF),
            vm((128, wide), F32),
            vm((images, rows, width), BF),
            vm((images, rows, width), BF),
            vm((padded, width), BF),
            vm((padded, pix), F32),
            vm((16, width), F32),
            vm((images, padded, rows), BF),
            vm((images, padded, pix), BF),
            vm((images, padded, rows), F32),
            vm((channels, images, pix), BF),
            dma,
            dma((3,)),
        ],
        (
            latents,
            pix_rows,
            keep_mask,
            pix_gain,
            pix_shift,
            norm_gains,
            norm_shifts,
            proj_biases,
            w_key,
            w_query,
        ),
        "aahhhhhhha",
        "look",
        3 * unit + 2 * cross,
        "vvvaaa",
    )
    tiles = call(
        functools.partial(join_one_body, channels),
        [((padded, lanes), BF)] * chips,
        [vm((padded, rows), BF)],
        (keep, swapped(send)),
        "vv",
        "join_one",
        1,
    )
    (tile,) = call(
        functools.partial(join_two_body, channels),
        [((padded, lanes), BF)],
        [vm((chips, padded, lanes), BF), dma((chips,))],
        (tiles[0], *around(tiles[1:])),
        "n" * chips,
        "join_two",
        1,
    )
    (tile,) = call(
        gather_body,
        [((padded, rows), BF)],
        [dma((chips,))],
        (tile, *around([tile] * (chips - 1))),
        "n" * chips,
        "gather",
        1,
        "a",
    )
    output, d_after, own_pack, small_grads, keep, send = trunk(
        [tile],
        latents,
        cotangent,
        norm_gains,
        norm_shifts,
        proj_biases,
        w_value,
        kv_bias[None],
        [w_out, w_first, w_second, w_qkv, w_self_out, w_third, w_fourth],
        channels,
        padded,
    )
    got_pack, send = lax.optimization_barrier((swapped(own_pack), send))
    got_send = swapped(send)
    both_keep = keep
    keep, send, both, score_grad, weights_low = call(
        functools.partial(back_one_body, channels),
        [
            ((padded, rows), F32),
            ((padded, rows), BF),
            ((images, padded, rows), BF),
            ((images, pix, rows), BF),
            ((images, pix, rows), BF),
        ],
        [
            vm((images, padded, rows), BF),
            vm((images, padded, rows), BF),
            vm((images, padded, pix), BF),
            vm((images, padded, rows), F32),
            dma((4,)),
        ],
        (own_pack, got_pack, query_pix, pix_normed),
        "anaa",
        "back_one",
        3 * cross,
    )
    keep, send, got_send = lax.optimization_barrier((keep, send, got_send))
    quarter = both_keep.shape[0] // 4
    adds = [vm((2, quarter, 128), BF), vm((2, quarter, 128), BF), dma((2, 2))]
    one, two = call(
        first_add_body,
        [((quarter, 128), BF)] * 2,
        adds,
        (both_keep, got_send),
        "an",
        "first_add",
        1,
    )
    got_output = swapped(output)
    tiles = call(
        back_join_one_body,
        [((padded, lanes), BF)] * chips,
        [vm((padded, rows), BF)],
        (keep, swapped(send)),
        "vv",
        "back_join_one",
        1,
    )
    tiles, score_grad, one, two = lax.optimization_barrier((tiles, score_grad, one, two))
    one, two = lax.ppermute(one, "img", LOW_PAIRS), lax.ppermute(two, "img", HIGH_PAIRS)
    d_pixels, sums, both_outputs = call(
        functools.partial(back_two_body, channels),
        [((channels, images, pix), F32), ((8, wide), F32), ((images, rows, width), BF)],
        [
            vm((padded, pix), F32),
            vm((wide, 128), F32),
            vm((images, padded, rows), BF),
            dma((3,)),
        ],
        (score_grad, weights_low, query_pix, both, pix_rows, par, output, got_output),
        "vvavhhan",
        "back_two",
        2 * cross,
    )
    (tile,) = call(
        functools.partial(back_join_two_body, channels),
        [((padded, lanes), BF)],
        [vm((chips, padded, lanes), BF), dma((chips,))],
        (tiles[0], *around(tiles[1:]), sums),
        "n" * chips + "v",
        "back_join_two",
        1,
    )
    tile, one, two = lax.optimization_barrier((tile, one, two))

    one, two = image_second(
        *call(
            second_add_body,
            [((quarter, 128), BF)] * 2,
            adds,
            (both_keep, got_send, one, two),
            "anvv",
            "second_add",
            1,
        )
    )
    tiles = [tile] + around([tile] * (chips - 1))
    last_rows = width + padded + 32 + 16
    d_lat, d_lat_low, keep, send = call(
        functools.partial(tail_body, channels),
        [
            ((rows, width), F32),
            ((rows, width), BF),
            ((last_rows, 128), BF),
            ((last_rows, 128), BF),
        ],
        [
            vm((rows, width), BF),
            vm((width, width), BF),
            vm((rows, width), F32),
            vm((padded, rows), BF),
            vm((padded, width), BF),
            vm((16, width), F32),
            vm((rows, width), BF),
            vm((rows, width), BF),
            vm((rows, width), F32),
            vm((2, rows, 128), F32),
            vm((2, 8, width), F32),
            vm((32, width), F32),
            dma,
            dma,
            dma,
            dma((chips,)),
        ],
        (
            *tiles,
            latents,
            w_query,
            d_after,
            query,
            w_key,
            norm_gains,
            norm_shifts,
            small_grads,
        ),
        "n" * chips + "aanhhhhh",
        "tail",
        3 * unit,
    )
    keep, send, d_lat_low, one, two = lax.optimization_barrier((keep, send, d_lat_low, one, two))
    got_one, got_two = image_third(one, two)
    part = last_rows // 4
    got_lat = swapped(d_lat_low)

    def partners(tiles):
        return [
            lax.ppermute(t, "img", [(i, i ^ (step + 1)) for i in range(4)])
            for step, t in enumerate(tiles)
        ]

    tiles = call(
        last_add_body,
        [((part, 128), BF)] * 4,
        [],
        (keep, swapped(send)),
        "vv",
        "last_add",
        1,
    )
    tiles, got_lat = lax.optimization_barrier((tiles, got_lat))
    arrived = partners(tiles[1:])
    square = (width, 128)
    first, pieces, shapes = 0, [], []
    for across in (1, 1, 1, 3, 1, 1, 1):
        pieces.append((first, width, across))
        shapes.append((width, 128 * across))
        first += width * across
    pieces += [(first, padded, 1), (first + channels, 1, 1)]
    shapes += [(channels, 128), (1, 128)]
    main = call(
        functools.partial(unpack_main_body, pieces),
        [(s, F32) for s in shapes],
        [vm((4 * one.shape[0], 128), BF), vm((32, 128), F32), dma((4,))],
        (one, two, got_one, got_two),
        "nnnn",
        "unpack_main",
        1,
    )
    d_pixels = jnp.transpose(d_pixels, (1, 2, 0))
    (both_latents,) = call(
        latents_body,
        [((images, rows, width), F32)],
        [],
        (d_lat, got_lat),
        "vv",
        "latents",
        1,
    )
    arrived, both_latents, d_pixels = lax.optimization_barrier((arrived, both_latents, d_pixels))
    (tile,) = call(
        last_sum_body,
        [((part, 128), BF)],
        [vm((4, part, 128), BF), dma((4,))],
        (tiles[0], *arrived),
        "nnnn",
        "last_sum",
        1,
    )
    parts = partners([tile] * 3)
    parts, main = lax.optimization_barrier((parts, main))
    at = width + padded
    rest = call(
        functools.partial(
            unpack_last_body,
            [
                (0, width, 1),
                (width, padded, 1),
                (at, 4, 1),
                (at + 4, 4, 1),
                (at + 8, 9, 1),
                (at + 32, 1, 1),
                (at + 35, 1, 1),
            ],
        ),
        [
            (s, F32)
            for s in (square, (channels, 128), (4, 128), (4, 128), (9, 128), (channels,), (channels,))
        ],
        [vm((last_rows, 128), BF), vm((32, 128), F32), dma((4,))],
        (tile, *parts),
        "nnnn",
        "unpack_last",
        1,
    )
    return (
        both_outputs,
        both_latents,
        d_pixels,
        rest[0],
        rest[1],
        main[7],
        main[8][0],
        main[6],
        main[5],
        main[4],
        main[3],
        main[2],
        main[1],
        main[0],
        rest[2],
        rest[3],
        rest[4],
        rest[5],
        rest[6],
    )


def on_device(*args):
    rows, width = args[0].shape[1:]
    chips = lax.axis_size("chip")
    if (width // chips) % 256 == 0 and width // chips == 256 and (rows // chips) % 128 == 0:
        return on_device_fast(*args)
    return on_device_slow(*args)


def solution(mesh):
    images, pieces = mesh.devices.shape
    split = Mesh(mesh.devices.reshape(images, pieces // 2, 2), ("img", "chip", "core"))
    latent = P("img", None, None)
    weight = P(None, PIX)
    placed = (latent, P("img", PIX, None), P("img", PIX), latent) + (P(),) * 16
    return jax.shard_map(
        on_device,
        mesh=split,
        in_specs=placed,
        out_specs=(latent, latent, P("img", PIX, None), weight, weight, weight, P(PIX))
        + (weight,) * 10
        + (P(), P()),
        check_vma=False,
    )
```
